32 devices in a mesh: ep: 8 (over z, x), tp: 4 (over y, core).
Axes of the slice: x: 2, y: 2, z: 4, core: 2. Of those that a mesh axis runs over, the one named last changes fastest.
Arguments:
- query_latent: bfloat16 [128, 64, 512], P('ep', 'tp'), may hold values from -50 to 50
- query_rope: bfloat16 [128, 64, 64], P('ep', 'tp'), may hold values from -5 to 5
- cache_latent: bfloat16 [128, 256, 512], P('ep'), may hold values from -6 to 6
- cache_rope: bfloat16 [128, 64, 256], P('ep'), may hold values from -5 to 5
- cache_lengths: int32 [128], P('ep'), may hold values from 2 to 256
- value_up: bfloat16 [64, 512, 128], P('tp'), may hold values from -0.25 to 0.25
- out_proj: bfloat16 [3584, 8192], P('ep', 'tp'), may hold values from -0.0625 to 0.0625
- residual: bfloat16 [128, 3584], P('ep'), may hold values from -6 to 6
- norm_gain: float32 [3584], replicated, may hold values from 0.1 to 1.9
- router: bfloat16 [3584, 8], replicated, may hold values from -0.09375 to 0.09375
- trainer_gate: bfloat16 [8, 3584, 1024], P('ep', None, 'tp'), may hold values from -0.09375 to 0.09375
- trainer_up: bfloat16 [8, 3584, 1024], P('ep', None, 'tp'), may hold values from -0.09375 to 0.09375
- trainer_down: bfloat16 [8, 1024, 3584], P('ep', 'tp'), may hold values from -0.1875 to 0.1875
- hot_experts: int32 [2], replicated, may hold values from 0 to 7, as said below
- replica_index: int32 [8], replicated, may hold values from 0 to 1, as said below
- token_experts: int32 [128, 8], P('ep'), may hold values from 0 to 7, as said below
- replica_pick: int32 [128, 8], P('ep'), may hold values from 0 to 1048575
Outputs:
- layer_out: bfloat16 [128, 3584], P('ep', 'tp')
The draws below stay inside these ranges and needn't reach their ends.
Inputs may be any that keep to these rules, and one draw needn't show every extreme that they name: `hot_experts`: the 2 hot experts differ, and the largest of them is 7. `replica_index`: the group right after the trainer of each hot expert (next index of ep, wrapping) holds a replica of that expert. `token_experts`: the 8 experts of one row differ, and every row names all hot experts.
All inputs are finite; a program needn't handle non-finite values.
Results may differ from the reference program's by a relative error of at most 0.008.
Values may be sent and summed in bfloat16 or wider, within the bound.
No kernel may reach another device: no remote copies, remote signals or barrier semaphores. Data moves between devices by JAX's collectives and lax.ppermute only.
A program may use at most 128 MiB of HBM per device.

```python
import jax
import jax.numpy as jnp
from jax import lax

D = 3584
FF = 1024
HEADS = 64
LATENT = 512
ROPE = 64
VDIM = 128
TOPK = 8
SLOT_DEV = 2
CAP = 2
HOT = 2
B_DEV = 16
LMAX = 256
EXPERTS = 8
GROUPS = 8
TOKENS = 128
N_EP = 8
N_TP = 4


def latent_rows(key):
    base = jnp.clip(jax.random.normal(jax.random.fold_in(key, 71), (TOKENS, LMAX, LATENT), jnp.float32), -5.0, 5.0)
    return base


def draw_cache_latent(key, part):
    return latent_rows(key).astype(jnp.bfloat16)


def draw_query_latent(key, part):
    query = jnp.clip(jax.random.normal(jax.random.fold_in(key, 72), (TOKENS, HEADS, LATENT), jnp.float32), -5.0, 5.0)
    return query.astype(jnp.bfloat16)


def hot_pair(key):
    drawn = jax.random.permutation(jax.random.fold_in(key, 81), EXPERTS)[:HOT].astype(jnp.int32)
    lift = (EXPERTS - 1 - jnp.max(drawn)).astype(jnp.int32)
    return (drawn + lift).astype(jnp.int32)


def draw_hot_experts(key, part):
    return hot_pair(key)


def draw_replica_index(key, part):
    hot = hot_pair(key)
    plan = jax.random.randint(jax.random.fold_in(key, 82), (GROUPS,), 0, HOT).astype(jnp.int32)
    group_ids = lax.iota(jnp.int32, GROUPS)
    for hot_rank in range(HOT):
        follower = (hot[hot_rank] + 1) % GROUPS
        plan = jnp.where(group_ids == follower, hot_rank, plan).astype(jnp.int32)
    return plan


def draw_token_experts(key, part):
    hot = hot_pair(key)
    expert_ids = lax.iota(jnp.int32, EXPERTS)
    raw = jax.random.randint(jax.random.fold_in(key, 83), (TOKENS, EXPERTS), 0, 65536).astype(jnp.int32)
    scores = raw * EXPERTS + expert_ids[None, :]
    is_hot = jnp.sum((expert_ids[None, :] == hot[:, None]).astype(jnp.int32), axis=0)
    scores = scores + is_hot[None, :] * (1 << 26)
    return lax.top_k(scores, TOPK)[1].astype(jnp.int32)


def touch_ends(values, own_key, smallest, top_value):
    dims = values.shape
    place = [jax.random.randint(jax.random.fold_in(own_key, axis), (), 0, dims[axis]) for axis in range(len(dims))]
    values = values.at[tuple(place)].set(smallest)
    longest = dims.index(max(dims))
    place[longest] = (place[longest] + 1) % dims[longest]
    return values.at[tuple(place)].set(top_value)


def block_levels(stream_key, shape, cuts, smallest, high):
    def one(position, blocks):
        heights = jax.random.uniform(jax.random.fold_in(jax.random.fold_in(stream_key, 6), position), (blocks,), jnp.float32, smallest / len(cuts), high / len(cuts))
        return jnp.repeat(jnp.exp(heights), shape[position] // blocks).reshape((-1,) + (1,) * (len(shape) - position - 1))

    level = one(*cuts[0])
    for cut in cuts[1:]:
        level = level * one(*cut)
    return level


def noise(key, dims, scale, most, cuts=(), kind=jnp.bfloat16):
    level = block_levels(key, dims, cuts, -0.22, 0.18) if cuts else 1.0
    values = jax.random.normal(key, dims, jnp.float32) * scale * level
    return jnp.minimum(jnp.maximum(values, -most), most).astype(kind)


def setup_inputs(seed: int = 0) -> dict:
    splits = jax.random.split(jax.random.key(seed), 18)
    query_latent = draw_query_latent(jax.random.fold_in(splits[17], 71), 0)
    query_rope = noise(splits[1], (TOKENS, HEADS, ROPE), 1.0, 5.0, ((0, 8), (1, 4)))
    cache_latent = draw_cache_latent(jax.random.fold_in(splits[17], 71), 0)
    cache_rope = noise(splits[3], (TOKENS, ROPE, LMAX), 1.0, 5.0, ((0, 8),))
    cache_lengths = touch_ends(jax.random.randint(splits[4], (TOKENS,), 2, LMAX + 1), jax.random.fold_in(splits[4], 1), 2, LMAX).astype(jnp.int32)
    value_up = noise(splits[5], (HEADS, LATENT, VDIM), LATENT ** -0.5, 0.25, ((0, 4),))
    out_proj = noise(splits[6], (D, HEADS * VDIM), (HEADS * VDIM) ** -0.5, 0.0625, ((0, 8), (1, 4)))
    residual = noise(splits[7], (TOKENS, D), 1.0, 6.0, ((0, 8),))
    norm_gain = jnp.clip(1.0 + 0.18 * jax.random.normal(splits[8], (D,), jnp.float32), 0.1, 1.9)
    router = noise(splits[9], (D, EXPERTS), D ** -0.5, 0.09375)
    trainer_gate = noise(splits[10], (EXPERTS, D, FF), D ** -0.5, 0.09375, ((0, 8), (2, 4)))
    trainer_up = noise(splits[11], (EXPERTS, D, FF), D ** -0.5, 0.09375, ((0, 8), (2, 4)))
    trainer_down = noise(splits[12], (EXPERTS, FF, D), FF ** -0.5, 0.1875, ((0, 8), (1, 4)))
    hot_experts = draw_hot_experts(jax.random.fold_in(splits[17], 71), 0)
    replica_index = draw_replica_index(jax.random.fold_in(splits[17], 71), 0)
    token_experts = draw_token_experts(jax.random.fold_in(splits[17], 71), 0)
    replica_pick = touch_ends(jax.random.randint(splits[16], (TOKENS, TOPK), 0, 1048576), jax.random.fold_in(splits[16], 1), 0, 1048575).astype(jnp.int32)
    return {"query_latent": query_latent, "query_rope": query_rope, "cache_latent": cache_latent, "cache_rope": cache_rope, "cache_lengths": cache_lengths, "value_up": value_up, "out_proj": out_proj, "residual": residual, "norm_gain": norm_gain, "router": router, "trainer_gate": trainer_gate, "trainer_up": trainer_up, "trainer_down": trainer_down, "hot_experts": hot_experts, "replica_index": replica_index, "token_experts": token_experts, "replica_pick": replica_pick}


score_scale = 192.0 ** (-0.5)
route_scale = 2.5
norm_eps = 1e-06

def choose_slots(expert_flat, pick_flat, hot_experts, replica_index, groups):
    slot_count = groups * SLOT_DEV
    slot_ids = lax.iota(jnp.int32, slot_count)
    owner_group = slot_ids // SLOT_DEV
    column = slot_ids % SLOT_DEV
    group_ids = lax.iota(jnp.int32, groups)
    owner_pick = lax.optimization_barrier(jnp.sum(jnp.where(owner_group[:, None] == group_ids[None, :], replica_index[None, :], 0), axis=1)).astype(jnp.int32)
    hot_ids = lax.iota(jnp.int32, HOT)
    owner_hot = lax.optimization_barrier(jnp.sum(jnp.where(owner_pick[:, None] == hot_ids[None, :], hot_experts[None, :], 0), axis=1)).astype(jnp.int32)
    slot_expert = jnp.where(column == 0, owner_group, owner_hot).astype(jnp.int32)
    holding = (expert_flat[:, None] == slot_expert[None, :]).astype(jnp.int32)
    holders = lax.optimization_barrier(jnp.sum(holding, axis=1)).astype(jnp.int32)
    candidate_rank = (jnp.cumsum(holding, axis=1) - 1).astype(jnp.int32)
    target = (pick_flat % holders).astype(jnp.int32)
    chosen = (holding * (candidate_rank == target[:, None]).astype(jnp.int32)).astype(jnp.int32)
    return (chosen, slot_expert)

def reference(query_latent, query_rope, cache_latent, cache_rope, cache_lengths, value_up, out_proj, residual, norm_gain, router, trainer_gate, trainer_up, trainer_down, hot_experts, replica_index, token_experts, replica_pick):
    tokens = query_latent.shape[0]
    latent_full = cache_latent.astype(jnp.float32)
    latent_term = jnp.einsum('thl,tpl->thp', query_latent.astype(jnp.float32), latent_full)
    rope_term = jnp.einsum('thr,trp->thp', query_rope.astype(jnp.float32), cache_rope.astype(jnp.float32))
    scores = (latent_term + rope_term) * score_scale
    places = lax.broadcasted_iota(jnp.int32, scores.shape, 2)
    in_range = places < cache_lengths[:, None, None]
    scores = jnp.where(in_range, scores, -1e+30)
    row_max = lax.optimization_barrier(jnp.max(scores, axis=2, keepdims=True))
    shifted = jnp.where(in_range, jnp.exp(scores - row_max), 0.0)
    probs_bf = (shifted / lax.optimization_barrier(jnp.sum(shifted, axis=2, keepdims=True))).astype(jnp.bfloat16)
    latent_out = jnp.einsum('thp,tpl->thl', probs_bf.astype(jnp.float32), latent_full).astype(jnp.bfloat16)
    head_values = jnp.einsum('thl,hlv->thv', latent_out.astype(jnp.float32), value_up.astype(jnp.float32)).astype(jnp.bfloat16)
    values_flat = head_values.reshape(tokens, -1)
    attention = jnp.dot(values_flat, out_proj.T, preferred_element_type=jnp.float32)
    hidden = residual.astype(jnp.float32) + attention
    root_mean = jnp.sqrt(lax.optimization_barrier(jnp.mean(hidden * hidden, axis=1)) + norm_eps)
    normed = (hidden * norm_gain[None, :] / root_mean[:, None]).astype(jnp.bfloat16)
    logits = jnp.dot(normed, router, preferred_element_type=jnp.float32)
    expert_ids = lax.iota(jnp.int32, logits.shape[1])
    picked = lax.optimization_barrier(jnp.sum(jnp.where(token_experts[:, :, None] == expert_ids[None, None, :], logits[:, None, :], 0.0), axis=2))
    affinity = jax.nn.sigmoid(picked)
    gates = route_scale * affinity / lax.optimization_barrier(jnp.sum(affinity, axis=1, keepdims=True))
    groups = N_EP
    slot_count = groups * SLOT_DEV
    chosen, slot_expert = choose_slots(token_experts.reshape(-1), replica_pick.reshape(-1), hot_experts, replica_index, groups)
    per_group = chosen.reshape(groups, -1, slot_count)
    earlier = (jnp.cumsum(per_group, axis=1) - per_group).astype(jnp.int32)
    prior = lax.optimization_barrier(jnp.sum(earlier * per_group, axis=2)).astype(jnp.int32).reshape(-1)
    kept = prior < CAP
    slot_of = lax.optimization_barrier(jnp.sum(chosen * lax.iota(jnp.int32, slot_count)[None, :], axis=1)).astype(jnp.int32)
    assign_ids = lax.iota(jnp.int32, chosen.shape[0])
    group_of = assign_ids // (B_DEV * TOPK)
    depth = groups * CAP
    dest = (slot_of * depth + group_of * CAP + prior).astype(jnp.int32)
    token_of = assign_ids // TOPK
    total = slot_count * depth
    table = jnp.full((total,), -1, jnp.int32).at[jnp.where(kept, dest, total)].set(token_of, mode='drop')
    block = FF // N_TP

    def run_slot(slot_index):
        row_ids = lax.dynamic_slice_in_dim(table, (slot_index * depth).astype(jnp.int32), depth, 0)
        present = row_ids >= 0
        rows = jnp.where(present[:, None], normed[jnp.maximum(row_ids, 0)], jnp.zeros((), jnp.bfloat16))
        expert = slot_expert[slot_index]
        weight_gate = lax.dynamic_index_in_dim(trainer_gate, expert, 0, keepdims=False)
        weight_up = lax.dynamic_index_in_dim(trainer_up, expert, 0, keepdims=False)
        weight_down = lax.dynamic_index_in_dim(trainer_down, expert, 0, keepdims=False)
        gate_val = jnp.dot(rows, weight_gate, preferred_element_type=jnp.float32)
        up_val = jnp.dot(rows, weight_up, preferred_element_type=jnp.float32)
        activated = (jax.nn.silu(gate_val) * up_val).astype(jnp.bfloat16)
        blocks = jnp.einsum('rtf,tfd->trd', activated.reshape(depth, N_TP, block).astype(jnp.float32), weight_down.reshape(N_TP, block, D).astype(jnp.float32))
        blocks = lax.optimization_barrier(blocks.astype(jnp.bfloat16)).astype(jnp.float32)
        return lax.optimization_barrier(jnp.sum(blocks, axis=0)).astype(jnp.bfloat16)
    outputs = lax.map(run_slot, lax.iota(jnp.int32, slot_count))
    flat_out = outputs.reshape(total, -1)
    fetched = flat_out[jnp.where(kept, dest, 0)].astype(jnp.float32) * kept[:, None].astype(jnp.float32)
    weighted = fetched * gates.reshape(-1)[:, None]
    moe = lax.optimization_barrier(jnp.sum(weighted.reshape(tokens, TOPK, -1), axis=1))
    return (hidden + moe).astype(jnp.bfloat16)
```

```python
import jax
import jax.numpy as jnp
from jax import lax
from jax.sharding import Mesh, PartitionSpec as P

TOPK = 8
SLOT_DEV = 2
CAP = 2
HOT = 2
CORES = 2
LANES = 128

score_scale = 192.0 ** (-0.5)
route_scale = 2.5
norm_eps = 1e-06
bf16 = jnp.bfloat16
f32 = jnp.float32


def choose_slots(expert_flat, pick_flat, hot_experts, replica_index, groups):
    slot_count = groups * SLOT_DEV
    slot_ids = lax.iota(jnp.int32, slot_count)
    owner_group = slot_ids // SLOT_DEV
    column = slot_ids % SLOT_DEV
    group_ids = lax.iota(jnp.int32, groups)
    owner_pick = jnp.sum(
        jnp.where(owner_group[:, None] == group_ids[None, :], replica_index[None, :], 0), axis=1
    )
    hot_ids = lax.iota(jnp.int32, HOT)
    owner_hot = jnp.sum(
        jnp.where(owner_pick[:, None] == hot_ids[None, :], hot_experts[None, :], 0), axis=1
    )
    slot_expert = jnp.where(column == 0, owner_group, owner_hot)
    holding = (expert_flat[:, None] == slot_expert[None, :]).astype(jnp.int32)
    holders = jnp.sum(holding, axis=1)
    candidate_rank = jnp.cumsum(holding, axis=1) - 1
    target = pick_flat % holders
    return holding * (candidate_rank == target[:, None]).astype(jnp.int32)


def keep_codes(token_experts, replica_pick, hot_experts, replica_index, groups, experts):
    chosen = choose_slots(
        token_experts.reshape(-1), replica_pick.reshape(-1), hot_experts, replica_index, groups
    )
    earlier = jnp.cumsum(chosen, axis=0) - chosen
    prior = jnp.sum(earlier * chosen, axis=1)
    code = 1.0 + (prior < CAP).astype(f32)
    expert_ids = lax.iota(jnp.int32, experts)
    named = token_experts[:, :, None] == expert_ids[None, None, :]
    return jnp.sum(jnp.where(named, code.reshape(token_experts.shape)[:, :, None], 0.0), axis=1)


def attend(query_latent, query_rope, cache_latent, cache_rope, cache_lengths, value_up):
    latent_term = jnp.einsum(
        "bhl,bpl->bhp", query_latent, cache_latent, preferred_element_type=f32
    )
    rope_term = jnp.einsum("bhr,brp->bhp", query_rope, cache_rope, preferred_element_type=f32)
    scores = (latent_term + rope_term) * score_scale
    places = lax.broadcasted_iota(jnp.int32, scores.shape, 2)
    in_range = places < cache_lengths[:, None, None]
    scores = jnp.where(in_range, scores, -1e30)
    row_max = jnp.max(scores, axis=2, keepdims=True)
    shifted = jnp.where(in_range, jnp.exp(scores - row_max), 0.0)
    probs_bf = (shifted / jnp.sum(shifted, axis=2, keepdims=True)).astype(bf16)
    latent_out = jnp.einsum(
        "bhp,bpl->bhl", probs_bf, cache_latent, preferred_element_type=f32
    ).astype(bf16)
    head_values = jnp.einsum(
        "bhl,hlv->bhv", latent_out, value_up, preferred_element_type=f32
    ).astype(bf16)
    return head_values.reshape(head_values.shape[0], -1)


def exchange(block, axis, size, mine):
    pieces = []
    for k in range(1, size):
        sent = lax.dynamic_index_in_dim(block, mine ^ k, 0, keepdims=False)
        pieces.append(lax.ppermute(sent, axis, [(i, i ^ k) for i in range(size)]))
    return lax.dynamic_index_in_dim(block, mine, 0, keepdims=False), pieces


def to_all(block, axes, count):
    spread = jnp.broadcast_to(block[None], (count,) + block.shape)
    return lax.all_to_all(spread, axes, split_axis=0, concat_axis=0, tiled=True)


def per_device(
    query_latent,
    query_rope,
    cache_latent,
    cache_rope,
    cache_lengths,
    value_up,
    out_proj,
    residual,
    norm_gain,
    router,
    trainer_gate,
    trainer_up,
    trainer_down,
    hot_experts,
    replica_index,
    token_experts,
    replica_pick,
):
    n_ep, n_y, n_c = lax.axis_size("ep"), lax.axis_size("y"), lax.axis_size("c")
    n_tp = n_y * n_c
    ep, y, c = lax.axis_index("ep"), lax.axis_index("y"), lax.axis_index("c")
    tp = y * n_c + c
    here, width = residual.shape
    tokens = here * n_ep
    quarter = tokens // n_tp
    experts = router.shape[1]
    block = out_proj.shape[0]
    sub = block // n_tp
    part = width // n_tp

    codes = keep_codes(
        token_experts, replica_pick, hot_experts, replica_index, n_ep, experts
    ).astype(bf16)
    shares = residual.reshape(here, n_ep, n_tp, sub)
    shares = lax.dynamic_index_in_dim(shares, tp, 2, keepdims=False).transpose(1, 0, 2)
    values = attend(
        query_latent, query_rope, cache_latent, cache_rope, cache_lengths, value_up
    )
    inner = values.shape[1]
    code_wide = -(-experts // LANES) * LANES
    sub_wide = -(-sub // LANES) * LANES
    parcel = jnp.concatenate(
        [
            jnp.broadcast_to(values[None], (n_ep, here, inner)),
            jnp.broadcast_to(
                jnp.pad(codes, ((0, 0), (0, code_wide - experts)))[None], (n_ep, here, code_wide)
            ),
            jnp.pad(shares, ((0, 0), (0, 0), (0, sub_wide - sub))),
        ],
        axis=2,
    )
    landed = lax.all_to_all(parcel, "ep", split_axis=0, concat_axis=0, tiled=True)
    landed = landed.reshape(tokens, -1)
    all_codes = landed[:, inner : inner + experts].astype(f32)
    all_shares = landed[:, inner + code_wide :]
    place = (
        lax.broadcasted_iota(jnp.int32, (sub_wide, block), 0) + tp * sub
        == lax.broadcasted_iota(jnp.int32, (sub_wide, block), 1)
    ) & (lax.broadcasted_iota(jnp.int32, (sub_wide, block), 0) < sub)
    column_part = lax.dot_general(
        landed[:, :inner], out_proj, (((1,), (1,)), ((), ())), preferred_element_type=f32
    ) + jnp.dot(all_shares, place.astype(bf16), preferred_element_type=f32)

    halves = column_part.reshape(n_y, n_c, quarter, block).transpose(1, 0, 2, 3)
    own, others = exchange(halves, "c", n_c, c)
    half = own + sum(others)
    own, others = exchange(half, "y", n_y, y)
    hidden_part = (own + sum(others)).astype(bf16)

    mine = to_all(hidden_part, ("ep", "y"), n_ep * n_y).reshape(n_ep, n_y, quarter, block)
    cores = [mine] + [
        lax.ppermute(mine, "c", [(i, i ^ k) for i in range(n_c)]) for k in range(1, n_c)
    ]
    ordered = []
    for j in range(n_c):
        pick = cores[0]
        for k in range(1, n_c):
            pick = jnp.where((c ^ k) == j, cores[k], pick)
        ordered.append(pick)
    rows = jnp.stack(ordered, axis=2).reshape(n_ep, tokens, block).transpose(1, 0, 2)
    hidden = rows.reshape(tokens, width).astype(f32)
    root_mean = jnp.sqrt(jnp.mean(hidden * hidden, axis=1, keepdims=True) + norm_eps)
    normed = (hidden * norm_gain[None, :] / root_mean).astype(bf16)
    logits = jnp.dot(normed, router, preferred_element_type=f32)
    affinity = jnp.where(all_codes > 0.5, jax.nn.sigmoid(logits), 0.0)
    gates = route_scale * affinity / jnp.sum(affinity, axis=1, keepdims=True)
    mine_only = lax.iota(jnp.int32, experts)[None, :] == ep
    weight = jnp.sum(
        jnp.where(mine_only & (all_codes > 1.5), gates, 0.0), axis=1, keepdims=True
    )

    gate_val = jnp.dot(normed, trainer_gate[0], preferred_element_type=f32)
    up_val = jnp.dot(normed, trainer_up[0], preferred_element_type=f32)
    act = (jax.nn.silu(gate_val) * up_val * weight).astype(bf16)
    partial = jnp.dot(act, trainer_down[0], preferred_element_type=f32).astype(bf16)

    split = partial.reshape(tokens, n_y, n_c, part).transpose(2, 1, 0, 3)
    own, others = exchange(split, "c", n_c, c)
    summed = own.astype(f32) + sum(o.astype(f32) for o in others)
    outbound = (
        summed.astype(bf16)
        .reshape(n_y, n_ep, here, part)
        .transpose(1, 0, 2, 3)
        .reshape(n_ep * n_y, here, part)
    )
    returned = lax.all_to_all(outbound, ("ep", "y"), split_axis=0, concat_axis=0, tiled=True)
    moe = jnp.sum(returned.astype(f32), axis=0)
    hidden_own = lax.dynamic_slice(hidden, (ep * here, tp * part), (here, part))
    return (hidden_own + moe).astype(bf16)


def solution(mesh):
    n_ep, n_tp = mesh.shape["ep"], mesh.shape["tp"]
    fine = Mesh(mesh.devices.reshape(n_ep, n_tp // CORES, CORES), ("ep", "y", "c"))
    tp = ("y", "c")
    placed = (
        P("ep", tp, None),
        P("ep", tp, None),
        P("ep", None, None),
        P("ep", None, None),
        P("ep"),
        P(tp, None, None),
        P("ep", tp),
        P("ep", None),
        P(),
        P(),
        P("ep", None, tp),
        P("ep", None, tp),
        P("ep", tp, None),
        P(),
        P(),
        P("ep", None),
        P("ep", None),
    )
    return jax.shard_map(
        per_device, mesh=fine, in_specs=placed, out_specs=P("ep", tp), check_vma=False
    )
```

```python
import functools

import jax
import jax.numpy as jnp
from jax import lax
from jax.experimental import pallas as pl
from jax.experimental.pallas import tpu as pltpu
from jax.sharding import Mesh, PartitionSpec as P

TOPK = 8
SLOT_DEV = 2
CAP = 2
HOT = 2
CORES = 2
LANES = 128

score_scale = 192.0 ** (-0.5)
route_scale = 2.5
norm_eps = 1e-06
bf16 = jnp.bfloat16
f32 = jnp.float32


def keep_codes(token_experts, replica_pick, hot_experts, replica_index, experts):
    ids = lax.iota(jnp.int32, experts)
    held = jnp.where(
        replica_index[:, None] == lax.iota(jnp.int32, HOT)[None, :], hot_experts[None, :], 0
    ).sum(axis=1)
    count = 1 + jnp.sum((held[:, None] == ids[None, :]).astype(jnp.int32), axis=0)
    match = token_experts[:, :, None] == ids[None, None, :]
    named = jnp.any(match, axis=1)
    place = jnp.sum(jnp.where(match, replica_pick[:, :, None], 0), axis=1) % count[None, :]
    place = jnp.where(named, place, -1)
    tokens = lax.iota(jnp.int32, place.shape[0])
    ahead = (tokens[None, :] < tokens[:, None])[:, :, None] & (
        place[None, :, :] == place[:, None, :]
    )
    prior = jnp.sum(ahead.astype(jnp.int32), axis=1)
    return jnp.where(named, jnp.where(prior < CAP, 2.0, 1.0), 0.0)


def attend_kernel(
    steps, lengths, ql, qr, cl, cr, shares, vu_hbm, out, lat, vu, sem
):
    step = pl.program_id(0)
    per = ql.shape[0]
    heads = ql.shape[1]
    here = per * steps
    copy = pltpu.make_async_copy(vu_hbm, vu, sem)

    @pl.when(step == 0)
    def _():
        copy.start()

    for i in range(per):
        cache = cl[i]
        scores = lax.dot_general(
            ql[i], cache, (((1,), (1,)), ((), ())), preferred_element_type=f32
        )
        scores += jnp.dot(qr[i], cr[i], preferred_element_type=f32)
        scores *= score_scale
        places = lax.broadcasted_iota(jnp.int32, scores.shape, 1)
        live = places < lengths[step * per + i]
        scores = jnp.where(live, scores, -1e30)
        peak = jnp.max(scores, axis=1, keepdims=True)
        shifted = jnp.where(live, jnp.exp(scores - peak), 0.0)
        probs = (shifted / jnp.sum(shifted, axis=1, keepdims=True)).astype(bf16)
        mixed = jnp.dot(probs, cache, preferred_element_type=f32)
        for j in range(lat.shape[0]):
            lat[j, pl.ds((step * per + i) * heads, heads), :] = mixed[
                :, j * LANES : (j + 1) * LANES
            ]

    @pl.when(step == steps - 1)
    def _():
        copy.wait()
        vdim = vu.shape[2]
        for h in range(heads):
            rows = jnp.concatenate(
                [lat[j, pl.ds(h, here, stride=heads), :] for j in range(lat.shape[0])], axis=1
            ).astype(bf16)
            got = jnp.dot(rows, vu[h], preferred_element_type=f32).astype(bf16)
            for j in range(out.shape[0]):
                out[j, :, h * vdim : (h + 1) * vdim] = got
        for j in range(out.shape[0]):
            out[j, :, heads * vdim :] = shares[j]


def attend(query_latent, query_rope, cache_latent, cache_rope, lengths, value_up, shares):
    here, heads, latent = query_latent.shape
    rope, places = cache_rope.shape[1:]
    vdim = value_up.shape[2]
    dests, _, extra = shares.shape
    steps = 4
    per = here // steps
    spec = lambda *dims: pl.BlockSpec((per,) + dims, lambda t: (t,) + (0,) * len(dims))
    whole = lambda shape: pl.BlockSpec(shape, lambda t: (0,) * len(shape))
    out_shape = (dests, here, heads * vdim + extra)
    return pl.pallas_call(
        functools.partial(attend_kernel, steps),
        grid=(steps,),
        out_shape=jax.ShapeDtypeStruct(out_shape, bf16),
        in_specs=[
            pl.BlockSpec(memory_space=pltpu.SMEM),
            spec(heads, latent),
            spec(heads, rope),
            spec(places, latent),
            spec(rope, places),
            whole(shares.shape),
            pl.BlockSpec(memory_space=pl.ANY),
        ],
        out_specs=whole(out_shape),
        scratch_shapes=[
            pltpu.VMEM((latent // LANES, here * heads, LANES), f32),
            pltpu.VMEM(value_up.shape, bf16),
            pltpu.SemaphoreType.DMA,
        ],
        compiler_params=pltpu.CompilerParams(dimension_semantics=("arbitrary",)),
        name="attend",
    )(lengths, query_latent, query_rope, cache_latent, cache_rope, shares, value_up)


def expert_kernel(
    dims, where_ref, mine, other, gain, router, gate_hbm, up_hbm, down_hbm,
    keep_out, send_out, gate, up, down, x, codes, sems
):
    n_ep, n_y, quarter, block, experts, part = dims
    core, ep = where_ref[0], where_ref[1]
    half = n_y * quarter
    here = 2 * half // n_ep
    per_quarter = quarter // here
    copies = []
    for j in range(n_ep):
        rows = pl.ds(j * block, block)
        copies.append(
            (
                pltpu.make_async_copy(gate_hbm.at[rows], gate.at[rows], sems.at[0, j]),
                pltpu.make_async_copy(up_hbm.at[rows], up.at[rows], sems.at[1, j]),
            )
        )
    down_copy = pltpu.make_async_copy(down_hbm, down, sems.at[2, 0])
    for a, b in copies:
        a.start()
        b.start()
    down_copy.start()

    squares = jnp.zeros((2 * half, 1), f32)
    logits = jnp.zeros((2 * half, experts), f32)
    gate_val = jnp.zeros((2 * half, gate.shape[1]), f32)
    up_val = jnp.zeros((2 * half, up.shape[1]), f32)
    for j in range(n_ep):
        for i, src in enumerate((mine, other)):
            rows = src[:, j, :, :block].reshape(half, block).astype(f32)
            x[j, i * half : (i + 1) * half, :] = (rows * gain[:, j * block : (j + 1) * block]).astype(bf16)
        own = mine[:, j, :, :block].reshape(half, block).astype(f32)
        oth = other[:, j, :, :block].reshape(half, block).astype(f32)
        squares += jnp.concatenate(
            [jnp.sum(own * own, axis=1, keepdims=True), jnp.sum(oth * oth, axis=1, keepdims=True)], axis=0
        )
        y_of, rest = j // (per_quarter * 2), j % (per_quarter * 2)
        core_of, slot = rest // per_quarter, rest % per_quarter
        at = jnp.where(core == core_of, 0, half) + y_of * quarter + slot * here
        codes[pl.ds(pl.multiple_of(at, here), here), :] = mine[0, j, :here, block : block + experts].astype(f32)
        xj = x[j]
        a, b = copies[j]
        a.wait()
        b.wait()
        rows = slice(j * block, (j + 1) * block)
        gate_val += jnp.dot(xj, gate[rows, :], preferred_element_type=f32)
        up_val += jnp.dot(xj, up[rows, :], preferred_element_type=f32)
        logits += jnp.dot(xj, router[rows, :], preferred_element_type=f32)

    width = n_ep * block
    scale = 1.0 / jnp.sqrt(squares / width + norm_eps)
    code = codes[...]
    affinity = jnp.where(code > 0.5, jax.nn.sigmoid(logits * scale), 0.0)
    gates = route_scale * affinity / jnp.sum(affinity, axis=1, keepdims=True)
    mine_only = lax.broadcasted_iota(jnp.int32, gates.shape, 1) == ep
    weight = jnp.sum(
        jnp.where(mine_only & (code > 1.5), gates, 0.0), axis=1, keepdims=True
    )
    act = (jax.nn.silu(gate_val * scale) * (up_val * scale) * weight).astype(bf16)
    down_copy.wait()
    for flip, out in ((1, send_out), (0, keep_out)):
        to_core = jnp.where(core == 0, flip, 1 - flip)
        for y in range(n_y):
            cols = pl.ds(pl.multiple_of((y * 2 + to_core) * part, LANES), part)
            got = jnp.dot(act, down[:, cols], preferred_element_type=f32).astype(bf16)
            for i in range(2):
                of_core = jnp.where(core == 0, i, 1 - i)
                for q in range(n_y):
                    at = pl.multiple_of((q * 2 + of_core) * quarter, quarter)
                    src = i * half + q * quarter
                    out[y, pl.ds(at, quarter), :] = got[src : src + quarter, :]


def expert_block(where_ids, mine, other, gain, router, gate, up, down, block):
    n_y, n_ep, quarter, _ = mine.shape
    tokens = 2 * n_y * quarter
    experts = router.shape[1]
    part = down.shape[1] // (2 * n_y)
    dims = (n_ep, n_y, quarter, block, experts, part)
    vmem = pl.BlockSpec(memory_space=pltpu.VMEM)
    any_ = pl.BlockSpec(memory_space=pl.ANY)
    shape = jax.ShapeDtypeStruct((n_y, tokens, part), bf16)
    return pl.pallas_call(
        functools.partial(expert_kernel, dims),
        out_shape=(shape, shape),
        in_specs=[pl.BlockSpec(memory_space=pltpu.SMEM), vmem, vmem, vmem, vmem, any_, any_, any_],
        out_specs=(vmem, vmem),
        scratch_shapes=[
            pltpu.VMEM(gate.shape, bf16),
            pltpu.VMEM(up.shape, bf16),
            pltpu.VMEM(down.shape, bf16),
            pltpu.VMEM((n_ep, tokens, block), bf16),
            pltpu.VMEM((tokens, experts), f32),
            pltpu.SemaphoreType.DMA((3, n_ep)),
        ],
        name="experts",
    )(where_ids, mine, other, gain, router, gate, up, down)


def expert_plain(ep, c, mine, other, gain, router, gate, up, down, block):
    n_y, n_ep, quarter, _ = mine.shape
    tokens = 2 * n_y * quarter
    here = tokens // n_ep
    experts = router.shape[1]
    part = down.shape[1] // (2 * n_y)
    both = jnp.stack([jnp.where(c == 0, mine, other), jnp.where(c == 0, other, mine)], axis=1)
    codes = both[0, 0, :, :here, block : block + experts].reshape(tokens, experts).astype(f32)
    hidden = both[..., :block].transpose(0, 1, 3, 2, 4).reshape(tokens, -1).astype(f32)
    root_mean = jnp.sqrt(jnp.mean(hidden * hidden, axis=1, keepdims=True) + norm_eps)
    normed = (hidden * gain / root_mean).astype(bf16)
    logits = jnp.dot(normed, router, preferred_element_type=f32)
    affinity = jnp.where(codes > 0.5, jax.nn.sigmoid(logits), 0.0)
    gates = route_scale * affinity / jnp.sum(affinity, axis=1, keepdims=True)
    mine_only = lax.iota(jnp.int32, experts)[None, :] == ep
    weight = jnp.sum(jnp.where(mine_only & (codes > 1.5), gates, 0.0), axis=1, keepdims=True)
    gate_val = jnp.dot(normed, gate, preferred_element_type=f32)
    up_val = jnp.dot(normed, up, preferred_element_type=f32)
    act = (jax.nn.silu(gate_val) * up_val * weight).astype(bf16)
    partial = jnp.dot(act, down, preferred_element_type=f32).astype(bf16)
    split = partial.reshape(tokens, n_y, 2, part).transpose(2, 1, 0, 3)
    return (
        lax.dynamic_index_in_dim(split, c, 0, keepdims=False),
        lax.dynamic_index_in_dim(split, 1 - c, 0, keepdims=False),
    )


def exchange(block, axis, size, mine):
    pieces = []
    for k in range(1, size):
        sent = lax.dynamic_index_in_dim(block, mine ^ k, 0, keepdims=False)
        pieces.append(lax.ppermute(sent, axis, [(i, i ^ k) for i in range(size)]))
    return lax.dynamic_index_in_dim(block, mine, 0, keepdims=False), pieces


def swap_cores(block):
    return lax.ppermute(block, "c", [(0, 1), (1, 0)])


def per_device(
    query_latent,
    query_rope,
    cache_latent,
    cache_rope,
    cache_lengths,
    value_up,
    out_proj,
    residual,
    norm_gain,
    router,
    trainer_gate,
    trainer_up,
    trainer_down,
    hot_experts,
    replica_index,
    token_experts,
    replica_pick,
):
    n_ep, n_y, n_c = lax.axis_size("ep"), lax.axis_size("y"), lax.axis_size("c")
    n_tp = n_y * n_c
    ep, y, c = lax.axis_index("ep"), lax.axis_index("y"), lax.axis_index("c")
    tp = y * n_c + c
    here, width = residual.shape
    tokens = here * n_ep
    quarter = tokens // n_tp
    experts = router.shape[1]
    block = out_proj.shape[0]
    sub = block // n_tp
    part = width // n_tp

    sub_wide = -(-sub // LANES) * LANES
    shares = residual.reshape(here, n_ep, n_tp, sub)
    shares = lax.dynamic_index_in_dim(shares, tp, 2, keepdims=False).transpose(1, 0, 2)
    shares = jnp.pad(shares, ((0, 0), (0, 0), (0, sub_wide - sub)))
    parcel = attend(
        query_latent, query_rope, cache_latent, cache_rope, cache_lengths, value_up, shares
    )
    inner = parcel.shape[2] - sub_wide
    landed = lax.all_to_all(parcel, "ep", split_axis=0, concat_axis=0, tiled=True)
    landed = landed.reshape(tokens, -1)
    at_row = lax.broadcasted_iota(jnp.int32, (sub_wide, block), 0)
    at_col = lax.broadcasted_iota(jnp.int32, (sub_wide, block), 1)
    spot = ((at_row + tp * sub == at_col) & (at_row < sub)).astype(bf16)
    column_part = lax.dot_general(
        landed[:, :inner], out_proj, (((1,), (1,)), ((), ())), preferred_element_type=f32
    ) + jnp.dot(landed[:, inner:], spot, preferred_element_type=f32)

    halves = column_part.reshape(n_y, n_c, quarter, block).transpose(1, 0, 2, 3)
    own, others = exchange(halves, "c", n_c, c)
    half = own + sum(others)
    own, others = exchange(half, "y", n_y, y)
    hidden_part = (own + sum(others)).astype(bf16)

    codes = keep_codes(token_experts, replica_pick, hot_experts, replica_index, experts)
    codes = jnp.pad(codes.astype(bf16), ((0, quarter - here), (0, 0)))
    wide = -(-(block + experts) // LANES) * LANES
    sent = jnp.concatenate(
        [hidden_part, codes, jnp.zeros((quarter, wide - block - experts), bf16)], axis=1
    )
    count = n_y * n_ep
    mine = lax.all_to_all(
        jnp.broadcast_to(sent[None], (count, quarter, wide)),
        ("y", "ep"),
        split_axis=0,
        concat_axis=0,
        tiled=True,
    ).reshape(n_y, n_ep, quarter, wide)
    other = swap_cores(mine)

    gain = norm_gain[None, :]
    weights = (trainer_gate[0], trainer_up[0], trainer_down[0])
    if block % 16 == 0 and tokens <= 256:
        keep, send = expert_block(
            jnp.stack([c, ep]), mine, other, gain, router, *weights, block
        )
    else:
        keep, send = expert_plain(ep, c, mine, other, gain, router, *weights, block)

    got = swap_cores(send)
    summed = (keep.astype(f32) + got.astype(f32)).astype(bf16)
    outbound = summed.reshape(count, here, part)
    returned = lax.all_to_all(outbound, ("y", "ep"), split_axis=0, concat_axis=0, tiled=True)
    moe = jnp.sum(returned.astype(f32), axis=0)

    per_part = n_ep // n_tp
    first = ep * here
    of_tp, row = first // quarter, first % quarter
    cut = lambda a: lax.dynamic_slice(
        a, (of_tp // n_c, tp * per_part, row, 0), (1, per_part, here, block)
    )[0]
    hidden_own = jnp.where(of_tp % n_c == c, cut(mine), cut(other))
    hidden_own = hidden_own.transpose(1, 0, 2).reshape(here, part).astype(f32)
    return (hidden_own + moe).astype(bf16)


def solution(mesh):
    n_ep, n_tp = mesh.shape["ep"], mesh.shape["tp"]
    fine = Mesh(mesh.devices.reshape(n_ep, n_tp // CORES, CORES), ("ep", "y", "c"))
    tp = ("y", "c")
    placed = (
        P("ep", tp, None),
        P("ep", tp, None),
        P("ep", None, None),
        P("ep", None, None),
        P("ep"),
        P(tp, None, None),
        P("ep", tp),
        P("ep", None),
        P(),
        P(),
        P("ep", None, tp),
        P("ep", None, tp),
        P("ep", tp, None),
        P(),
        P(),
        P("ep", None),
        P("ep", None),
    )
    return jax.shard_map(
        per_device, mesh=fine, in_specs=placed, out_specs=P("ep", tp), check_vma=False
    )
```

```python
import functools

import jax
import jax.numpy as jnp
from jax import lax
from jax.experimental import pallas as pl
from jax.experimental.pallas import tpu as pltpu
from jax.sharding import Mesh, PartitionSpec as P

TOPK = 8
SLOT_DEV = 2
CAP = 2
HOT = 2
CORES = 2
LANES = 128

score_scale = 192.0 ** (-0.5)
route_scale = 2.5
norm_eps = 1e-06
bf16 = jnp.bfloat16
f32 = jnp.float32


def keep_codes(token_experts, replica_pick, hot_experts, replica_index, experts):
    ids = lax.iota(jnp.int32, experts)
    held = jnp.where(
        replica_index[:, None] == lax.iota(jnp.int32, HOT)[None, :], hot_experts[None, :], 0
    ).sum(axis=1)
    count = 1 + jnp.sum((held[:, None] == ids[None, :]).astype(jnp.int32), axis=0)
    match = token_experts[:, :, None] == ids[None, None, :]
    named = jnp.any(match, axis=1)
    place = jnp.sum(jnp.where(match, replica_pick[:, :, None], 0), axis=1) % count[None, :]
    place = jnp.where(named, place, -1)
    tokens = lax.iota(jnp.int32, place.shape[0])
    ahead = (tokens[None, :] < tokens[:, None])[:, :, None] & (
        place[None, :, :] == place[:, None, :]
    )
    prior = jnp.sum(ahead.astype(jnp.int32), axis=1)
    return jnp.where(named, jnp.where(prior < CAP, 2.0, 1.0), 0.0)


def attend_kernel(
    steps, sub, block, lengths, ql, qr, cl, cr, residual, vu_hbm, out, lat, vu, wide_res, sem
):
    step = pl.program_id(0)
    per, heads = ql.shape[:2]
    here = per * steps
    tp = lax.axis_index("y") * lax.axis_size("c") + lax.axis_index("c")
    copy = pltpu.make_async_copy(vu_hbm, vu, sem)
    vdim = vu.shape[2]
    values = heads * vdim

    @pl.when(step == 0)
    def _():
        copy.start()
        width = residual.shape[1]
        wide_res[...] = residual[...].astype(f32)
        span = 2 * LANES
        lane = lax.broadcasted_iota(jnp.int32, (here, LANES), 1)
        for j in range(out.shape[0]):
            base = j * block + tp * sub
            start = jnp.minimum(base // LANES * LANES, width - span)
            piece = wide_res[:, pl.ds(pl.multiple_of(start, LANES), span)]
            piece = pltpu.roll(piece, span - (base - start), axis=1)[:, :LANES]
            out[j, :, values:] = jnp.where(lane < sub, piece, 0.0).astype(bf16)

    scores = [
        lax.dot_general(ql[i], cl[i], (((1,), (1,)), ((), ())), preferred_element_type=f32)
        for i in range(per)
    ]
    scores = [
        (s + jnp.dot(qr[i], cr[i], preferred_element_type=f32)) * score_scale
        for i, s in enumerate(scores)
    ]
    places = lax.broadcasted_iota(jnp.int32, scores[0].shape, 1)
    scores = [
        jnp.where(places < lengths[step * per + i], s, -1e30) for i, s in enumerate(scores)
    ]
    peaks = [jnp.max(s, axis=1, keepdims=True) for s in scores]
    shifted = [jnp.exp(s - m) for s, m in zip(scores, peaks)]
    inverse = [1.0 / jnp.sum(p, axis=1, keepdims=True) for p in shifted]
    mixed = [
        jnp.dot(p.astype(bf16), cl[i], preferred_element_type=f32)
        for i, p in enumerate(shifted)
    ]
    for i in range(per):
        got = mixed[i] * inverse[i]
        for j in range(lat.shape[0]):
            lat[j, pl.ds((step * per + i) * heads, heads), :] = got[
                :, j * LANES : (j + 1) * LANES
            ]

    @pl.when(step == steps - 1)
    def _():
        copy.wait()
        head_rows = lambda h: jnp.concatenate(
            [lat[j, pl.ds(h, here, stride=heads), :] for j in range(lat.shape[0])], axis=1
        ).astype(bf16)
        for h in range(0, heads, 2):
            rows = jnp.concatenate([head_rows(h), head_rows(h + 1)], axis=0)
            both = jnp.concatenate([vu[h], vu[h + 1]], axis=1)
            got = jnp.dot(rows, both, preferred_element_type=f32).astype(bf16)
            for j in range(out.shape[0]):
                out[j, :, h * vdim : (h + 1) * vdim] = got[:here, :vdim]
                out[j, :, (h + 1) * vdim : (h + 2) * vdim] = got[here:, vdim:]


def attend(
    query_latent, query_rope, cache_latent, cache_rope, lengths, value_up, residual, dests, sub, block
):
    here, heads, latent = query_latent.shape
    rope, places = cache_rope.shape[1:]
    vdim = value_up.shape[2]
    steps = 4
    per = here // steps
    spec = lambda *dims: pl.BlockSpec((per,) + dims, lambda t: (t,) + (0,) * len(dims))
    whole = lambda shape: pl.BlockSpec(shape, lambda t: (0,) * len(shape))
    out_shape = (dests, here, heads * vdim + LANES)
    return pl.pallas_call(
        functools.partial(attend_kernel, steps, sub, block),
        grid=(steps,),
        out_shape=jax.ShapeDtypeStruct(out_shape, bf16),
        in_specs=[
            pl.BlockSpec(memory_space=pltpu.SMEM),
            spec(heads, latent),
            spec(heads, rope),
            spec(places, latent),
            spec(rope, places),
            whole(residual.shape),
            pl.BlockSpec(memory_space=pl.ANY),
        ],
        out_specs=whole(out_shape),
        scratch_shapes=[
            pltpu.VMEM((latent // LANES, here * heads, LANES), f32),
            pltpu.VMEM(value_up.shape, bf16),
            pltpu.VMEM(residual.shape, f32),
            pltpu.SemaphoreType.DMA,
        ],
        compiler_params=pltpu.CompilerParams(
            dimension_semantics=("arbitrary",), vmem_limit_bytes=24 * 2**20
        ),
        name="attend",
    )(lengths, query_latent, query_rope, cache_latent, cache_rope, residual, value_up)


def expert_kernel(dims, mine, other, gate, up, down, keep_out, send_out, extras):
    n_ep, n_y, quarter, block, experts, part = dims
    core, ep = lax.axis_index("c"), lax.axis_index("ep")
    half = n_y * quarter
    here = 2 * half // n_ep
    per_quarter = quarter // here
    spare = mine.shape[3] - block

    lane = lax.broadcasted_iota(jnp.int32, (half, LANES), 1)
    sums = []
    sides = []
    for src in (mine, other):
        pieces = []
        total = jnp.zeros((half, LANES), f32)
        for j in range(0, n_ep, 2):
            low = src[:, j].reshape(half, -1)
            high = src[:, j + 1].reshape(half, -1)
            shared = jnp.where(lane < spare, low[:, -LANES:], high[:, :LANES])
            pieces += [low[:, :-LANES], shared, high[:, LANES:]]
            total += jnp.where(
                lane < spare, high[:, :LANES].astype(f32), low[:, -LANES:].astype(f32)
            )
        sides.append(jnp.concatenate(pieces, axis=1))
        sums.append(total)
    x = jnp.concatenate(sides, axis=0)
    total = jnp.concatenate(sums, axis=0)
    total = total[:, :spare] + total[:, spare:]
    for j in range(n_ep):
        y_of, rest = j // (per_quarter * 2), j % (per_quarter * 2)
        core_of, slot = rest // per_quarter, rest % per_quarter
        at = jnp.where(core == core_of, 0, half) + y_of * quarter + slot * here
        own = mine[0, j, :here, :]
        own = own[:, :spare] if j % 2 else own[:, block:]
        extras[pl.ds(pl.multiple_of(at, here), here), :] = own.astype(f32)
    square, logits, code = spare_lanes(total, extras[...], experts)

    gate_val = jnp.dot(x, gate[...], preferred_element_type=f32)
    up_val = jnp.dot(x, up[...], preferred_element_type=f32)
    scale = lax.rsqrt(square / (n_ep * block) + norm_eps)
    weight = row_weight(logits * scale, code, ep)
    act = (jax.nn.silu(gate_val * scale) * (up_val * (scale * weight))).astype(bf16)
    for flip, out in ((1, send_out), (0, keep_out)):
        to_core = jnp.where(core == 0, flip, 1 - flip)
        for y in range(n_y):
            cols = pl.ds(pl.multiple_of((y * 2 + to_core) * part, LANES), part)
            got = jnp.dot(act, down[:, cols], preferred_element_type=f32).astype(bf16)
            for i in range(2):
                of_core = jnp.where(core == 0, i, 1 - i)
                for q in range(n_y):
                    at = pl.multiple_of((q * 2 + of_core) * quarter, quarter)
                    src = i * half + q * quarter
                    out[y, pl.ds(at, quarter), :] = got[src : src + quarter, :]


def spare_lanes(total, own, experts):
    square = total[:, 0:1] + total[:, 1:2]
    logits = total[:, 2 : 2 + experts] + total[:, 2 + experts : 2 + 2 * experts]
    return square, logits, own[:, 2 + 2 * experts : 2 + 3 * experts]


def row_weight(logits, code, ep):
    affinity = jnp.where(code > 0.5, jax.nn.sigmoid(logits), 0.0)
    gates = route_scale * affinity / jnp.sum(affinity, axis=1, keepdims=True)
    mine_only = lax.broadcasted_iota(jnp.int32, gates.shape, 1) == ep
    return jnp.sum(jnp.where(mine_only & (code > 1.5), gates, 0.0), axis=1, keepdims=True)


def expert_block(mine, other, gate, up, down, block, experts):
    n_y, n_ep, quarter, wide = mine.shape
    tokens = 2 * n_y * quarter
    part = down.shape[1] // (2 * n_y)
    dims = (n_ep, n_y, quarter, block, experts, part)
    vmem = pl.BlockSpec(memory_space=pltpu.VMEM)
    shape = jax.ShapeDtypeStruct((n_y, tokens, part), bf16)
    return pl.pallas_call(
        functools.partial(expert_kernel, dims),
        out_shape=(shape, shape),
        in_specs=[vmem] * 5,
        out_specs=(vmem, vmem),
        scratch_shapes=[pltpu.VMEM((tokens, wide - block), f32)],
        compiler_params=pltpu.CompilerParams(vmem_limit_bytes=24 * 2**20),
        name="experts",
    )(mine, other, gate, up, down)


def expert_plain(ep, c, mine, other, gate, up, down, block, experts):
    n_y, n_ep, quarter, _ = mine.shape
    tokens = 2 * n_y * quarter
    here = tokens // n_ep
    part = down.shape[1] // (2 * n_y)
    both = jnp.stack([jnp.where(c == 0, mine, other), jnp.where(c == 0, other, mine)], axis=1)
    own = both[0, 0, :, :here, block:].reshape(tokens, -1).astype(f32)
    total = jnp.sum(both[..., block:].astype(f32), axis=2).reshape(tokens, -1)
    square, logits, code = spare_lanes(total, own, experts)
    x = both[..., :block].transpose(0, 1, 3, 2, 4).reshape(tokens, -1)
    scale = lax.rsqrt(square / x.shape[1] + norm_eps)
    weight = row_weight(logits * scale, code, ep)
    gate_val = jnp.dot(x, gate, preferred_element_type=f32) * scale
    up_val = jnp.dot(x, up, preferred_element_type=f32) * scale
    act = (jax.nn.silu(gate_val) * up_val * weight).astype(bf16)
    partial = jnp.dot(act, down, preferred_element_type=f32).astype(bf16)
    split = partial.reshape(tokens, n_y, 2, part).transpose(2, 1, 0, 3)
    return (
        lax.dynamic_index_in_dim(split, c, 0, keepdims=False),
        lax.dynamic_index_in_dim(split, 1 - c, 0, keepdims=False),
    )


def exchange(block, axis, size, mine):
    pieces = []
    for k in range(1, size):
        sent = lax.dynamic_index_in_dim(block, mine ^ k, 0, keepdims=False)
        pieces.append(lax.ppermute(sent, axis, [(i, i ^ k) for i in range(size)]))
    return lax.dynamic_index_in_dim(block, mine, 0, keepdims=False), pieces


def high_low(value):
    high = lax.reduce_precision(value, 8, 7)
    return [high.astype(bf16), (value - high).astype(bf16)]


def swap_cores(block):
    return lax.ppermute(block, "c", [(0, 1), (1, 0)])


def per_device(
    query_latent,
    query_rope,
    cache_latent,
    cache_rope,
    cache_lengths,
    value_up,
    out_proj,
    residual,
    norm_gain,
    router,
    trainer_gate,
    trainer_up,
    trainer_down,
    hot_experts,
    replica_index,
    token_experts,
    replica_pick,
):
    n_ep, n_y, n_c = lax.axis_size("ep"), lax.axis_size("y"), lax.axis_size("c")
    n_tp = n_y * n_c
    ep, y, c = lax.axis_index("ep"), lax.axis_index("y"), lax.axis_index("c")
    tp = y * n_c + c
    here, width = residual.shape
    tokens = here * n_ep
    quarter = tokens // n_tp
    experts = router.shape[1]
    block = out_proj.shape[0]
    sub = block // n_tp
    part = width // n_tp

    parcel = attend(
        query_latent, query_rope, cache_latent, cache_rope, cache_lengths, value_up,
        residual, n_ep, sub, block,
    )
    sub_wide = LANES
    inner = parcel.shape[2] - sub_wide
    landed = lax.all_to_all(parcel, "ep", split_axis=0, concat_axis=0, tiled=True)
    landed = landed.reshape(tokens, -1)
    at_row = lax.broadcasted_iota(jnp.int32, (sub_wide, block), 0)
    at_col = lax.broadcasted_iota(jnp.int32, (sub_wide, block), 1)
    spot = ((at_row + tp * sub == at_col) & (at_row < sub)).astype(bf16)
    column_part = lax.dot_general(
        landed[:, :inner], out_proj, (((1,), (1,)), ((), ())), preferred_element_type=f32
    ) + jnp.dot(landed[:, inner:], spot, preferred_element_type=f32)

    halves = column_part.reshape(n_y, n_c, quarter, block).transpose(1, 0, 2, 3)
    own, others = exchange(halves, "c", n_c, c)
    half = own + sum(others)
    own, others = exchange(half, "y", n_y, y)
    hidden_part = own + sum(others)

    codes = keep_codes(token_experts, replica_pick, hot_experts, replica_index, experts)
    codes = jnp.pad(codes.astype(bf16), ((0, quarter - here), (0, 0)))
    gain_part = lax.dynamic_slice_in_dim(norm_gain, ep * block, block, 0)
    router_part = lax.dynamic_slice_in_dim(router, ep * block, block, 0)
    scaled = (hidden_part * gain_part[None, :]).astype(bf16)
    square = jnp.sum(hidden_part * hidden_part, axis=1, keepdims=True)
    logits = jnp.dot(scaled, router_part, preferred_element_type=f32)
    wide = -(-(block + 2 + 3 * experts) // LANES) * LANES
    extras = jnp.concatenate(
        high_low(square)
        + high_low(logits)
        + [codes, jnp.zeros((quarter, wide - block - 2 - 3 * experts), bf16)],
        axis=1,
    )
    paired = block % LANES == LANES // 2 == wide - block and n_ep // n_tp % 2 == 0
    sent = jnp.concatenate([scaled, extras], axis=1)
    if paired:
        sent = jnp.where(ep % 2 == 0, sent, jnp.concatenate([extras, scaled], axis=1))
    count = n_y * n_ep
    mine = lax.all_to_all(
        jnp.broadcast_to(sent[None], (count, quarter, wide)),
        ("y", "ep"),
        split_axis=0,
        concat_axis=0,
        tiled=True,
    ).reshape(n_y, n_ep, quarter, wide)
    other = swap_cores(mine)

    weights = (trainer_gate[0], trainer_up[0], trainer_down[0])
    if paired and block % 16 == 0 and tokens <= 256:
        keep, send = expert_block(mine, other, *weights, block, experts)
    else:
        keep, send = expert_plain(ep, c, mine, other, *weights, block, experts)

    got = swap_cores(send)
    summed = (keep.astype(f32) + got.astype(f32)).astype(bf16)
    outbound = summed.reshape(count, here, part)
    returned = lax.all_to_all(outbound, ("y", "ep"), split_axis=0, concat_axis=0, tiled=True)
    moe = jnp.sum(returned.astype(f32), axis=0)

    per_part = n_ep // n_tp
    first = ep * here
    of_tp, row = first // quarter, first % quarter
    cut = lambda a: lax.dynamic_slice(
        a, (of_tp // n_c, tp * per_part, row, 0), (1, per_part, here, wide)
    )[0]
    rows = jnp.where(of_tp % n_c == c, cut(mine), cut(other))
    pieces = [
        rows[j, :, wide - block :] if paired and j % 2 else rows[j, :, :block]
        for j in range(per_part)
    ]
    gain_own = lax.dynamic_slice_in_dim(norm_gain, tp * part, part, 0)
    hidden_own = jnp.concatenate(pieces, axis=1).astype(f32) / gain_own[None, :]
    return (hidden_own + moe).astype(bf16)


def solution(mesh):
    n_ep, n_tp = mesh.shape["ep"], mesh.shape["tp"]
    fine = Mesh(mesh.devices.reshape(n_ep, n_tp // CORES, CORES), ("ep", "y", "c"))
    tp = ("y", "c")
    placed = (
        P("ep", tp, None),
        P("ep", tp, None),
        P("ep", None, None),
        P("ep", None, None),
        P("ep"),
        P(tp, None, None),
        P("ep", tp),
        P("ep", None),
        P(),
        P(),
        P("ep", None, tp),
        P("ep", None, tp),
        P("ep", tp, None),
        P(),
        P(),
        P("ep", None),
        P("ep", None),
    )
    return jax.shard_map(
        per_device, mesh=fine, in_specs=placed, out_specs=P("ep", tp), check_vma=False
    )
```

```python
import functools

import jax
import jax.numpy as jnp
from jax import lax
from jax.experimental import pallas as pl
from jax.experimental.pallas import tpu as pltpu
from jax.sharding import Mesh, PartitionSpec as P

TOPK = 8
SLOT_DEV = 2
CAP = 2
HOT = 2
CORES = 2
LANES = 128

score_scale = 192.0 ** (-0.5)
route_scale = 2.5
norm_eps = 1e-06
bf16 = jnp.bfloat16
f32 = jnp.float32


def keep_codes(token_experts, replica_pick, hot_experts, replica_index, experts):
    ids = lax.iota(jnp.int32, experts)
    held = jnp.where(
        replica_index[:, None] == lax.iota(jnp.int32, HOT)[None, :], hot_experts[None, :], 0
    ).sum(axis=1)
    count = 1 + jnp.sum((held[:, None] == ids[None, :]).astype(jnp.int32), axis=0)
    match = token_experts[:, :, None] == ids[None, None, :]
    named = jnp.any(match, axis=1)
    place = jnp.sum(jnp.where(match, replica_pick[:, :, None], 0), axis=1) % count[None, :]
    place = jnp.where(named, place, -1)
    tokens = lax.iota(jnp.int32, place.shape[0])
    ahead = (tokens[None, :] < tokens[:, None])[:, :, None] & (
        place[None, :, :] == place[:, None, :]
    )
    prior = jnp.sum(ahead.astype(jnp.int32), axis=1)
    return jnp.where(named, jnp.where(prior < CAP, 2.0, 1.0), 0.0)


def attend_kernel(
    steps, sub, block, lengths, ql, qr, cl, cr, residual, vu_hbm, out, lat, vu, wide_res, sem
):
    step = pl.program_id(0)
    per, heads = ql.shape[:2]
    here = per * steps
    tp = lax.axis_index("y") * lax.axis_size("c") + lax.axis_index("c")
    copy = pltpu.make_async_copy(vu_hbm, vu, sem)
    vdim = vu.shape[2]
    values = heads * vdim

    @pl.when(step == 0)
    def _():
        copy.start()
        width = residual.shape[1]
        wide_res[...] = residual[...].astype(f32)
        span = 2 * LANES
        lane = lax.broadcasted_iota(jnp.int32, (here, LANES), 1)
        for j in range(out.shape[0]):
            base = j * block + tp * sub
            start = jnp.minimum(base // LANES * LANES, width - span)
            piece = wide_res[:, pl.ds(pl.multiple_of(start, LANES), span)]
            piece = pltpu.roll(piece, span - (base - start), axis=1)[:, :LANES]
            out[j, :, values:] = jnp.where(lane < sub, piece, 0.0).astype(bf16)

    scores = [
        lax.dot_general(ql[i], cl[i], (((1,), (1,)), ((), ())), preferred_element_type=f32)
        for i in range(per)
    ]
    scores = [
        (s + jnp.dot(qr[i], cr[i], preferred_element_type=f32)) * score_scale
        for i, s in enumerate(scores)
    ]
    places = lax.broadcasted_iota(jnp.int32, scores[0].shape, 1)
    scores = [
        jnp.where(places < lengths[step * per + i], s, -1e30) for i, s in enumerate(scores)
    ]
    peaks = [jnp.max(s, axis=1, keepdims=True) for s in scores]
    shifted = [jnp.exp(s - m) for s, m in zip(scores, peaks)]
    inverse = [1.0 / jnp.sum(p, axis=1, keepdims=True) for p in shifted]
    mixed = [
        jnp.dot(p.astype(bf16), cl[i], preferred_element_type=f32)
        for i, p in enumerate(shifted)
    ]
    for i in range(per):
        got = mixed[i] * inverse[i]
        for j in range(lat.shape[0]):
            lat[j, pl.ds((step * per + i) * heads, heads), :] = got[
                :, j * LANES : (j + 1) * LANES
            ]

    @pl.when(step == steps - 1)
    def _():
        copy.wait()
        head_rows = lambda h: jnp.concatenate(
            [lat[j, pl.ds(h, here, stride=heads), :] for j in range(lat.shape[0])], axis=1
        ).astype(bf16)
        for h in range(0, heads, 2):
            rows = jnp.concatenate([head_rows(h), head_rows(h + 1)], axis=0)
            both = jnp.concatenate([vu[h], vu[h + 1]], axis=1)
            got = jnp.dot(rows, both, preferred_element_type=f32).astype(bf16)
            for j in range(out.shape[0]):
                out[j, :, h * vdim : (h + 1) * vdim] = got[:here, :vdim]
                out[j, :, (h + 1) * vdim : (h + 2) * vdim] = got[here:, vdim:]


def in_hbm(array):
    return pltpu.with_memory_space_constraint(array, pltpu.HBM)


def fetch_kernel(count, *refs):
    sems = refs[-1]
    ins, outs = refs[:count], refs[count : 2 * count]
    copies = [pltpu.make_async_copy(a, b, sems.at[i]) for i, (a, b) in enumerate(zip(ins, outs))]
    for copy in copies:
        copy.start()
    for copy in copies:
        copy.wait()


def fetch(*arrays):
    count = len(arrays)
    return pl.pallas_call(
        functools.partial(fetch_kernel, count),
        out_shape=tuple(jax.ShapeDtypeStruct(a.shape, a.dtype) for a in arrays),
        in_specs=[pl.BlockSpec(memory_space=pl.ANY)] * count,
        out_specs=(pl.BlockSpec(memory_space=pltpu.VMEM),) * count,
        scratch_shapes=[pltpu.SemaphoreType.DMA((count,))],
        compiler_params=pltpu.CompilerParams(vmem_limit_bytes=12 * 2**20),
        cost_estimate=pl.CostEstimate(
            flops=0, bytes_accessed=sum(2 * a.size * a.dtype.itemsize for a in arrays), transcendentals=0
        ),
        name="fetch",
    )(*map(in_hbm, arrays))


def project_kernel(sub, landed, out_proj, keep, send):
    n_y, quarter, block = keep.shape
    tokens = landed.shape[0]
    inner = out_proj.shape[1]
    core = lax.axis_index("c")
    tp = lax.axis_index("y") * lax.axis_size("c") + core
    rest = landed.shape[1] - inner
    at_row = lax.broadcasted_iota(jnp.int32, (rest, block), 0)
    at_col = lax.broadcasted_iota(jnp.int32, (rest, block), 1)
    spot = jnp.where((at_row + tp * sub == at_col) & (at_row < sub), 1.0, 0.0).astype(bf16)
    part = lax.dot_general(
        landed[:, :inner], out_proj[...], (((1,), (1,)), ((), ())), preferred_element_type=f32
    ) + jnp.dot(landed[:, inner:], spot, preferred_element_type=f32)
    for y in range(n_y):
        zero = part[2 * y * quarter : (2 * y + 1) * quarter]
        one = part[(2 * y + 1) * quarter : (2 * y + 2) * quarter]
        keep[y] = jnp.where(core == 0, zero, one)
        send[y] = jnp.where(core == 0, one, zero)


def project(landed, out_proj, sub, n_y):
    tokens = landed.shape[0]
    block = out_proj.shape[0]
    vmem = pl.BlockSpec(memory_space=pltpu.VMEM)
    shape = jax.ShapeDtypeStruct((n_y, tokens // (2 * n_y), block), f32)
    return pl.pallas_call(
        functools.partial(project_kernel, sub),
        out_shape=(shape, shape),
        in_specs=[vmem] * 2,
        out_specs=(vmem, vmem),
        compiler_params=pltpu.CompilerParams(vmem_limit_bytes=8 * 2**20),
        name="project",
    )(landed, out_proj)


def bundle_kernel(own, got, gain, router_t, codes, out):
    hidden = own[...] + got[...]
    rows, block = hidden.shape
    experts = router_t.shape[0]
    scaled = (hidden * gain[...]).astype(bf16)
    square = jnp.sum(hidden * hidden, axis=1, keepdims=True)
    logits = lax.dot_general(
        scaled, router_t[...], (((1,), (1,)), ((), ())), preferred_element_type=f32
    )
    spare = out.shape[2] - block
    both = high_low(square) + high_low(logits) + [codes[...]]
    extras = jnp.concatenate(
        [b.astype(f32) for b in both] + [jnp.zeros((rows, spare - 2 - 3 * experts), f32)], axis=1
    ).astype(bf16)
    odd = lax.rem(lax.axis_index("ep"), 2) == 1

    @pl.when(jnp.logical_not(odd))
    def _():
        row = jnp.concatenate([scaled, extras], axis=1)
        for j in range(out.shape[0]):
            out[j] = row

    @pl.when(odd)
    def _():
        row = jnp.concatenate([extras, scaled], axis=1)
        for j in range(out.shape[0]):
            out[j] = row


def bundle(own, got, gain, router_t, codes, count, wide):
    rows = own.shape[0]
    vmem = pl.BlockSpec(memory_space=pltpu.VMEM)
    return pl.pallas_call(
        bundle_kernel,
        out_shape=jax.ShapeDtypeStruct((count, rows, wide), bf16),
        in_specs=[vmem] * 5,
        out_specs=vmem,
        compiler_params=pltpu.CompilerParams(vmem_limit_bytes=4 * 2**20),
        name="bundle",
    )(own, got, gain, router_t, codes)


def attend(
    query_latent, query_rope, cache_latent, cache_rope, lengths, value_up, residual, dests, sub, block
):
    here, heads, latent = query_latent.shape
    rope, places = cache_rope.shape[1:]
    vdim = value_up.shape[2]
    steps = 4
    per = here // steps
    spec = lambda *dims: pl.BlockSpec((per,) + dims, lambda t: (t,) + (0,) * len(dims))
    whole = lambda shape: pl.BlockSpec(shape, lambda t: (0,) * len(shape))
    out_shape = (dests, here, heads * vdim + LANES)
    return pl.pallas_call(
        functools.partial(attend_kernel, steps, sub, block),
        grid=(steps,),
        out_shape=jax.ShapeDtypeStruct(out_shape, bf16),
        in_specs=[
            pl.BlockSpec(memory_space=pltpu.SMEM),
            spec(heads, latent),
            spec(heads, rope),
            spec(places, latent),
            spec(rope, places),
            whole(residual.shape),
            pl.BlockSpec(memory_space=pl.ANY),
        ],
        out_specs=whole(out_shape),
        scratch_shapes=[
            pltpu.VMEM((latent // LANES, here * heads, LANES), f32),
            pltpu.VMEM(value_up.shape, bf16),
            pltpu.VMEM(residual.shape, f32),
            pltpu.SemaphoreType.DMA,
        ],
        compiler_params=pltpu.CompilerParams(
            dimension_semantics=("arbitrary",), vmem_limit_bytes=24 * 2**20
        ),
        name="attend",
    )(lengths, *map(in_hbm, (query_latent, query_rope, cache_latent, cache_rope, residual, value_up)))


def expert_kernel(dims, mine, other, gate, up, down, keep_out, send_out, extras):
    n_ep, n_y, quarter, block, experts, part = dims
    core, ep = lax.axis_index("c"), lax.axis_index("ep")
    half = n_y * quarter
    here = 2 * half // n_ep
    per_quarter = quarter // here
    spare = mine.shape[3] - block

    lane = lax.broadcasted_iota(jnp.int32, (half, LANES), 1)
    sums = []
    sides = []
    for src in (mine, other):
        pieces = []
        total = jnp.zeros((half, LANES), f32)
        for j in range(0, n_ep, 2):
            low = src[:, j].reshape(half, -1)
            high = src[:, j + 1].reshape(half, -1)
            shared = jnp.where(lane < spare, low[:, -LANES:], high[:, :LANES])
            pieces += [low[:, :-LANES], shared, high[:, LANES:]]
            total += jnp.where(
                lane < spare, high[:, :LANES].astype(f32), low[:, -LANES:].astype(f32)
            )
        sides.append(jnp.concatenate(pieces, axis=1))
        sums.append(total)
    x = jnp.concatenate(sides, axis=0)
    total = jnp.concatenate(sums, axis=0)
    total = total[:, :spare] + total[:, spare:]
    for j in range(n_ep):
        y_of, rest = j // (per_quarter * 2), j % (per_quarter * 2)
        core_of, slot = rest // per_quarter, rest % per_quarter
        at = jnp.where(core == core_of, 0, half) + y_of * quarter + slot * here
        own = mine[0, j, :here, :]
        own = own[:, :spare] if j % 2 else own[:, block:]
        extras[pl.ds(pl.multiple_of(at, here), here), :] = own.astype(f32)
    square, logits, code = spare_lanes(total, extras[...], experts)

    gate_val = jnp.dot(x, gate[...], preferred_element_type=f32)
    up_val = jnp.dot(x, up[...], preferred_element_type=f32)
    scale = lax.rsqrt(square / (n_ep * block) + norm_eps)
    weight = row_weight(logits * scale, code, ep)
    act = (jax.nn.silu(gate_val * scale) * (up_val * (scale * weight))).astype(bf16)
    for flip, out in ((1, send_out), (0, keep_out)):
        to_core = jnp.where(core == 0, flip, 1 - flip)
        for y in range(n_y):
            cols = pl.ds(pl.multiple_of((y * 2 + to_core) * part, LANES), part)
            got = jnp.dot(act, down[:, cols], preferred_element_type=f32).astype(bf16)
            for i in range(2):
                of_core = jnp.where(core == 0, i, 1 - i)
                for q in range(n_y):
                    at = pl.multiple_of((q * 2 + of_core) * quarter, quarter)
                    src = i * half + q * quarter
                    out[y, pl.ds(at, quarter), :] = got[src : src + quarter, :]


def spare_lanes(total, own, experts):
    square = total[:, 0:1] + total[:, 1:2]
    logits = total[:, 2 : 2 + experts] + total[:, 2 + experts : 2 + 2 * experts]
    return square, logits, own[:, 2 + 2 * experts : 2 + 3 * experts]


def row_weight(logits, code, ep):
    affinity = jnp.where(code > 0.5, jax.nn.sigmoid(logits), 0.0)
    gates = route_scale * affinity / jnp.sum(affinity, axis=1, keepdims=True)
    mine_only = lax.broadcasted_iota(jnp.int32, gates.shape, 1) == ep
    return jnp.sum(jnp.where(mine_only & (code > 1.5), gates, 0.0), axis=1, keepdims=True)


def expert_block(mine, other, gate, up, down, block, experts):
    n_y, n_ep, quarter, wide = mine.shape
    tokens = 2 * n_y * quarter
    part = down.shape[1] // (2 * n_y)
    dims = (n_ep, n_y, quarter, block, experts, part)
    vmem = pl.BlockSpec(memory_space=pltpu.VMEM)
    shape = jax.ShapeDtypeStruct((n_y, tokens, part), bf16)
    return pl.pallas_call(
        functools.partial(expert_kernel, dims),
        out_shape=(shape, shape),
        in_specs=[vmem] * 5,
        out_specs=(vmem, vmem),
        scratch_shapes=[pltpu.VMEM((tokens, wide - block), f32)],
        compiler_params=pltpu.CompilerParams(vmem_limit_bytes=24 * 2**20),
        name="experts",
    )(mine, other, gate, up, down)


def expert_plain(ep, c, mine, other, gate, up, down, block, experts):
    n_y, n_ep, quarter, _ = mine.shape
    tokens = 2 * n_y * quarter
    here = tokens // n_ep
    part = down.shape[1] // (2 * n_y)
    both = jnp.stack([jnp.where(c == 0, mine, other), jnp.where(c == 0, other, mine)], axis=1)
    own = both[0, 0, :, :here, block:].reshape(tokens, -1).astype(f32)
    total = jnp.sum(both[..., block:].astype(f32), axis=2).reshape(tokens, -1)
    square, logits, code = spare_lanes(total, own, experts)
    x = both[..., :block].transpose(0, 1, 3, 2, 4).reshape(tokens, -1)
    scale = lax.rsqrt(square / x.shape[1] + norm_eps)
    weight = row_weight(logits * scale, code, ep)
    gate_val = jnp.dot(x, gate, preferred_element_type=f32) * scale
    up_val = jnp.dot(x, up, preferred_element_type=f32) * scale
    act = (jax.nn.silu(gate_val) * up_val * weight).astype(bf16)
    partial = jnp.dot(act, down, preferred_element_type=f32).astype(bf16)
    split = partial.reshape(tokens, n_y, 2, part).transpose(2, 1, 0, 3)
    return (
        lax.dynamic_index_in_dim(split, c, 0, keepdims=False),
        lax.dynamic_index_in_dim(split, 1 - c, 0, keepdims=False),
    )


def exchange(block, axis, size, mine):
    pieces = []
    for k in range(1, size):
        sent = lax.dynamic_index_in_dim(block, mine ^ k, 0, keepdims=False)
        pieces.append(lax.ppermute(sent, axis, [(i, i ^ k) for i in range(size)]))
    return lax.dynamic_index_in_dim(block, mine, 0, keepdims=False), pieces


def high_low(value):
    high = lax.reduce_precision(value, 8, 7)
    return [high, value - high]


def swap_cores(block):
    return lax.ppermute(block, "c", [(0, 1), (1, 0)])


def per_device(
    query_latent,
    query_rope,
    cache_latent,
    cache_rope,
    cache_lengths,
    value_up,
    out_proj,
    residual,
    norm_gain,
    router,
    trainer_gate,
    trainer_up,
    trainer_down,
    hot_experts,
    replica_index,
    token_experts,
    replica_pick,
):
    n_ep, n_y, n_c = lax.axis_size("ep"), lax.axis_size("y"), lax.axis_size("c")
    n_tp = n_y * n_c
    ep, y, c = lax.axis_index("ep"), lax.axis_index("y"), lax.axis_index("c")
    tp = y * n_c + c
    here, width = residual.shape
    tokens = here * n_ep
    quarter = tokens // n_tp
    experts = router.shape[1]
    block = out_proj.shape[0]
    sub = block // n_tp
    part = width // n_tp

    parcel = attend(
        query_latent, query_rope, cache_latent, cache_rope, cache_lengths, value_up,
        residual, n_ep, sub, block,
    )
    sub_wide = LANES
    inner = parcel.shape[2] - sub_wide
    landed = lax.all_to_all(parcel, "ep", split_axis=0, concat_axis=0, tiled=True)
    landed = landed.reshape(tokens, -1)
    wide = -(-(block + 2 + 3 * experts) // LANES) * LANES
    paired = block % LANES == LANES // 2 == wide - block and n_ep // n_tp % 2 == 0
    paired = paired and block % 16 == 0 and tokens <= 256
    weights = (trainer_gate[0], trainer_up[0], trainer_down[0])
    gain_part = lax.dynamic_slice_in_dim(norm_gain, ep * block, block, 0)[None, :]
    router_part = lax.dynamic_slice_in_dim(router.T, ep * block, block, 1)
    if paired:
        keep, send = project(landed, out_proj, sub, n_y)
        half = keep + swap_cores(send)
    else:
        at_row = lax.broadcasted_iota(jnp.int32, (sub_wide, block), 0)
        at_col = lax.broadcasted_iota(jnp.int32, (sub_wide, block), 1)
        spot = ((at_row + tp * sub == at_col) & (at_row < sub)).astype(bf16)
        column_part = lax.dot_general(
            landed[:, :inner], out_proj, (((1,), (1,)), ((), ())), preferred_element_type=f32
        ) + jnp.dot(landed[:, inner:], spot, preferred_element_type=f32)
        halves = column_part.reshape(n_y, n_c, quarter, block).transpose(1, 0, 2, 3)
        own, others = exchange(halves, "c", n_c, c)
        half = own + sum(others)
    own, others = exchange(half, "y", n_y, y)

    codes = keep_codes(token_experts, replica_pick, hot_experts, replica_index, experts)
    codes = jnp.pad(codes.astype(bf16), ((0, quarter - here), (0, 0)))
    count = n_y * n_ep
    if paired:
        sent = bundle(own, sum(others), gain_part, router_part, codes, count, wide)
    else:
        hidden_part = own + sum(others)
        scaled = (hidden_part * gain_part).astype(bf16)
        square = jnp.sum(hidden_part * hidden_part, axis=1, keepdims=True)
        logits = jnp.dot(scaled, router_part.T, preferred_element_type=f32)
        both = high_low(square) + high_low(logits)
        sent = jnp.concatenate([scaled] + [b.astype(bf16) for b in both] + [codes], axis=1)
        sent = jnp.pad(sent, ((0, 0), (0, wide - sent.shape[1])))
        sent = jnp.broadcast_to(sent[None], (count, quarter, wide))
    mine = lax.all_to_all(
        sent, ("y", "ep"), split_axis=0, concat_axis=0, tiled=True
    ).reshape(n_y, n_ep, quarter, wide)
    other = swap_cores(mine)

    if paired:
        keep, send = expert_block(mine, other, *weights[:2], fetch(weights[2])[0], block, experts)
    else:
        keep, send = expert_plain(ep, c, mine, other, *weights, block, experts)

    got = swap_cores(send)
    summed = (keep.astype(f32) + got.astype(f32)).astype(bf16)
    outbound = summed.reshape(count, here, part)
    returned = lax.all_to_all(outbound, ("y", "ep"), split_axis=0, concat_axis=0, tiled=True)
    moe = jnp.sum(returned.astype(f32), axis=0)

    per_part = n_ep // n_tp
    first = ep * here
    of_tp, row = first // quarter, first % quarter
    cut = lambda a: lax.dynamic_slice(
        a, (of_tp // n_c, tp * per_part, row, 0), (1, per_part, here, wide)
    )[0]
    rows = jnp.where(of_tp % n_c == c, cut(mine), cut(other))
    pieces = [
        rows[j, :, wide - block :] if paired and j % 2 else rows[j, :, :block]
        for j in range(per_part)
    ]
    gain_own = lax.dynamic_slice_in_dim(norm_gain, tp * part, part, 0)
    hidden_own = jnp.concatenate(pieces, axis=1).astype(f32) / gain_own[None, :]
    return (hidden_own + moe).astype(bf16)


def solution(mesh):
    n_ep, n_tp = mesh.shape["ep"], mesh.shape["tp"]
    fine = Mesh(mesh.devices.reshape(n_ep, n_tp // CORES, CORES), ("ep", "y", "c"))
    tp = ("y", "c")
    placed = (
        P("ep", tp, None),
        P("ep", tp, None),
        P("ep", None, None),
        P("ep", None, None),
        P("ep"),
        P(tp, None, None),
        P("ep", tp),
        P("ep", None),
        P(),
        P(),
        P("ep", None, tp),
        P("ep", None, tp),
        P("ep", tp, None),
        P(),
        P(),
        P("ep", None),
        P("ep", None),
    )
    return jax.shard_map(
        per_device, mesh=fine, in_specs=placed, out_specs=P("ep", tp), check_vma=False
    )
```

```python
import functools

import jax
import jax.numpy as jnp
from jax import lax
from jax.experimental import pallas as pl
from jax.experimental.pallas import tpu as pltpu
from jax.sharding import Mesh, PartitionSpec as P

TOPK = 8
SLOT_DEV = 2
CAP = 2
HOT = 2
CORES = 2
LANES = 128

score_scale = 192.0 ** (-0.5)
route_scale = 2.5
norm_eps = 1e-06

bf16 = jnp.bfloat16
f32 = jnp.float32


def keep_codes(token_experts, replica_pick, hot_experts, replica_index, experts):
    ids = lax.iota(jnp.int32, experts)
    held = jnp.where(
        replica_index[:, None] == lax.iota(jnp.int32, HOT)[None, :], hot_experts[None, :], 0
    ).sum(axis=1)
    count = 1 + jnp.sum((held[:, None] == ids[None, :]).astype(jnp.int32), axis=0)
    match = token_experts[:, :, None] == ids[None, None, :]
    named = jnp.any(match, axis=1)
    place = jnp.sum(jnp.where(match, replica_pick[:, :, None], 0), axis=1) % count[None, :]
    place = jnp.where(named, place, -1)
    tokens = lax.iota(jnp.int32, place.shape[0])
    ahead = (tokens[None, :] < tokens[:, None])[:, :, None] & (
        place[None, :, :] == place[:, None, :]
    )
    prior = jnp.sum(ahead.astype(jnp.int32), axis=1)
    return jnp.where(named, jnp.where(prior < CAP, 2.0, 1.0), 0.0)


def attend_kernel(steps, dests, sub, block, lengths, ql, qr, cl, cr, residual, vu_hbm, *refs):
    *outs, lat, vu, wide_res, sem = refs
    apart = len(outs) > 1
    ep = lax.axis_index("ep")
    outs = outs if apart else [outs[0].at[j] for j in range(dests)]
    step = pl.program_id(0)
    per, heads = ql.shape[:2]
    here = per * steps
    tp = lax.axis_index("y") * lax.axis_size("c") + lax.axis_index("c")
    copy = pltpu.make_async_copy(vu_hbm, vu, sem)
    vdim = vu.shape[2]
    values = heads * vdim

    @pl.when(step == 0)
    def _():
        copy.start()
        width = residual.shape[1]
        wide_res[...] = residual[...].astype(f32)
        span = 2 * LANES
        lane = lax.broadcasted_iota(jnp.int32, (here, LANES), 1)
        for j, out in enumerate(outs):
            base = ((ep ^ j) if apart else j) * block + tp * sub
            start = jnp.minimum(base // LANES * LANES, width - span)
            piece = wide_res[:, pl.ds(pl.multiple_of(start, LANES), span)]
            piece = pltpu.roll(piece, span - (base - start), axis=1)[:, :LANES]
            out[:, values:] = jnp.where(lane < sub, piece, 0.0).astype(bf16)

    scores = [
        lax.dot_general(ql[i], cl[i], (((1,), (1,)), ((), ())), preferred_element_type=f32)
        for i in range(per)
    ]
    scores = [
        (s + jnp.dot(qr[i], cr[i], preferred_element_type=f32)) * score_scale
        for i, s in enumerate(scores)
    ]
    places = lax.broadcasted_iota(jnp.int32, scores[0].shape, 1)
    scores = [
        jnp.where(places < lengths[step * per + i], s, -1e30) for i, s in enumerate(scores)
    ]
    peaks = [jnp.max(s, axis=1, keepdims=True) for s in scores]
    shifted = [jnp.exp(s - m) for s, m in zip(scores, peaks)]
    inverse = [1.0 / jnp.sum(p, axis=1, keepdims=True) for p in shifted]
    mixed = [
        jnp.dot(p.astype(bf16), cl[i], preferred_element_type=f32)
        for i, p in enumerate(shifted)
    ]
    for i in range(per):
        got = mixed[i] * inverse[i]
        for j in range(lat.shape[0]):
            lat[j, pl.ds((step * per + i) * heads, heads), :] = got[
                :, j * LANES : (j + 1) * LANES
            ]

    @pl.when(step == steps - 1)
    def _():
        copy.wait()
        head_rows = lambda h: jnp.concatenate(
            [lat[j, pl.ds(h, here, stride=heads), :] for j in range(lat.shape[0])], axis=1
        ).astype(bf16)
        for h in range(0, heads, 2):
            rows = jnp.concatenate([head_rows(h), head_rows(h + 1)], axis=0)
            both = jnp.concatenate([vu[h], vu[h + 1]], axis=1)
            got = jnp.dot(rows, both, preferred_element_type=f32).astype(bf16)
            for out in outs:
                out[:, h * vdim : (h + 1) * vdim] = got[:here, :vdim]
                out[:, (h + 1) * vdim : (h + 2) * vdim] = got[here:, vdim:]


def in_hbm(array):
    return pltpu.with_memory_space_constraint(array, pltpu.HBM)


def fetch_kernel(count, *refs):
    sems = refs[-1]
    ins, outs = refs[:count], refs[count : 2 * count]
    copies = [pltpu.make_async_copy(a, b, sems.at[i]) for i, (a, b) in enumerate(zip(ins, outs))]
    for copy in copies:
        copy.start()
    for copy in copies:
        copy.wait()


def fetch(*arrays):
    count = len(arrays)
    return pl.pallas_call(
        functools.partial(fetch_kernel, count),
        out_shape=tuple(jax.ShapeDtypeStruct(a.shape, a.dtype) for a in arrays),
        in_specs=[pl.BlockSpec(memory_space=pl.ANY)] * count,
        out_specs=(pl.BlockSpec(memory_space=pltpu.VMEM),) * count,
        scratch_shapes=[pltpu.SemaphoreType.DMA((count,))],
        compiler_params=pltpu.CompilerParams(vmem_limit_bytes=12 * 2**20),
        cost_estimate=pl.CostEstimate(
            flops=0, bytes_accessed=sum(2 * a.size * a.dtype.itemsize for a in arrays), transcendentals=0
        ),
        name="fetch",
    )(*map(in_hbm, arrays))


def project_kernel(sub, *refs):
    *parcels, out_proj, keep, send, landed = refs
    half, block = keep.shape
    here = parcels[0].shape[0]
    inner = out_proj.shape[1]
    core, ep = lax.axis_index("c"), lax.axis_index("ep")
    tp = lax.axis_index("y") * lax.axis_size("c") + core
    for k, parcel in enumerate(parcels):
        landed[pl.ds(pl.multiple_of((ep ^ k) * here, here), here), :] = parcel[...]
    rest = landed.shape[1] - inner
    at_row = lax.broadcasted_iota(jnp.int32, (rest, block), 0)
    at_col = lax.broadcasted_iota(jnp.int32, (rest, block), 1)
    spot = jnp.where((at_row + tp * sub == at_col) & (at_row < sub), 1.0, 0.0).astype(bf16)
    part = lax.dot_general(
        landed[:, :inner], out_proj[...], (((1,), (1,)), ((), ())), preferred_element_type=f32
    ) + jnp.dot(landed[:, inner:], spot, preferred_element_type=f32)
    keep[...] = jnp.where(core == 0, part[:half], part[half:])
    send[...] = jnp.where(core == 0, part[half:], part[:half])


def project(parcels, out_proj, sub):
    here, inner = parcels[0].shape
    tokens = here * len(parcels)
    vmem = pl.BlockSpec(memory_space=pltpu.VMEM)
    shape = jax.ShapeDtypeStruct((tokens // 2, out_proj.shape[0]), f32)
    return pl.pallas_call(
        functools.partial(project_kernel, sub),
        out_shape=(shape, shape),
        in_specs=[vmem] * (len(parcels) + 1),
        out_specs=(vmem, vmem),
        scratch_shapes=[pltpu.VMEM((tokens, inner), bf16)],
        compiler_params=pltpu.CompilerParams(vmem_limit_bytes=8 * 2**20),
        name="project",
    )(*parcels, out_proj)


def bundle_kernel(own, got, gain, router_t, codes, out):
    hidden = own[...].astype(f32) + got[...].astype(f32)
    rows, block = hidden.shape
    experts = router_t.shape[0]
    scaled = (hidden * gain[...]).astype(bf16)
    square = jnp.sum(hidden * hidden, axis=1, keepdims=True)
    logits = lax.dot_general(
        scaled, router_t[...], (((1,), (1,)), ((), ())), preferred_element_type=f32
    )
    spare = out.shape[1] - block
    both = high_low(square) + high_low(logits) + [codes[...]]
    extras = jnp.concatenate(
        [b.astype(f32) for b in both] + [jnp.zeros((rows, spare - 2 - 3 * experts), f32)], axis=1
    ).astype(bf16)
    odd = lax.rem(lax.axis_index("ep"), 2) == 1

    @pl.when(jnp.logical_not(odd))
    def _():
        out[...] = jnp.concatenate([scaled, extras], axis=1)

    @pl.when(odd)
    def _():
        out[...] = jnp.concatenate([extras, scaled], axis=1)


def bundle(own, got, gain, router_t, codes, wide):
    rows = own.shape[0]
    vmem = pl.BlockSpec(memory_space=pltpu.VMEM)
    return pl.pallas_call(
        bundle_kernel,
        out_shape=jax.ShapeDtypeStruct((rows, wide), bf16),
        in_specs=[vmem] * 5,
        out_specs=vmem,
        compiler_params=pltpu.CompilerParams(vmem_limit_bytes=4 * 2**20),
        name="bundle",
    )(own, got, gain, router_t, codes)


def attend(
    query_latent, query_rope, cache_latent, cache_rope, lengths, value_up, residual, dests, sub, block, apart
):
    here, heads, latent = query_latent.shape
    rope, places = cache_rope.shape[1:]
    vdim = value_up.shape[2]
    steps = 4
    per = here // steps
    spec = lambda *dims: pl.BlockSpec((per,) + dims, lambda t: (t,) + (0,) * len(dims))
    whole = lambda shape: pl.BlockSpec(shape, lambda t: (0,) * len(shape))
    parcel = (here, heads * vdim + LANES)
    shapes = [parcel] * dests if apart else [(dests,) + parcel]
    return pl.pallas_call(
        functools.partial(attend_kernel, steps, dests, sub, block),
        grid=(steps,),
        out_shape=[jax.ShapeDtypeStruct(shape, bf16) for shape in shapes],
        in_specs=[
            pl.BlockSpec(memory_space=pltpu.SMEM),
            spec(heads, latent),
            spec(heads, rope),
            spec(places, latent),
            spec(rope, places),
            whole(residual.shape),
            pl.BlockSpec(memory_space=pl.ANY),
        ],
        out_specs=[whole(shape) for shape in shapes],
        scratch_shapes=[
            pltpu.VMEM((latent // LANES, here * heads, LANES), f32),
            pltpu.VMEM(value_up.shape, bf16),
            pltpu.VMEM(residual.shape, f32),
            pltpu.SemaphoreType.DMA,
        ],
        compiler_params=pltpu.CompilerParams(
            dimension_semantics=("arbitrary",), vmem_limit_bytes=24 * 2**20
        ),
        name="attend",
    )(*map(in_hbm, (lengths, query_latent, query_rope, cache_latent, cache_rope, residual, value_up)))


def expert_kernel(dims, *refs):
    n_ep, n_y, block, experts, part = dims
    mine, other, rest = refs[:n_ep], refs[n_ep : 2 * n_ep], refs[2 * n_ep :]
    gate, up, down, keep_out, send_out, own_out, x, sums = rest
    core, ep = lax.axis_index("c"), lax.axis_index("ep")
    tp = lax.axis_index("y") * lax.axis_size("c") + core
    half, wide = mine[0].shape
    here = 2 * half // n_ep
    spare = wide - block

    lane = lax.broadcasted_iota(jnp.int32, (half, LANES), 1)
    even = lax.rem(ep, 2) == 0
    for i, blocks in enumerate((mine, other)):
        rows = pl.ds(pl.multiple_of((core ^ i) * half, half), half)
        total = jnp.zeros((half, LANES), f32)
        for k in range(0, n_ep, 2):
            low = jnp.where(even, blocks[k][...], blocks[k + 1][...])
            high = jnp.where(even, blocks[k + 1][...], blocks[k][...])
            shared = jnp.where(lane < spare, low[:, -LANES:], high[:, :LANES])
            pair = jnp.concatenate([low[:, :-LANES], shared, high[:, LANES:]], axis=1)
            at = pl.multiple_of(((ep ^ k) // 2) * (2 * block), LANES)
            x[rows, pl.ds(at, 2 * block)] = pair
            total += jnp.where(
                lane < spare, high[:, :LANES].astype(f32), low[:, -LANES:].astype(f32)
            )
        sums[rows, :] = total[:, :spare] + total[:, spare:]
    own_out[...] = x[
        pl.ds(pl.multiple_of(ep * here, here), here), pl.ds(pl.multiple_of(tp * part, LANES), part)
    ]
    total = sums[...]
    square, logits, code = spare_lanes(total, total, experts)

    gate_val = jnp.dot(x[...], gate[...], preferred_element_type=f32)
    up_val = jnp.dot(x[...], up[...], preferred_element_type=f32)
    scale = lax.rsqrt(square / (n_ep * block) + norm_eps)
    weight = row_weight(logits * scale, code, ep)
    act = (jax.nn.silu(gate_val * scale) * (up_val * (scale * weight))).astype(bf16)
    for flip, out in ((1, send_out), (0, keep_out)):
        for y in range(n_y):
            cols = pl.ds(pl.multiple_of((y * 2 + (core ^ flip)) * part, LANES), part)
            out[y] = jnp.dot(act, down[:, cols], preferred_element_type=f32).astype(bf16)


def spare_lanes(total, own, experts):
    square = total[:, 0:1] + total[:, 1:2]
    logits = total[:, 2 : 2 + experts] + total[:, 2 + experts : 2 + 2 * experts]
    return square, logits, own[:, 2 + 2 * experts : 2 + 3 * experts]


def row_weight(logits, code, ep):
    affinity = jnp.where(code > 0.5, jax.nn.sigmoid(logits), 0.0)
    gates = route_scale * affinity / jnp.sum(affinity, axis=1, keepdims=True)
    mine_only = lax.broadcasted_iota(jnp.int32, gates.shape, 1) == ep
    return jnp.sum(jnp.where(mine_only & (code > 1.5), gates, 0.0), axis=1, keepdims=True)


def expert_block(mine, other, gate, up, down, n_y, block, experts):
    n_ep = len(mine)
    half, wide = mine[0].shape
    part = down.shape[1] // (2 * n_y)
    dims = (n_ep, n_y, block, experts, part)
    vmem = pl.BlockSpec(memory_space=pltpu.VMEM)
    shape = jax.ShapeDtypeStruct((n_y, 2 * half, part), bf16)
    own = jax.ShapeDtypeStruct((2 * half // n_ep, part), bf16)
    return pl.pallas_call(
        functools.partial(expert_kernel, dims),
        out_shape=(shape, shape, own),
        in_specs=[vmem] * (2 * n_ep + 3),
        out_specs=(vmem, vmem, vmem),
        scratch_shapes=[
            pltpu.VMEM((2 * half, n_ep * block), bf16),
            pltpu.VMEM((2 * half, wide - block), f32),
        ],
        compiler_params=pltpu.CompilerParams(vmem_limit_bytes=16 * 2**20),
        name="experts",
    )(*mine, *other, gate, up, down)


def expert_plain(ep, c, mine, other, gate, up, down, block, experts):
    n_y, n_ep, quarter, _ = mine.shape
    tokens = 2 * n_y * quarter
    here = tokens // n_ep
    part = down.shape[1] // (2 * n_y)
    both = jnp.stack([jnp.where(c == 0, mine, other), jnp.where(c == 0, other, mine)], axis=1)
    own = both[0, 0, :, :here, block:].reshape(tokens, -1).astype(f32)
    total = jnp.sum(both[..., block:].astype(f32), axis=2).reshape(tokens, -1)
    square, logits, code = spare_lanes(total, own, experts)
    x = both[..., :block].transpose(0, 1, 3, 2, 4).reshape(tokens, -1)
    scale = lax.rsqrt(square / x.shape[1] + norm_eps)
    weight = row_weight(logits * scale, code, ep)
    gate_val = jnp.dot(x, gate, preferred_element_type=f32) * scale
    up_val = jnp.dot(x, up, preferred_element_type=f32) * scale
    act = (jax.nn.silu(gate_val) * up_val * weight).astype(bf16)
    partial = jnp.dot(act, down, preferred_element_type=f32).astype(bf16)
    split = partial.reshape(tokens, n_y, 2, part).transpose(2, 1, 0, 3)
    return (
        lax.dynamic_index_in_dim(split, c, 0, keepdims=False),
        lax.dynamic_index_in_dim(split, 1 - c, 0, keepdims=False),
    )


def exchange(block, axis, size, mine):
    pieces = []
    for k in range(1, size):
        sent = lax.dynamic_index_in_dim(block, mine ^ k, 0, keepdims=False)
        pieces.append(lax.ppermute(sent, axis, [(i, i ^ k) for i in range(size)]))
    return lax.dynamic_index_in_dim(block, mine, 0, keepdims=False), pieces


def high_low(value):
    high = lax.reduce_precision(value, 8, 7)
    return [high, value - high]


def swap_cores(block):
    return lax.ppermute(block, "c", [(0, 1), (1, 0)])


def per_device(
    query_latent,
    query_rope,
    cache_latent,
    cache_rope,
    cache_lengths,
    value_up,
    out_proj,
    residual,
    norm_gain,
    router,
    trainer_gate,
    trainer_up,
    trainer_down,
    hot_experts,
    replica_index,
    token_experts,
    replica_pick,
):
    n_ep, n_y, n_c = lax.axis_size("ep"), lax.axis_size("y"), lax.axis_size("c")
    n_tp = n_y * n_c
    ep, y, c = lax.axis_index("ep"), lax.axis_index("y"), lax.axis_index("c")
    tp = y * n_c + c
    here, width = residual.shape
    tokens = here * n_ep
    quarter = tokens // n_tp
    experts = router.shape[1]
    block = out_proj.shape[0]
    sub = block // n_tp
    part = width // n_tp

    wide = -(-(block + 2 + 3 * experts) // LANES) * LANES
    apart = block % LANES == LANES // 2 == wide - block and block % 16 == 0
    apart = apart and n_ep & (n_ep - 1) == 0 and n_ep // n_tp % 2 == 0 and tokens <= 256
    parcels = attend(
        query_latent, query_rope, cache_latent, cache_rope, cache_lengths, value_up,
        residual, n_ep, sub, block, apart,
    )
    codes = keep_codes(token_experts, replica_pick, hot_experts, replica_index, experts)
    gain_part = lax.dynamic_slice_in_dim(norm_gain, ep * block, block, 0)[None, :]
    router_part = lax.dynamic_slice_in_dim(router.T, ep * block, block, 1)
    gain_own = lax.dynamic_slice_in_dim(norm_gain, tp * part, part, 0)
    weights = (trainer_gate[0], trainer_up[0], trainer_down[0])

    if apart:
        keep, send, x_own = near(
            parcels, out_proj, codes, gain_part, router_part, weights, sub, wide
        )
    else:
        keep, send, x_own = wide_slice(
            parcels[0], out_proj, codes, gain_part, router_part, weights, sub, wide
        )

    got = swap_cores(send)
    summed = (keep.astype(f32) + got.astype(f32)).astype(bf16)
    outbound = summed.reshape(n_y * n_ep, here, part)
    returned = lax.all_to_all(outbound, ("y", "ep"), split_axis=0, concat_axis=0, tiled=True)
    moe = jnp.sum(returned.astype(f32), axis=0)
    hidden_own = x_own.astype(f32) / gain_own[None, :]
    return (hidden_own + moe).astype(bf16)


def pass_on(block, axis, size):
    return [block] + [
        lax.ppermute(block, axis, [(i, i ^ k) for i in range(size)]) for k in range(1, size)
    ]


def near(parcels, out_proj, codes, gain_part, router_part, weights, sub, wide):
    n_ep, n_y = lax.axis_size("ep"), lax.axis_size("y")
    ep, c = lax.axis_index("ep"), lax.axis_index("c")
    block = out_proj.shape[0]
    here, experts = codes.shape
    half = here * n_ep // 2
    landed = [parcels[0]] + [
        lax.ppermute(parcels[k], "ep", [(i, i ^ k) for i in range(n_ep)]) for k in range(1, n_ep)
    ]
    keep, send = project(landed, out_proj, sub)
    summed = (keep + swap_cores(send)).astype(bf16)
    others = pass_on(summed, "y", n_y)[1:]
    total = others[0]
    for extra in others[1:]:
        total = total + extra
    rows = lax.iota(jnp.int32, half)
    placed = jnp.where((rows // here + c * (half // here) == ep)[:, None], jnp.tile(codes, (half // here, 1)), 0.0)
    sent = bundle(summed, total, gain_part, router_part, placed.astype(bf16), wide)
    mine = pass_on(sent, "ep", n_ep)
    sent, weights = lax.optimization_barrier((sent, weights))
    weights = fetch(*weights)
    other = [swap_cores(block_k) for block_k in mine]
    return expert_block(mine, other, *weights, n_y, block, experts)


def wide_slice(parcel, out_proj, codes, gain_part, router_part, weights, sub, wide):
    n_ep, n_y, n_c = lax.axis_size("ep"), lax.axis_size("y"), lax.axis_size("c")
    n_tp = n_y * n_c
    ep, y, c = lax.axis_index("ep"), lax.axis_index("y"), lax.axis_index("c")
    tp = y * n_c + c
    block, inner = out_proj.shape
    here, experts = codes.shape
    tokens = here * n_ep
    quarter = tokens // n_tp
    landed = lax.all_to_all(parcel, "ep", split_axis=0, concat_axis=0, tiled=True)
    landed = landed.reshape(tokens, -1)
    at_row = lax.broadcasted_iota(jnp.int32, (LANES, block), 0)
    at_col = lax.broadcasted_iota(jnp.int32, (LANES, block), 1)
    spot = ((at_row + tp * sub == at_col) & (at_row < sub)).astype(bf16)
    column_part = lax.dot_general(
        landed[:, :inner], out_proj, (((1,), (1,)), ((), ())), preferred_element_type=f32
    ) + jnp.dot(landed[:, inner:], spot, preferred_element_type=f32)
    halves = column_part.reshape(n_y, n_c, quarter, block).transpose(1, 0, 2, 3)
    own, others = exchange(halves, "c", n_c, c)
    own, others = exchange(own + sum(others), "y", n_y, y)
    hidden_part = own + sum(others)
    codes = jnp.pad(codes.astype(bf16), ((0, quarter - here), (0, 0)))
    scaled = (hidden_part * gain_part).astype(bf16)
    square = jnp.sum(hidden_part * hidden_part, axis=1, keepdims=True)
    logits = jnp.dot(scaled, router_part.T, preferred_element_type=f32)
    both = high_low(square) + high_low(logits)
    sent = jnp.concatenate([scaled] + [b.astype(bf16) for b in both] + [codes], axis=1)
    sent = jnp.pad(sent, ((0, 0), (0, wide - sent.shape[1])))
    sent = jnp.broadcast_to(sent[None], (n_y * n_ep, quarter, wide))
    mine = lax.all_to_all(
        sent, ("y", "ep"), split_axis=0, concat_axis=0, tiled=True
    ).reshape(n_y, n_ep, quarter, wide)
    other = swap_cores(mine)
    keep, send = expert_plain(ep, c, mine, other, *weights, block, experts)

    part = keep.shape[2]
    per_part = n_ep // n_tp
    first = ep * here
    of_tp, row = first // quarter, first % quarter
    cut = lambda a: lax.dynamic_slice(
        a, (of_tp // n_c, tp * per_part, row, 0), (1, per_part, here, wide)
    )[0]
    rows = jnp.where(of_tp % n_c == c, cut(mine), cut(other))
    return keep, send, rows[:, :, :block].transpose(1, 0, 2).reshape(here, part)


def solution(mesh):
    n_ep, n_tp = mesh.shape["ep"], mesh.shape["tp"]
    fine = Mesh(mesh.devices.reshape(n_ep, n_tp // CORES, CORES), ("ep", "y", "c"))
    tp = ("y", "c")
    placed = (
        P("ep", tp, None),
        P("ep", tp, None),
        P("ep", None, None),
        P("ep", None, None),
        P("ep"),
        P(tp, None, None),
        P("ep", tp),
        P("ep", None),
        P(),
        P(),
        P("ep", None, tp),
        P("ep", None, tp),
        P("ep", tp, None),
        P(),
        P(),
        P("ep", None),
        P("ep", None),
    )
    return jax.shard_map(
        per_device, mesh=fine, in_specs=placed, out_specs=P("ep", tp), check_vma=False
    )
```

```python
import functools

import jax
import jax.numpy as jnp
from jax import lax
from jax.experimental import pallas as pl
from jax.experimental.pallas import tpu as pltpu
from jax.sharding import Mesh, PartitionSpec as P

TOPK = 8
SLOT_DEV = 2
CAP = 2
HOT = 2
CORES = 2
LANES = 128

score_scale = 192.0 ** (-0.5)
route_scale = 2.5
norm_eps = 1e-06

bf16 = jnp.bfloat16
f32 = jnp.float32


def keep_codes(token_experts, replica_pick, hot_experts, replica_index, experts):
    ids = lax.iota(jnp.int32, experts)
    held = jnp.where(
        replica_index[:, None] == lax.iota(jnp.int32, HOT)[None, :], hot_experts[None, :], 0
    ).sum(axis=1)
    count = 1 + jnp.sum((held[:, None] == ids[None, :]).astype(jnp.int32), axis=0)
    match = token_experts[:, :, None] == ids[None, None, :]
    named = jnp.any(match, axis=1)
    place = jnp.sum(jnp.where(match, replica_pick[:, :, None], 0), axis=1) % count[None, :]
    place = jnp.where(named, place, -1)
    tokens = lax.iota(jnp.int32, place.shape[0])
    ahead = (tokens[None, :] < tokens[:, None])[:, :, None] & (
        place[None, :, :] == place[:, None, :]
    )
    prior = jnp.sum(ahead.astype(jnp.int32), axis=1)
    return jnp.where(named, jnp.where(prior < CAP, 2.0, 1.0), 0.0)


def attend_kernel(steps, dests, sub, block, lengths, ql, qr, cl, cr, residual, vu_hbm, *refs):
    *outs, lat, vu, wide_res, sem = refs
    apart = len(outs) > 1
    ep = lax.axis_index("ep")
    outs = outs if apart else [outs[0].at[j] for j in range(dests)]
    step = pl.program_id(0)
    per, heads = ql.shape[:2]
    here = per * steps
    tp = lax.axis_index("y") * lax.axis_size("c") + lax.axis_index("c")
    copy = pltpu.make_async_copy(vu_hbm, vu, sem)
    vdim = vu.shape[2]
    values = heads * vdim

    @pl.when(step == 0)
    def _():
        copy.start()
        width = residual.shape[1]
        wide_res[...] = residual[...].astype(f32)
        span = 2 * LANES
        lane = lax.broadcasted_iota(jnp.int32, (here, LANES), 1)
        spots = [(out, j, values) for j, out in enumerate(outs)]
        if apart:
            spots = [
                (out, ep ^ (2 * j + i), values + i * LANES) for j, out in enumerate(outs) for i in (0, 1)
            ]
        for out, dest, at in spots:
            base = dest * block + tp * sub
            start = jnp.minimum(base // LANES * LANES, width - span)
            piece = wide_res[:, pl.ds(pl.multiple_of(start, LANES), span)]
            piece = pltpu.roll(piece, span - (base - start), axis=1)[:, :LANES]
            out[:, at : at + LANES] = jnp.where(lane < sub, piece, 0.0).astype(bf16)

    scores = [
        lax.dot_general(ql[i], cl[i], (((1,), (1,)), ((), ())), preferred_element_type=f32)
        for i in range(per)
    ]
    scores = [
        (s + jnp.dot(qr[i], cr[i], preferred_element_type=f32)) * score_scale
        for i, s in enumerate(scores)
    ]
    places = lax.broadcasted_iota(jnp.int32, scores[0].shape, 1)
    scores = [
        jnp.where(places < lengths[step * per + i], s, -1e30) for i, s in enumerate(scores)
    ]
    peaks = [jnp.max(s, axis=1, keepdims=True) for s in scores]
    shifted = [jnp.exp(s - m) for s, m in zip(scores, peaks)]
    inverse = [1.0 / jnp.sum(p, axis=1, keepdims=True) for p in shifted]
    mixed = [
        jnp.dot(p.astype(bf16), cl[i], preferred_element_type=f32)
        for i, p in enumerate(shifted)
    ]
    for i in range(per):
        got = mixed[i] * inverse[i]
        for j in range(lat.shape[0]):
            lat[j, pl.ds((step * per + i) * heads, heads), :] = got[
                :, j * LANES : (j + 1) * LANES
            ]

    @pl.when(step == steps - 1)
    def _():
        copy.wait()
        head_rows = lambda h: jnp.concatenate(
            [lat[j, pl.ds(h, here, stride=heads), :] for j in range(lat.shape[0])], axis=1
        ).astype(bf16)
        for h in range(0, heads, 2):
            rows = jnp.concatenate([head_rows(h), head_rows(h + 1)], axis=0)
            both = jnp.concatenate([vu[h], vu[h + 1]], axis=1)
            got = jnp.dot(rows, both, preferred_element_type=f32).astype(bf16)
            for out in outs:
                out[:, h * vdim : (h + 1) * vdim] = got[:here, :vdim]
                out[:, (h + 1) * vdim : (h + 2) * vdim] = got[here:, vdim:]


def in_hbm(array):
    return pltpu.with_memory_space_constraint(array, pltpu.HBM)


def fetch_kernel(count, *refs):
    sems = refs[-1]
    ins, outs = refs[:count], refs[count : 2 * count]
    copies = [pltpu.make_async_copy(a, b, sems.at[i]) for i, (a, b) in enumerate(zip(ins, outs))]
    for copy in copies:
        copy.start()
    for copy in copies:
        copy.wait()


def fetch(*arrays):
    count = len(arrays)
    return pl.pallas_call(
        functools.partial(fetch_kernel, count),
        out_shape=tuple(jax.ShapeDtypeStruct(a.shape, a.dtype) for a in arrays),
        in_specs=[pl.BlockSpec(memory_space=pl.ANY)] * count,
        out_specs=(pl.BlockSpec(memory_space=pltpu.VMEM),) * count,
        scratch_shapes=[pltpu.SemaphoreType.DMA((count,))],
        compiler_params=pltpu.CompilerParams(vmem_limit_bytes=12 * 2**20),
        cost_estimate=pl.CostEstimate(
            flops=0, bytes_accessed=sum(2 * a.size * a.dtype.itemsize for a in arrays), transcendentals=0
        ),
        name="fetch",
    )(*map(in_hbm, arrays))


def project_kernel(sub, *refs):
    *parcels, out_proj, keep, send, landed = refs
    half, block = keep.shape
    here = parcels[0].shape[0]
    inner = out_proj.shape[1]
    core, ep = lax.axis_index("c"), lax.axis_index("ep")
    tp = lax.axis_index("y") * lax.axis_size("c") + core
    for k, parcel in enumerate(parcels):
        rows = pl.ds(pl.multiple_of((ep ^ k) * here, here), here)
        share = inner + k % 2 * LANES
        landed[rows, :inner] = parcel[:, :inner]
        landed[rows, inner:] = parcel[:, share : share + LANES]
    rest = landed.shape[1] - inner
    at_row = lax.broadcasted_iota(jnp.int32, (rest, block), 0)
    at_col = lax.broadcasted_iota(jnp.int32, (rest, block), 1)
    spot = jnp.where((at_row + tp * sub == at_col) & (at_row < sub), 1.0, 0.0).astype(bf16)
    part = lax.dot_general(
        landed[:, :inner], out_proj[...], (((1,), (1,)), ((), ())), preferred_element_type=f32
    ) + jnp.dot(landed[:, inner:], spot, preferred_element_type=f32)
    keep[...] = jnp.where(core == 0, part[:half], part[half:])
    send[...] = jnp.where(core == 0, part[half:], part[:half])


def project(parcels, out_proj, sub):
    here = parcels[0].shape[0]
    inner = out_proj.shape[1] + LANES
    tokens = here * len(parcels)
    vmem = pl.BlockSpec(memory_space=pltpu.VMEM)
    shape = jax.ShapeDtypeStruct((tokens // 2, out_proj.shape[0]), f32)
    return pl.pallas_call(
        functools.partial(project_kernel, sub),
        out_shape=(shape, shape),
        in_specs=[vmem] * (len(parcels) + 1),
        out_specs=(vmem, vmem),
        scratch_shapes=[pltpu.VMEM((tokens, inner), bf16)],
        compiler_params=pltpu.CompilerParams(vmem_limit_bytes=8 * 2**20),
        name="project",
    )(*parcels, out_proj)


def bundle_kernel(own, got, gain, router_t, codes, out):
    hidden = own[...].astype(f32) + got[...].astype(f32)
    rows, block = hidden.shape
    experts = router_t.shape[0]
    scaled = (hidden * gain[...]).astype(bf16)
    square = jnp.sum(hidden * hidden, axis=1, keepdims=True)
    logits = lax.dot_general(
        scaled, router_t[...], (((1,), (1,)), ((), ())), preferred_element_type=f32
    )
    spare = out.shape[1] - block
    both = high_low(square) + high_low(logits) + [codes[...]]
    extras = jnp.concatenate(
        [b.astype(f32) for b in both] + [jnp.zeros((rows, spare - 2 - 3 * experts), f32)], axis=1
    ).astype(bf16)
    odd = lax.rem(lax.axis_index("ep"), 2) == 1

    @pl.when(jnp.logical_not(odd))
    def _():
        out[...] = jnp.concatenate([scaled, extras], axis=1)

    @pl.when(odd)
    def _():
        out[...] = jnp.concatenate([extras, scaled], axis=1)


def bundle(own, got, gain, router_t, codes, wide):
    rows = own.shape[0]
    vmem = pl.BlockSpec(memory_space=pltpu.VMEM)
    return pl.pallas_call(
        bundle_kernel,
        out_shape=jax.ShapeDtypeStruct((rows, wide), bf16),
        in_specs=[vmem] * 5,
        out_specs=vmem,
        compiler_params=pltpu.CompilerParams(vmem_limit_bytes=4 * 2**20),
        name="bundle",
    )(own, got, gain, router_t, codes)


def attend(
    query_latent, query_rope, cache_latent, cache_rope, lengths, value_up, residual, dests, sub, block, apart
):
    here, heads, latent = query_latent.shape
    rope, places = cache_rope.shape[1:]
    vdim = value_up.shape[2]
    steps = 4
    per = here // steps
    spec = lambda *dims: pl.BlockSpec((per,) + dims, lambda t: (t,) + (0,) * len(dims))
    whole = lambda shape: pl.BlockSpec(shape, lambda t: (0,) * len(shape))
    values = heads * vdim
    shapes = [(dests, here, values + LANES)]
    if apart:
        shapes = [(here, values + 2 * LANES)] * (dests // 2)
    return pl.pallas_call(
        functools.partial(attend_kernel, steps, dests, sub, block),
        grid=(steps,),
        out_shape=[jax.ShapeDtypeStruct(shape, bf16) for shape in shapes],
        in_specs=[
            pl.BlockSpec(memory_space=pltpu.SMEM),
            spec(heads, latent),
            spec(heads, rope),
            spec(places, latent),
            spec(rope, places),
            whole(residual.shape),
            pl.BlockSpec(memory_space=pl.ANY),
        ],
        out_specs=[whole(shape) for shape in shapes],
        scratch_shapes=[
            pltpu.VMEM((latent // LANES, here * heads, LANES), f32),
            pltpu.VMEM(value_up.shape, bf16),
            pltpu.VMEM(residual.shape, f32),
            pltpu.SemaphoreType.DMA,
        ],
        compiler_params=pltpu.CompilerParams(
            dimension_semantics=("arbitrary",), vmem_limit_bytes=24 * 2**20
        ),
        name="attend",
    )(*map(in_hbm, (lengths, query_latent, query_rope, cache_latent, cache_rope, residual, value_up)))


def expert_kernel(dims, *refs):
    n_ep, n_y, block, experts, part = dims
    mine, other, rest = refs[:n_ep], refs[n_ep : 2 * n_ep], refs[2 * n_ep :]
    gate, up, down, keep_out, send_out, own_out, x, sums = rest
    core, ep = lax.axis_index("c"), lax.axis_index("ep")
    tp = lax.axis_index("y") * lax.axis_size("c") + core
    half, wide = mine[0].shape
    here = 2 * half // n_ep
    spare = wide - block

    lane = lax.broadcasted_iota(jnp.int32, (half, LANES), 1)
    even = lax.rem(ep, 2) == 0
    for i, blocks in enumerate((mine, other)):
        rows = pl.ds(pl.multiple_of((core ^ i) * half, half), half)
        total = jnp.zeros((half, LANES), f32)
        for k in range(0, n_ep, 2):
            low = jnp.where(even, blocks[k][...], blocks[k + 1][...])
            high = jnp.where(even, blocks[k + 1][...], blocks[k][...])
            shared = jnp.where(lane < spare, low[:, -LANES:], high[:, :LANES])
            pair = jnp.concatenate([low[:, :-LANES], shared, high[:, LANES:]], axis=1)
            at = pl.multiple_of(((ep ^ k) // 2) * (2 * block), LANES)
            x[rows, pl.ds(at, 2 * block)] = pair
            total += jnp.where(
                lane < spare, high[:, :LANES].astype(f32), low[:, -LANES:].astype(f32)
            )
        sums[rows, :] = total[:, :spare] + total[:, spare:]
    own_out[...] = x[
        pl.ds(pl.multiple_of(ep * here, here), here), pl.ds(pl.multiple_of(tp * part, LANES), part)
    ]
    total = sums[...]
    square, logits, code = spare_lanes(total, total, experts)

    gate_val = jnp.dot(x[...], gate[...], preferred_element_type=f32)
    up_val = jnp.dot(x[...], up[...], preferred_element_type=f32)
    scale = lax.rsqrt(square / (n_ep * block) + norm_eps)
    weight = row_weight(logits * scale, code, ep)
    act = (jax.nn.silu(gate_val * scale) * (up_val * (scale * weight))).astype(bf16)
    for flip, out in ((1, send_out), (0, keep_out)):
        for y in range(n_y):
            cols = pl.ds(pl.multiple_of((y * 2 + (core ^ flip)) * part, LANES), part)
            out[y] = jnp.dot(act, down[:, cols], preferred_element_type=f32).astype(bf16)


def spare_lanes(total, own, experts):
    square = total[:, 0:1] + total[:, 1:2]
    logits = total[:, 2 : 2 + experts] + total[:, 2 + experts : 2 + 2 * experts]
    return square, logits, own[:, 2 + 2 * experts : 2 + 3 * experts]


def row_weight(logits, code, ep):
    affinity = jnp.where(code > 0.5, jax.nn.sigmoid(logits), 0.0)
    gates = route_scale * affinity / jnp.sum(affinity, axis=1, keepdims=True)
    mine_only = lax.broadcasted_iota(jnp.int32, gates.shape, 1) == ep
    return jnp.sum(jnp.where(mine_only & (code > 1.5), gates, 0.0), axis=1, keepdims=True)


def expert_block(mine, other, gate, up, down, n_y, block, experts):
    n_ep = len(mine)
    half, wide = mine[0].shape
    part = down.shape[1] // (2 * n_y)
    dims = (n_ep, n_y, block, experts, part)
    vmem = pl.BlockSpec(memory_space=pltpu.VMEM)
    shape = jax.ShapeDtypeStruct((n_y, 2 * half, part), bf16)
    own = jax.ShapeDtypeStruct((2 * half // n_ep, part), bf16)
    return pl.pallas_call(
        functools.partial(expert_kernel, dims),
        out_shape=(shape, shape, own),
        in_specs=[vmem] * (2 * n_ep + 3),
        out_specs=(vmem, vmem, vmem),
        scratch_shapes=[
            pltpu.VMEM((2 * half, n_ep * block), bf16),
            pltpu.VMEM((2 * half, wide - block), f32),
        ],
        compiler_params=pltpu.CompilerParams(vmem_limit_bytes=16 * 2**20),
        name="experts",
    )(*mine, *other, gate, up, down)


def expert_plain(ep, c, mine, other, gate, up, down, block, experts):
    n_y, n_ep, quarter, _ = mine.shape
    tokens = 2 * n_y * quarter
    here = tokens // n_ep
    part = down.shape[1] // (2 * n_y)
    both = jnp.stack([jnp.where(c == 0, mine, other), jnp.where(c == 0, other, mine)], axis=1)
    own = both[0, 0, :, :here, block:].reshape(tokens, -1).astype(f32)
    total = jnp.sum(both[..., block:].astype(f32), axis=2).reshape(tokens, -1)
    square, logits, code = spare_lanes(total, own, experts)
    x = both[..., :block].transpose(0, 1, 3, 2, 4).reshape(tokens, -1)
    scale = lax.rsqrt(square / x.shape[1] + norm_eps)
    weight = row_weight(logits * scale, code, ep)
    gate_val = jnp.dot(x, gate, preferred_element_type=f32) * scale
    up_val = jnp.dot(x, up, preferred_element_type=f32) * scale
    act = (jax.nn.silu(gate_val) * up_val * weight).astype(bf16)
    partial = jnp.dot(act, down, preferred_element_type=f32).astype(bf16)
    split = partial.reshape(tokens, n_y, 2, part).transpose(2, 1, 0, 3)
    return (
        lax.dynamic_index_in_dim(split, c, 0, keepdims=False),
        lax.dynamic_index_in_dim(split, 1 - c, 0, keepdims=False),
    )


def exchange(block, axis, size, mine):
    pieces = []
    for k in range(1, size):
        sent = lax.dynamic_index_in_dim(block, mine ^ k, 0, keepdims=False)
        pieces.append(lax.ppermute(sent, axis, [(i, i ^ k) for i in range(size)]))
    return lax.dynamic_index_in_dim(block, mine, 0, keepdims=False), pieces


def high_low(value):
    high = lax.reduce_precision(value, 8, 7)
    return [high, value - high]


def swap_cores(block):
    return lax.ppermute(block, "c", [(0, 1), (1, 0)])


def per_device(
    query_latent,
    query_rope,
    cache_latent,
    cache_rope,
    cache_lengths,
    value_up,
    out_proj,
    residual,
    norm_gain,
    router,
    trainer_gate,
    trainer_up,
    trainer_down,
    hot_experts,
    replica_index,
    token_experts,
    replica_pick,
):
    n_ep, n_y, n_c = lax.axis_size("ep"), lax.axis_size("y"), lax.axis_size("c")
    n_tp = n_y * n_c
    ep, y, c = lax.axis_index("ep"), lax.axis_index("y"), lax.axis_index("c")
    tp = y * n_c + c
    here, width = residual.shape
    tokens = here * n_ep
    quarter = tokens // n_tp
    experts = router.shape[1]
    block = out_proj.shape[0]
    sub = block // n_tp
    part = width // n_tp

    wide = -(-(block + 2 + 3 * experts) // LANES) * LANES
    apart = block % LANES == LANES // 2 == wide - block and block % 16 == 0
    apart = apart and n_ep & (n_ep - 1) == 0 and n_ep // n_tp % 2 == 0 and tokens <= 256
    parcels = attend(
        query_latent, query_rope, cache_latent, cache_rope, cache_lengths, value_up,
        residual, n_ep, sub, block, apart,
    )
    codes = keep_codes(token_experts, replica_pick, hot_experts, replica_index, experts)
    gain_part = lax.dynamic_slice_in_dim(norm_gain, ep * block, block, 0)[None, :]
    router_part = lax.dynamic_slice_in_dim(router.T, ep * block, block, 1)
    gain_own = lax.dynamic_slice_in_dim(norm_gain, tp * part, part, 0)
    weights = (trainer_gate[0], trainer_up[0], trainer_down[0])

    if apart:
        keep, send, x_own = near(
            parcels, out_proj, codes, gain_part, router_part, weights, sub, wide
        )
    else:
        keep, send, x_own = wide_slice(
            parcels[0], out_proj, codes, gain_part, router_part, weights, sub, wide
        )

    got = swap_cores(send)
    summed = (keep.astype(f32) + got.astype(f32)).astype(bf16)
    outbound = summed.reshape(n_y * n_ep, here, part)
    returned = lax.all_to_all(outbound, ("y", "ep"), split_axis=0, concat_axis=0, tiled=True)
    moe = jnp.sum(returned.astype(f32), axis=0)
    hidden_own = x_own.astype(f32) / gain_own[None, :]
    return (hidden_own + moe).astype(bf16)


def send_to(block, axis, size, flip):
    return lax.ppermute(block, axis, [(i, i ^ flip) for i in range(size)])


def gather(blocks, size):
    got = [blocks[0]] + [None] * (size - 1)
    far = list(range(2, size, 2))
    for k in far[1:] + far[:1]:
        got[k] = send_to(blocks[k // 2], "ep", size, k)
    for k in [0] + far[1:] + far[:1]:
        got[k + 1] = send_to(got[k], "ep", size, 1)
    return got


def near(parcels, out_proj, codes, gain_part, router_part, weights, sub, wide):
    n_ep, n_y = lax.axis_size("ep"), lax.axis_size("y")
    ep, c = lax.axis_index("ep"), lax.axis_index("c")
    block = out_proj.shape[0]
    here, experts = codes.shape
    half = here * n_ep // 2
    landed = gather(parcels, n_ep)
    landed[-1], gain_part, router_part = lax.optimization_barrier(
        (landed[-1], gain_part, router_part)
    )
    keep, send = project(landed, out_proj, sub)
    summed = (keep + swap_cores(send)).astype(bf16)
    summed, weights = lax.optimization_barrier((summed, weights))
    *weights, gain_part = fetch(*weights, gain_part)
    total = sum(send_to(summed, "y", n_y, k).astype(f32) for k in range(1, n_y))
    rows = lax.iota(jnp.int32, half)
    placed = jnp.where((rows // here + c * (half // here) == ep)[:, None], jnp.tile(codes, (half // here, 1)), 0.0)
    sent = bundle(summed, total, gain_part, router_part, placed.astype(bf16), wide)
    mine = gather([sent] * (n_ep // 2), n_ep)
    other = [swap_cores(block_k) for block_k in mine]
    return expert_block(mine, other, *weights, n_y, block, experts)


def wide_slice(parcel, out_proj, codes, gain_part, router_part, weights, sub, wide):
    n_ep, n_y, n_c = lax.axis_size("ep"), lax.axis_size("y"), lax.axis_size("c")
    n_tp = n_y * n_c
    ep, y, c = lax.axis_index("ep"), lax.axis_index("y"), lax.axis_index("c")
    tp = y * n_c + c
    block, inner = out_proj.shape
    here, experts = codes.shape
    tokens = here * n_ep
    quarter = tokens // n_tp
    landed = lax.all_to_all(parcel, "ep", split_axis=0, concat_axis=0, tiled=True)
    landed = landed.reshape(tokens, -1)
    at_row = lax.broadcasted_iota(jnp.int32, (LANES, block), 0)
    at_col = lax.broadcasted_iota(jnp.int32, (LANES, block), 1)
    spot = ((at_row + tp * sub == at_col) & (at_row < sub)).astype(bf16)
    column_part = lax.dot_general(
        landed[:, :inner], out_proj, (((1,), (1,)), ((), ())), preferred_element_type=f32
    ) + jnp.dot(landed[:, inner:], spot, preferred_element_type=f32)
    halves = column_part.reshape(n_y, n_c, quarter, block).transpose(1, 0, 2, 3)
    own, others = exchange(halves, "c", n_c, c)
    own, others = exchange(own + sum(others), "y", n_y, y)
    hidden_part = own + sum(others)
    codes = jnp.pad(codes.astype(bf16), ((0, quarter - here), (0, 0)))
    scaled = (hidden_part * gain_part).astype(bf16)
    square = jnp.sum(hidden_part * hidden_part, axis=1, keepdims=True)
    logits = jnp.dot(scaled, router_part.T, preferred_element_type=f32)
    both = high_low(square) + high_low(logits)
    sent = jnp.concatenate([scaled] + [b.astype(bf16) for b in both] + [codes], axis=1)
    sent = jnp.pad(sent, ((0, 0), (0, wide - sent.shape[1])))
    sent = jnp.broadcast_to(sent[None], (n_y * n_ep, quarter, wide))
    mine = lax.all_to_all(
        sent, ("y", "ep"), split_axis=0, concat_axis=0, tiled=True
    ).reshape(n_y, n_ep, quarter, wide)
    other = swap_cores(mine)
    keep, send = expert_plain(ep, c, mine, other, *weights, block, experts)

    part = keep.shape[2]
    per_part = n_ep // n_tp
    first = ep * here
    of_tp, row = first // quarter, first % quarter
    cut = lambda a: lax.dynamic_slice(
        a, (of_tp // n_c, tp * per_part, row, 0), (1, per_part, here, wide)
    )[0]
    rows = jnp.where(of_tp % n_c == c, cut(mine), cut(other))
    return keep, send, rows[:, :, :block].transpose(1, 0, 2).reshape(here, part)


def solution(mesh):
    n_ep, n_tp = mesh.shape["ep"], mesh.shape["tp"]
    fine = Mesh(mesh.devices.reshape(n_ep, n_tp // CORES, CORES), ("ep", "y", "c"))
    tp = ("y", "c")
    placed = (
        P("ep", tp, None),
        P("ep", tp, None),
        P("ep", None, None),
        P("ep", None, None),
        P("ep"),
        P(tp, None, None),
        P("ep", tp),
        P("ep", None),
        P(),
        P(),
        P("ep", None, tp),
        P("ep", None, tp),
        P("ep", tp, None),
        P(),
        P(),
        P("ep", None),
        P("ep", None),
    )
    return jax.shard_map(
        per_device, mesh=fine, in_specs=placed, out_specs=P("ep", tp), check_vma=False
    )
```

```python
import functools

import jax
import jax.numpy as jnp
from jax import lax
from jax.experimental import pallas as pl
from jax.experimental.pallas import tpu as pltpu
from jax.sharding import Mesh, PartitionSpec as P

TOPK = 8
SLOT_DEV = 2
CAP = 2
HOT = 2
CORES = 2
LANES = 128

score_scale = 192.0 ** (-0.5)
route_scale = 2.5
norm_eps = 1e-06

bf16 = jnp.bfloat16
f32 = jnp.float32


def keep_codes(token_experts, replica_pick, hot_experts, replica_index, experts):
    ids = lax.iota(jnp.int32, experts)
    held = jnp.where(
        replica_index[:, None] == lax.iota(jnp.int32, HOT)[None, :], hot_experts[None, :], 0
    ).sum(axis=1)
    count = 1 + jnp.sum((held[:, None] == ids[None, :]).astype(jnp.int32), axis=0)
    match = token_experts[:, :, None] == ids[None, None, :]
    named = jnp.any(match, axis=1)
    place = jnp.sum(jnp.where(match, replica_pick[:, :, None], 0), axis=1) % count[None, :]
    place = jnp.where(named, place, -1)
    tokens = lax.iota(jnp.int32, place.shape[0])
    ahead = (tokens[None, :] < tokens[:, None])[:, :, None] & (
        place[None, :, :] == place[:, None, :]
    )
    prior = jnp.sum(ahead.astype(jnp.int32), axis=1)
    return jnp.where(named, jnp.where(prior < CAP, 2.0, 1.0), 0.0)


def attend_kernel(steps, dests, sub, block, lengths, ql, qr, cl, cr, residual, vu_hbm, *refs):
    *outs, lat, vu, wide_res, sem = refs
    apart = len(outs) > 1
    ep = lax.axis_index("ep")
    outs = outs if apart else [outs[0].at[j] for j in range(dests)]
    step = pl.program_id(0)
    per, heads = ql.shape[:2]
    here = per * steps
    tp = lax.axis_index("y") * lax.axis_size("c") + lax.axis_index("c")
    copy = pltpu.make_async_copy(vu_hbm, vu, sem)
    vdim = vu.shape[2]
    values = heads * vdim

    @pl.when(step == 0)
    def _():
        copy.start()
        width = residual.shape[1]
        wide_res[...] = residual[...].astype(f32)
        span = 2 * LANES
        lane = lax.broadcasted_iota(jnp.int32, (here, LANES), 1)
        spots = [(out, j, values) for j, out in enumerate(outs)]
        if apart:
            spots = [
                (out, ep ^ (2 * j + i), values + i * LANES) for j, out in enumerate(outs) for i in (0, 1)
            ]
        for out, dest, at in spots:
            base = dest * block + tp * sub
            start = jnp.minimum(base // LANES * LANES, width - span)
            piece = wide_res[:, pl.ds(pl.multiple_of(start, LANES), span)]
            piece = pltpu.roll(piece, span - (base - start), axis=1)[:, :LANES]
            out[:, at : at + LANES] = jnp.where(lane < sub, piece, 0.0).astype(bf16)

    scores = [
        lax.dot_general(ql[i], cl[i], (((1,), (1,)), ((), ())), preferred_element_type=f32)
        for i in range(per)
    ]
    scores = [
        (s + jnp.dot(qr[i], cr[i], preferred_element_type=f32)) * score_scale
        for i, s in enumerate(scores)
    ]
    places = lax.broadcasted_iota(jnp.int32, scores[0].shape, 1)
    scores = [
        jnp.where(places < lengths[step * per + i], s, -1e30) for i, s in enumerate(scores)
    ]
    peaks = [jnp.max(s, axis=1, keepdims=True) for s in scores]
    shifted = [jnp.exp(s - m) for s, m in zip(scores, peaks)]
    inverse = [1.0 / jnp.sum(p, axis=1, keepdims=True) for p in shifted]
    mixed = [
        jnp.dot(p.astype(bf16), cl[i], preferred_element_type=f32)
        for i, p in enumerate(shifted)
    ]
    for i in range(per):
        got = mixed[i] * inverse[i]
        for j in range(lat.shape[0]):
            lat[j, pl.ds((step * per + i) * heads, heads), :] = got[
                :, j * LANES : (j + 1) * LANES
            ]

    @pl.when(step == steps - 1)
    def _():
        copy.wait()
        head_rows = lambda h: jnp.concatenate(
            [lat[j, pl.ds(h, here, stride=heads), :] for j in range(lat.shape[0])], axis=1
        ).astype(bf16)
        for h in range(0, heads, 2):
            rows = jnp.concatenate([head_rows(h), head_rows(h + 1)], axis=0)
            both = jnp.concatenate([vu[h], vu[h + 1]], axis=1)
            got = jnp.dot(rows, both, preferred_element_type=f32).astype(bf16)
            for out in outs:
                out[:, h * vdim : (h + 1) * vdim] = got[:here, :vdim]
                out[:, (h + 1) * vdim : (h + 2) * vdim] = got[here:, vdim:]


def in_hbm(array):
    return pltpu.with_memory_space_constraint(array, pltpu.HBM)


def fetch_kernel(count, *refs):
    sems = refs[-1]
    ins, outs = refs[:count], refs[count : 2 * count]
    copies = [pltpu.make_async_copy(a, b, sems.at[i]) for i, (a, b) in enumerate(zip(ins, outs))]
    for copy in copies:
        copy.start()
    for copy in copies:
        copy.wait()


def fetch(*arrays):
    count = len(arrays)
    return pl.pallas_call(
        functools.partial(fetch_kernel, count),
        out_shape=tuple(jax.ShapeDtypeStruct(a.shape, a.dtype) for a in arrays),
        in_specs=[pl.BlockSpec(memory_space=pl.ANY)] * count,
        out_specs=(pl.BlockSpec(memory_space=pltpu.VMEM),) * count,
        scratch_shapes=[pltpu.SemaphoreType.DMA((count,))],
        compiler_params=pltpu.CompilerParams(vmem_limit_bytes=12 * 2**20),
        cost_estimate=pl.CostEstimate(
            flops=0, bytes_accessed=sum(2 * a.size * a.dtype.itemsize for a in arrays), transcendentals=0
        ),
        name="fetch",
    )(*map(in_hbm, arrays))


def project_kernel(sub, *refs):
    *parcels, out_proj, keep, send, landed = refs
    half, block = keep.shape
    here = parcels[0].shape[0]
    inner = out_proj.shape[1]
    core, ep = lax.axis_index("c"), lax.axis_index("ep")
    tp = lax.axis_index("y") * lax.axis_size("c") + core
    for k, parcel in enumerate(parcels):
        rows = pl.ds(pl.multiple_of((ep ^ k) * here, here), here)
        share = inner + k % 2 * LANES
        landed[rows, :inner] = parcel[:, :inner]
        landed[rows, inner:] = parcel[:, share : share + LANES]
    rest = landed.shape[1] - inner
    at_row = lax.broadcasted_iota(jnp.int32, (rest, block), 0)
    at_col = lax.broadcasted_iota(jnp.int32, (rest, block), 1)
    spot = jnp.where((at_row + tp * sub == at_col) & (at_row < sub), 1.0, 0.0).astype(bf16)
    part = lax.dot_general(
        landed[:, :inner], out_proj[...], (((1,), (1,)), ((), ())), preferred_element_type=f32
    ) + jnp.dot(landed[:, inner:], spot, preferred_element_type=f32)
    keep[...] = jnp.where(core == 0, part[:half], part[half:])
    send[...] = jnp.where(core == 0, part[half:], part[:half])


def project(parcels, out_proj, sub):
    here = parcels[0].shape[0]
    inner = out_proj.shape[1] + LANES
    tokens = here * len(parcels)
    vmem = pl.BlockSpec(memory_space=pltpu.VMEM)
    shape = jax.ShapeDtypeStruct((tokens // 2, out_proj.shape[0]), f32)
    return pl.pallas_call(
        functools.partial(project_kernel, sub),
        out_shape=(shape, shape),
        in_specs=[vmem] * (len(parcels) + 1),
        out_specs=(vmem, vmem),
        scratch_shapes=[pltpu.VMEM((tokens, inner), bf16)],
        compiler_params=pltpu.CompilerParams(vmem_limit_bytes=8 * 2**20),
        name="project",
    )(*parcels, out_proj)


def bundle_kernel(own, got, gain, router_t, codes, out):
    hidden = own[...].astype(f32) + got[...].astype(f32)
    rows, block = hidden.shape
    experts = router_t.shape[0]
    scaled = (hidden * gain[...]).astype(bf16)
    square = jnp.sum(hidden * hidden, axis=1, keepdims=True)
    logits = lax.dot_general(
        scaled, router_t[...], (((1,), (1,)), ((), ())), preferred_element_type=f32
    )
    spare = out.shape[1] - block
    both = high_low(square) + high_low(logits) + [codes[...]]
    extras = jnp.concatenate(
        [b.astype(f32) for b in both] + [jnp.zeros((rows, spare - 2 - 3 * experts), f32)], axis=1
    ).astype(bf16)
    odd = lax.rem(lax.axis_index("ep"), 2) == 1

    @pl.when(jnp.logical_not(odd))
    def _():
        out[...] = jnp.concatenate([scaled, extras], axis=1)

    @pl.when(odd)
    def _():
        out[...] = jnp.concatenate([extras, scaled], axis=1)


def bundle(own, got, gain, router_t, codes, wide):
    rows = own.shape[0]
    vmem = pl.BlockSpec(memory_space=pltpu.VMEM)
    return pl.pallas_call(
        bundle_kernel,
        out_shape=jax.ShapeDtypeStruct((rows, wide), bf16),
        in_specs=[vmem] * 5,
        out_specs=vmem,
        compiler_params=pltpu.CompilerParams(vmem_limit_bytes=4 * 2**20),
        name="bundle",
    )(own, got, gain, router_t, codes)


def attend(
    query_latent, query_rope, cache_latent, cache_rope, lengths, value_up, residual, dests, sub, block, apart
):
    here, heads, latent = query_latent.shape
    rope, places = cache_rope.shape[1:]
    vdim = value_up.shape[2]
    steps = 2
    per = here // steps
    spec = lambda *dims: pl.BlockSpec((per,) + dims, lambda t: (t,) + (0,) * len(dims))
    whole = lambda shape: pl.BlockSpec(shape, lambda t: (0,) * len(shape))
    values = heads * vdim
    shapes = [(dests, here, values + LANES)]
    if apart:
        shapes = [(here, values + 2 * LANES)] * (dests // 2)
    return pl.pallas_call(
        functools.partial(attend_kernel, steps, dests, sub, block),
        grid=(steps,),
        out_shape=[jax.ShapeDtypeStruct(shape, bf16) for shape in shapes],
        in_specs=[
            pl.BlockSpec(memory_space=pltpu.SMEM),
            spec(heads, latent),
            spec(heads, rope),
            spec(places, latent),
            spec(rope, places),
            whole(residual.shape),
            pl.BlockSpec(memory_space=pl.ANY),
        ],
        out_specs=[whole(shape) for shape in shapes],
        scratch_shapes=[
            pltpu.VMEM((latent // LANES, here * heads, LANES), f32),
            pltpu.VMEM(value_up.shape, bf16),
            pltpu.VMEM(residual.shape, f32),
            pltpu.SemaphoreType.DMA,
        ],
        compiler_params=pltpu.CompilerParams(
            dimension_semantics=("arbitrary",), vmem_limit_bytes=24 * 2**20
        ),
        name="attend",
    )(*map(in_hbm, (lengths, query_latent, query_rope, cache_latent, cache_rope, residual, value_up)))


def expert_kernel(dims, *refs):
    n_ep, n_y, block, experts, part = dims
    mine, other, rest = refs[:n_ep], refs[n_ep : 2 * n_ep], refs[2 * n_ep :]
    gate, up, down, keep_out, send_out, own_out, x, sums = rest
    core, ep = lax.axis_index("c"), lax.axis_index("ep")
    tp = lax.axis_index("y") * lax.axis_size("c") + core
    half, wide = mine[0].shape
    here = 2 * half // n_ep
    spare = wide - block

    lane = lax.broadcasted_iota(jnp.int32, (half, LANES), 1)
    even = lax.rem(ep, 2) == 0
    for i, blocks in enumerate((mine, other)):
        rows = pl.ds(pl.multiple_of((core ^ i) * half, half), half)
        total = jnp.zeros((half, LANES), f32)
        for k in range(0, n_ep, 2):
            low = jnp.where(even, blocks[k][...], blocks[k + 1][...])
            high = jnp.where(even, blocks[k + 1][...], blocks[k][...])
            shared = jnp.where(lane < spare, low[:, -LANES:], high[:, :LANES])
            pair = jnp.concatenate([low[:, :-LANES], shared, high[:, LANES:]], axis=1)
            at = pl.multiple_of(((ep ^ k) // 2) * (2 * block), LANES)
            x[rows, pl.ds(at, 2 * block)] = pair
            total += jnp.where(
                lane < spare, high[:, :LANES].astype(f32), low[:, -LANES:].astype(f32)
            )
        sums[rows, :] = total[:, :spare] + total[:, spare:]
    own_out[...] = x[
        pl.ds(pl.multiple_of(ep * here, here), here), pl.ds(pl.multiple_of(tp * part, LANES), part)
    ]
    total = sums[...]
    square, logits, code = spare_lanes(total, total, experts)

    gate_val = jnp.dot(x[...], gate[...], preferred_element_type=f32)
    up_val = jnp.dot(x[...], up[...], preferred_element_type=f32)
    scale = lax.rsqrt(square / (n_ep * block) + norm_eps)
    weight = row_weight(logits * scale, code, ep)
    act = (jax.nn.silu(gate_val * scale) * (up_val * (scale * weight))).astype(bf16)
    for flip, out in ((1, send_out), (0, keep_out)):
        for y in range(n_y):
            cols = pl.ds(pl.multiple_of((y * 2 + (core ^ flip)) * part, LANES), part)
            out[y] = jnp.dot(act, down[:, cols], preferred_element_type=f32).astype(bf16)


def spare_lanes(total, own, experts):
    square = total[:, 0:1] + total[:, 1:2]
    logits = total[:, 2 : 2 + experts] + total[:, 2 + experts : 2 + 2 * experts]
    return square, logits, own[:, 2 + 2 * experts : 2 + 3 * experts]


def row_weight(logits, code, ep):
    affinity = jnp.where(code > 0.5, jax.nn.sigmoid(logits), 0.0)
    gates = route_scale * affinity / jnp.sum(affinity, axis=1, keepdims=True)
    mine_only = lax.broadcasted_iota(jnp.int32, gates.shape, 1) == ep
    return jnp.sum(jnp.where(mine_only & (code > 1.5), gates, 0.0), axis=1, keepdims=True)


def expert_block(mine, other, gate, up, down, n_y, block, experts):
    n_ep = len(mine)
    half, wide = mine[0].shape
    part = down.shape[1] // (2 * n_y)
    dims = (n_ep, n_y, block, experts, part)
    vmem = pl.BlockSpec(memory_space=pltpu.VMEM)
    shape = jax.ShapeDtypeStruct((n_y, 2 * half, part), bf16)
    own = jax.ShapeDtypeStruct((2 * half // n_ep, part), bf16)
    return pl.pallas_call(
        functools.partial(expert_kernel, dims),
        out_shape=(shape, shape, own),
        in_specs=[vmem] * (2 * n_ep + 3),
        out_specs=(vmem, vmem, vmem),
        scratch_shapes=[
            pltpu.VMEM((2 * half, n_ep * block), bf16),
            pltpu.VMEM((2 * half, wide - block), f32),
        ],
        compiler_params=pltpu.CompilerParams(vmem_limit_bytes=16 * 2**20),
        name="experts",
    )(*mine, *other, gate, up, down)


def expert_plain(ep, c, mine, other, gate, up, down, block, experts):
    n_y, n_ep, quarter, _ = mine.shape
    tokens = 2 * n_y * quarter
    here = tokens // n_ep
    part = down.shape[1] // (2 * n_y)
    both = jnp.stack([jnp.where(c == 0, mine, other), jnp.where(c == 0, other, mine)], axis=1)
    own = both[0, 0, :, :here, block:].reshape(tokens, -1).astype(f32)
    total = jnp.sum(both[..., block:].astype(f32), axis=2).reshape(tokens, -1)
    square, logits, code = spare_lanes(total, own, experts)
    x = both[..., :block].transpose(0, 1, 3, 2, 4).reshape(tokens, -1)
    scale = lax.rsqrt(square / x.shape[1] + norm_eps)
    weight = row_weight(logits * scale, code, ep)
    gate_val = jnp.dot(x, gate, preferred_element_type=f32) * scale
    up_val = jnp.dot(x, up, preferred_element_type=f32) * scale
    act = (jax.nn.silu(gate_val) * up_val * weight).astype(bf16)
    partial = jnp.dot(act, down, preferred_element_type=f32).astype(bf16)
    split = partial.reshape(tokens, n_y, 2, part).transpose(2, 1, 0, 3)
    return (
        lax.dynamic_index_in_dim(split, c, 0, keepdims=False),
        lax.dynamic_index_in_dim(split, 1 - c, 0, keepdims=False),
    )


def exchange(block, axis, size, mine):
    pieces = []
    for k in range(1, size):
        sent = lax.dynamic_index_in_dim(block, mine ^ k, 0, keepdims=False)
        pieces.append(lax.ppermute(sent, axis, [(i, i ^ k) for i in range(size)]))
    return lax.dynamic_index_in_dim(block, mine, 0, keepdims=False), pieces


def high_low(value):
    high = lax.reduce_precision(value, 8, 7)
    return [high, value - high]


def swap_cores(block):
    return lax.ppermute(block, "c", [(0, 1), (1, 0)])


def per_device(
    query_latent,
    query_rope,
    cache_latent,
    cache_rope,
    cache_lengths,
    value_up,
    out_proj,
    residual,
    norm_gain,
    router,
    trainer_gate,
    trainer_up,
    trainer_down,
    hot_experts,
    replica_index,
    token_experts,
    replica_pick,
):
    n_ep, n_y, n_c = lax.axis_size("ep"), lax.axis_size("y"), lax.axis_size("c")
    n_tp = n_y * n_c
    ep, y, c = lax.axis_index("ep"), lax.axis_index("y"), lax.axis_index("c")
    tp = y * n_c + c
    here, width = residual.shape
    tokens = here * n_ep
    quarter = tokens // n_tp
    experts = router.shape[1]
    block = out_proj.shape[0]
    sub = block // n_tp
    part = width // n_tp

    wide = -(-(block + 2 + 3 * experts) // LANES) * LANES
    apart = block % LANES == LANES // 2 == wide - block and block % 16 == 0
    apart = apart and n_ep & (n_ep - 1) == 0 and n_ep // n_tp % 2 == 0 and tokens <= 256
    parcels = attend(
        query_latent, query_rope, cache_latent, cache_rope, cache_lengths, value_up,
        residual, n_ep, sub, block, apart,
    )
    codes = keep_codes(token_experts, replica_pick, hot_experts, replica_index, experts)
    gain_part = lax.dynamic_slice_in_dim(norm_gain, ep * block, block, 0)[None, :]
    router_part = lax.dynamic_slice_in_dim(router.T, ep * block, block, 1)
    gain_own = lax.dynamic_slice_in_dim(norm_gain, tp * part, part, 0)
    weights = (trainer_gate[0], trainer_up[0], trainer_down[0])

    if apart:
        keep, send, x_own = near(
            parcels, out_proj, codes, gain_part, router_part, weights, sub, wide
        )
    else:
        keep, send, x_own = wide_slice(
            parcels[0], out_proj, codes, gain_part, router_part, weights, sub, wide
        )

    got = swap_cores(send)
    summed = (keep.astype(f32) + got.astype(f32)).astype(bf16)
    outbound = summed.reshape(n_y * n_ep, here, part)
    returned = lax.all_to_all(outbound, ("y", "ep"), split_axis=0, concat_axis=0, tiled=True)
    moe = jnp.sum(returned.astype(f32), axis=0)
    hidden_own = x_own.astype(f32) / gain_own[None, :]
    return (hidden_own + moe).astype(bf16)


def send_to(block, axis, size, flip):
    return lax.ppermute(block, axis, [(i, i ^ flip) for i in range(size)])


def gather(blocks, size):
    got = [blocks[0]] + [None] * (size - 1)
    far = list(range(2, size, 2))
    for k in far[1:] + far[:1]:
        got[k] = send_to(blocks[k // 2], "ep", size, k)
    for k in [0] + far[1:] + far[:1]:
        got[k + 1] = send_to(got[k], "ep", size, 1)
    return got


def near(parcels, out_proj, codes, gain_part, router_part, weights, sub, wide):
    n_ep, n_y = lax.axis_size("ep"), lax.axis_size("y")
    ep, c = lax.axis_index("ep"), lax.axis_index("c")
    block = out_proj.shape[0]
    here, experts = codes.shape
    half = here * n_ep // 2
    landed = gather(parcels, n_ep)
    landed[-1], gain_part, router_part = lax.optimization_barrier(
        (landed[-1], gain_part, router_part)
    )
    keep, send = project(landed, out_proj, sub)
    summed = (keep + swap_cores(send)).astype(bf16)
    summed, weights = lax.optimization_barrier((summed, weights))
    *weights, gain_part = fetch(*weights, gain_part)
    total = sum(send_to(summed, "y", n_y, k).astype(f32) for k in range(1, n_y))
    rows = lax.iota(jnp.int32, half)
    placed = jnp.where((rows // here + c * (half // here) == ep)[:, None], jnp.tile(codes, (half // here, 1)), 0.0)
    sent = bundle(summed, total, gain_part, router_part, placed.astype(bf16), wide)
    mine = gather([sent] * (n_ep // 2), n_ep)
    other = [swap_cores(block_k) for block_k in mine]
    return expert_block(mine, other, *weights, n_y, block, experts)


def wide_slice(parcel, out_proj, codes, gain_part, router_part, weights, sub, wide):
    n_ep, n_y, n_c = lax.axis_size("ep"), lax.axis_size("y"), lax.axis_size("c")
    n_tp = n_y * n_c
    ep, y, c = lax.axis_index("ep"), lax.axis_index("y"), lax.axis_index("c")
    tp = y * n_c + c
    block, inner = out_proj.shape
    here, experts = codes.shape
    tokens = here * n_ep
    quarter = tokens // n_tp
    landed = lax.all_to_all(parcel, "ep", split_axis=0, concat_axis=0, tiled=True)
    landed = landed.reshape(tokens, -1)
    at_row = lax.broadcasted_iota(jnp.int32, (LANES, block), 0)
    at_col = lax.broadcasted_iota(jnp.int32, (LANES, block), 1)
    spot = ((at_row + tp * sub == at_col) & (at_row < sub)).astype(bf16)
    column_part = lax.dot_general(
        landed[:, :inner], out_proj, (((1,), (1,)), ((), ())), preferred_element_type=f32
    ) + jnp.dot(landed[:, inner:], spot, preferred_element_type=f32)
    halves = column_part.reshape(n_y, n_c, quarter, block).transpose(1, 0, 2, 3)
    own, others = exchange(halves, "c", n_c, c)
    own, others = exchange(own + sum(others), "y", n_y, y)
    hidden_part = own + sum(others)
    codes = jnp.pad(codes.astype(bf16), ((0, quarter - here), (0, 0)))
    scaled = (hidden_part * gain_part).astype(bf16)
    square = jnp.sum(hidden_part * hidden_part, axis=1, keepdims=True)
    logits = jnp.dot(scaled, router_part.T, preferred_element_type=f32)
    both = high_low(square) + high_low(logits)
    sent = jnp.concatenate([scaled] + [b.astype(bf16) for b in both] + [codes], axis=1)
    sent = jnp.pad(sent, ((0, 0), (0, wide - sent.shape[1])))
    sent = jnp.broadcast_to(sent[None], (n_y * n_ep, quarter, wide))
    mine = lax.all_to_all(
        sent, ("y", "ep"), split_axis=0, concat_axis=0, tiled=True
    ).reshape(n_y, n_ep, quarter, wide)
    other = swap_cores(mine)
    keep, send = expert_plain(ep, c, mine, other, *weights, block, experts)

    part = keep.shape[2]
    per_part = n_ep // n_tp
    first = ep * here
    of_tp, row = first // quarter, first % quarter
    cut = lambda a: lax.dynamic_slice(
        a, (of_tp // n_c, tp * per_part, row, 0), (1, per_part, here, wide)
    )[0]
    rows = jnp.where(of_tp % n_c == c, cut(mine), cut(other))
    return keep, send, rows[:, :, :block].transpose(1, 0, 2).reshape(here, part)


def solution(mesh):
    n_ep, n_tp = mesh.shape["ep"], mesh.shape["tp"]
    fine = Mesh(mesh.devices.reshape(n_ep, n_tp // CORES, CORES), ("ep", "y", "c"))
    tp = ("y", "c")
    placed = (
        P("ep", tp, None),
        P("ep", tp, None),
        P("ep", None, None),
        P("ep", None, None),
        P("ep"),
        P(tp, None, None),
        P("ep", tp),
        P("ep", None),
        P(),
        P(),
        P("ep", None, tp),
        P("ep", None, tp),
        P("ep", tp, None),
        P(),
        P(),
        P("ep", None),
        P("ep", None),
    )
    return jax.shard_map(
        per_device, mesh=fine, in_specs=placed, out_specs=P("ep", tp), check_vma=False
    )
```

```python
import functools

import jax
import jax.numpy as jnp
from jax import lax
from jax.experimental import pallas as pl
from jax.experimental.pallas import tpu as pltpu
from jax.sharding import Mesh, PartitionSpec as P

TOPK = 8
SLOT_DEV = 2
CAP = 2
HOT = 2
CORES = 2
LANES = 128

score_scale = 192.0 ** (-0.5)
route_scale = 2.5
norm_eps = 1e-06

bf16 = jnp.bfloat16
f32 = jnp.float32


def keep_codes(token_experts, replica_pick, hot_experts, replica_index, experts):
    ids = lax.iota(jnp.int32, experts)
    held = jnp.where(
        replica_index[:, None] == lax.iota(jnp.int32, HOT)[None, :], hot_experts[None, :], 0
    ).sum(axis=1)
    count = 1 + jnp.sum((held[:, None] == ids[None, :]).astype(jnp.int32), axis=0)
    match = token_experts[:, :, None] == ids[None, None, :]
    named = jnp.any(match, axis=1)
    place = jnp.sum(jnp.where(match, replica_pick[:, :, None], 0), axis=1) % count[None, :]
    place = jnp.where(named, place, -1)
    tokens = lax.iota(jnp.int32, place.shape[0])
    ahead = (tokens[None, :] < tokens[:, None])[:, :, None] & (
        place[None, :, :] == place[:, None, :]
    )
    prior = jnp.sum(ahead.astype(jnp.int32), axis=1)
    return jnp.where(named, jnp.where(prior < CAP, 2.0, 1.0), 0.0)


def attend_kernel(steps, dests, sub, block, lengths, ql, qr, cl, cr, residual, vu_hbm, *refs):
    *outs, lat, vu, wide_res, sem = refs
    apart = len(outs) > 1
    ep = lax.axis_index("ep")
    outs = outs if apart else [outs[0].at[j] for j in range(dests)]
    step = pl.program_id(0)
    per, heads = ql.shape[:2]
    here = per * steps
    tp = lax.axis_index("y") * lax.axis_size("c") + lax.axis_index("c")
    copy = pltpu.make_async_copy(vu_hbm, vu, sem)
    vdim = vu.shape[2]
    values = heads * vdim

    @pl.when(step == 0)
    def _():
        copy.start()
        width = residual.shape[1]
        wide_res[...] = residual[...].astype(f32)
        span = 2 * LANES
        lane = lax.broadcasted_iota(jnp.int32, (here, LANES), 1)
        spots = [(out, j, values) for j, out in enumerate(outs)]
        if apart:
            spots = [
                (out, ep ^ (2 * j + i), values + i * LANES) for j, out in enumerate(outs) for i in (0, 1)
            ]
        for out, dest, at in spots:
            base = dest * block + tp * sub
            start = jnp.minimum(base // LANES * LANES, width - span)
            piece = wide_res[:, pl.ds(pl.multiple_of(start, LANES), span)]
            piece = pltpu.roll(piece, span - (base - start), axis=1)[:, :LANES]
            out[:, at : at + LANES] = jnp.where(lane < sub, piece, 0.0).astype(bf16)

    scores = [
        lax.dot_general(ql[i], cl[i], (((1,), (1,)), ((), ())), preferred_element_type=f32)
        for i in range(per)
    ]
    scores = [
        (s + jnp.dot(qr[i], cr[i], preferred_element_type=f32)) * score_scale
        for i, s in enumerate(scores)
    ]
    places = lax.broadcasted_iota(jnp.int32, scores[0].shape, 1)
    scores = [
        jnp.where(places < lengths[step * per + i], s, -1e30) for i, s in enumerate(scores)
    ]
    peaks = [jnp.max(s, axis=1, keepdims=True) for s in scores]
    shifted = [jnp.exp(s - m) for s, m in zip(scores, peaks)]
    inverse = [1.0 / jnp.sum(p, axis=1, keepdims=True) for p in shifted]
    mixed = [
        jnp.dot(p.astype(bf16), cl[i], preferred_element_type=f32)
        for i, p in enumerate(shifted)
    ]
    for i in range(per):
        got = mixed[i] * inverse[i]
        for j in range(lat.shape[0]):
            lat[j, pl.ds((step * per + i) * heads, heads), :] = got[
                :, j * LANES : (j + 1) * LANES
            ]

    @pl.when(step == steps - 1)
    def _():
        copy.wait()
        head_rows = lambda h: jnp.concatenate(
            [lat[j, pl.ds(h, here, stride=heads), :] for j in range(lat.shape[0])], axis=1
        ).astype(bf16)
        for h in range(0, heads, 2):
            rows = jnp.concatenate([head_rows(h), head_rows(h + 1)], axis=0)
            both = jnp.concatenate([vu[h], vu[h + 1]], axis=1)
            got = jnp.dot(rows, both, preferred_element_type=f32).astype(bf16)
            for out in outs:
                out[:, h * vdim : (h + 1) * vdim] = got[:here, :vdim]
                out[:, (h + 1) * vdim : (h + 2) * vdim] = got[here:, vdim:]


def in_hbm(array):
    return pltpu.with_memory_space_constraint(array, pltpu.HBM)


def fetch_kernel(count, *refs):
    sems = refs[-1]
    ins, outs = refs[:count], refs[count : 2 * count]
    copies = [pltpu.make_async_copy(a, b, sems.at[i]) for i, (a, b) in enumerate(zip(ins, outs))]
    for copy in copies:
        copy.start()
    for copy in copies:
        copy.wait()


def fetch(*arrays):
    count = len(arrays)
    return pl.pallas_call(
        functools.partial(fetch_kernel, count),
        out_shape=tuple(jax.ShapeDtypeStruct(a.shape, a.dtype) for a in arrays),
        in_specs=[pl.BlockSpec(memory_space=pl.ANY)] * count,
        out_specs=(pl.BlockSpec(memory_space=pltpu.VMEM),) * count,
        scratch_shapes=[pltpu.SemaphoreType.DMA((count,))],
        compiler_params=pltpu.CompilerParams(vmem_limit_bytes=12 * 2**20),
        cost_estimate=pl.CostEstimate(
            flops=0, bytes_accessed=sum(2 * a.size * a.dtype.itemsize for a in arrays), transcendentals=0
        ),
        name="fetch",
    )(*map(in_hbm, arrays))


def project_kernel(sub, *refs):
    *parcels, out_proj, keep, send, landed = refs
    half, block = keep.shape
    here = parcels[0].shape[0]
    inner = out_proj.shape[1]
    core, ep = lax.axis_index("c"), lax.axis_index("ep")
    tp = lax.axis_index("y") * lax.axis_size("c") + core
    for k, parcel in enumerate(parcels):
        rows = pl.ds(pl.multiple_of((ep ^ k) * here, here), here)
        share = inner + k % 2 * LANES
        landed[rows, :inner] = parcel[:, :inner]
        landed[rows, inner:] = parcel[:, share : share + LANES]
    rest = landed.shape[1] - inner
    at_row = lax.broadcasted_iota(jnp.int32, (rest, block), 0)
    at_col = lax.broadcasted_iota(jnp.int32, (rest, block), 1)
    spot = jnp.where((at_row + tp * sub == at_col) & (at_row < sub), 1.0, 0.0).astype(bf16)
    part = lax.dot_general(
        landed[:, :inner], out_proj[...], (((1,), (1,)), ((), ())), preferred_element_type=f32
    ) + jnp.dot(landed[:, inner:], spot, preferred_element_type=f32)
    keep[...] = jnp.where(core == 0, part[:half], part[half:])
    send[...] = jnp.where(core == 0, part[half:], part[:half])


def project(parcels, out_proj, sub):
    here = parcels[0].shape[0]
    inner = out_proj.shape[1] + LANES
    tokens = here * len(parcels)
    vmem = pl.BlockSpec(memory_space=pltpu.VMEM)
    shape = jax.ShapeDtypeStruct((tokens // 2, out_proj.shape[0]), f32)
    return pl.pallas_call(
        functools.partial(project_kernel, sub),
        out_shape=(shape, shape),
        in_specs=[vmem] * (len(parcels) + 1),
        out_specs=(vmem, vmem),
        scratch_shapes=[pltpu.VMEM((tokens, inner), bf16)],
        compiler_params=pltpu.CompilerParams(vmem_limit_bytes=8 * 2**20),
        name="project",
    )(*parcels, out_proj)


def bundle_kernel(own, got, gain, router_t, codes, out):
    hidden = own[...].astype(f32) + got[...].astype(f32)
    rows, block = hidden.shape
    experts = router_t.shape[0]
    scaled = (hidden * gain[...]).astype(bf16)
    square = jnp.sum(hidden * hidden, axis=1, keepdims=True)
    logits = lax.dot_general(
        scaled, router_t[...], (((1,), (1,)), ((), ())), preferred_element_type=f32
    )
    spare = out.shape[1] - block
    both = high_low(square) + high_low(logits) + [codes[...]]
    extras = jnp.concatenate(
        [b.astype(f32) for b in both] + [jnp.zeros((rows, spare - 2 - 3 * experts), f32)], axis=1
    ).astype(bf16)
    odd = lax.rem(lax.axis_index("ep"), 2) == 1

    @pl.when(jnp.logical_not(odd))
    def _():
        out[...] = jnp.concatenate([scaled, extras], axis=1)

    @pl.when(odd)
    def _():
        out[...] = jnp.concatenate([extras, scaled], axis=1)


def bundle(own, got, gain, router_t, codes, wide):
    rows = own.shape[0]
    vmem = pl.BlockSpec(memory_space=pltpu.VMEM)
    return pl.pallas_call(
        bundle_kernel,
        out_shape=jax.ShapeDtypeStruct((rows, wide), bf16),
        in_specs=[vmem] * 5,
        out_specs=vmem,
        compiler_params=pltpu.CompilerParams(vmem_limit_bytes=4 * 2**20),
        name="bundle",
    )(own, got, gain, router_t, codes)


def attend(
    query_latent, query_rope, cache_latent, cache_rope, lengths, value_up, residual, dests, sub, block, apart
):
    here, heads, latent = query_latent.shape
    rope, places = cache_rope.shape[1:]
    vdim = value_up.shape[2]
    steps = 2
    per = here // steps
    spec = lambda *dims: pl.BlockSpec((per,) + dims, lambda t: (t,) + (0,) * len(dims))
    whole = lambda shape: pl.BlockSpec(shape, lambda t: (0,) * len(shape))
    values = heads * vdim
    shapes = [(dests, here, values + LANES)]
    if apart:
        shapes = [(here, values + 2 * LANES)] * (dests // 2)
    return pl.pallas_call(
        functools.partial(attend_kernel, steps, dests, sub, block),
        grid=(steps,),
        out_shape=[jax.ShapeDtypeStruct(shape, bf16) for shape in shapes],
        in_specs=[
            pl.BlockSpec(memory_space=pltpu.SMEM),
            spec(heads, latent),
            spec(heads, rope),
            spec(places, latent),
            spec(rope, places),
            whole(residual.shape),
            pl.BlockSpec(memory_space=pl.ANY),
        ],
        out_specs=[whole(shape) for shape in shapes],
        scratch_shapes=[
            pltpu.VMEM((latent // LANES, here * heads, LANES), f32),
            pltpu.VMEM(value_up.shape, bf16),
            pltpu.VMEM(residual.shape, f32),
            pltpu.SemaphoreType.DMA,
        ],
        compiler_params=pltpu.CompilerParams(
            dimension_semantics=("arbitrary",), vmem_limit_bytes=24 * 2**20
        ),
        name="attend",
    )(*map(in_hbm, (lengths, query_latent, query_rope, cache_latent, cache_rope, residual, value_up)))


def expert_kernel(dims, *refs):
    n_ep, n_y, block, experts, part = dims
    mine, other, rest = refs[:n_ep], refs[n_ep : 2 * n_ep], refs[2 * n_ep :]
    gate, up, down, *outs, own_out, x, sums = rest
    y = lax.axis_index("y")
    core, ep = lax.axis_index("c"), lax.axis_index("ep")
    tp = lax.axis_index("y") * lax.axis_size("c") + core
    half, wide = mine[0].shape
    here = 2 * half // n_ep
    spare = wide - block

    lane = lax.broadcasted_iota(jnp.int32, (half, LANES), 1)
    even = lax.rem(ep, 2) == 0
    for i, blocks in enumerate((mine, other)):
        rows = pl.ds(pl.multiple_of((core ^ i) * half, half), half)
        total = jnp.zeros((half, LANES), f32)
        for k in range(0, n_ep, 2):
            low = jnp.where(even, blocks[k][...], blocks[k + 1][...])
            high = jnp.where(even, blocks[k + 1][...], blocks[k][...])
            shared = jnp.where(lane < spare, low[:, -LANES:], high[:, :LANES])
            pair = jnp.concatenate([low[:, :-LANES], shared, high[:, LANES:]], axis=1)
            at = pl.multiple_of(((ep ^ k) // 2) * (2 * block), LANES)
            x[rows, pl.ds(at, 2 * block)] = pair
            total += jnp.where(
                lane < spare, high[:, :LANES].astype(f32), low[:, -LANES:].astype(f32)
            )
        sums[rows, :] = total[:, :spare] + total[:, spare:]
    own_out[...] = x[
        pl.ds(pl.multiple_of(ep * here, here), here), pl.ds(pl.multiple_of(tp * part, LANES), part)
    ]
    total = sums[...]
    square, logits, code = spare_lanes(total, total, experts)

    gate_val = jnp.dot(x[...], gate[...], preferred_element_type=f32)
    up_val = jnp.dot(x[...], up[...], preferred_element_type=f32)
    scale = lax.rsqrt(square / (n_ep * block) + norm_eps)
    weight = row_weight(logits * scale, code, ep)
    act = (jax.nn.silu(gate_val * scale) * (up_val * (scale * weight))).astype(bf16)
    for i, out in enumerate(outs):
        far, flip = 1 - i // 2, 1 - i % 2
        cols = pl.ds(pl.multiple_of(((y ^ far) * 2 + (core ^ flip)) * part, LANES), part)
        got = jnp.dot(act, down[:, cols], preferred_element_type=f32).astype(bf16)
        for group in range(n_ep):
            k = ep ^ group
            out[k % 2, k // 2] = got[group * here : (group + 1) * here]


def spare_lanes(total, own, experts):
    square = total[:, 0:1] + total[:, 1:2]
    logits = total[:, 2 : 2 + experts] + total[:, 2 + experts : 2 + 2 * experts]
    return square, logits, own[:, 2 + 2 * experts : 2 + 3 * experts]


def row_weight(logits, code, ep):
    affinity = jnp.where(code > 0.5, jax.nn.sigmoid(logits), 0.0)
    gates = route_scale * affinity / jnp.sum(affinity, axis=1, keepdims=True)
    mine_only = lax.broadcasted_iota(jnp.int32, gates.shape, 1) == ep
    return jnp.sum(jnp.where(mine_only & (code > 1.5), gates, 0.0), axis=1, keepdims=True)


def expert_block(mine, other, gate, up, down, n_y, block, experts):
    n_ep = len(mine)
    half, wide = mine[0].shape
    part = down.shape[1] // (2 * n_y)
    dims = (n_ep, n_y, block, experts, part)
    vmem = pl.BlockSpec(memory_space=pltpu.VMEM)
    shape = jax.ShapeDtypeStruct((2, n_ep // 2, 2 * half // n_ep, part), bf16)
    own = jax.ShapeDtypeStruct((2 * half // n_ep, part), bf16)
    return pl.pallas_call(
        functools.partial(expert_kernel, dims),
        out_shape=(shape,) * 4 + (own,),
        in_specs=[vmem] * (2 * n_ep + 3),
        out_specs=(vmem,) * 5,
        scratch_shapes=[
            pltpu.VMEM((2 * half, n_ep * block), bf16),
            pltpu.VMEM((2 * half, wide - block), f32),
        ],
        compiler_params=pltpu.CompilerParams(vmem_limit_bytes=16 * 2**20),
        name="experts",
    )(*mine, *other, gate, up, down)


def expert_plain(ep, c, mine, other, gate, up, down, block, experts):
    n_y, n_ep, quarter, _ = mine.shape
    tokens = 2 * n_y * quarter
    here = tokens // n_ep
    part = down.shape[1] // (2 * n_y)
    both = jnp.stack([jnp.where(c == 0, mine, other), jnp.where(c == 0, other, mine)], axis=1)
    own = both[0, 0, :, :here, block:].reshape(tokens, -1).astype(f32)
    total = jnp.sum(both[..., block:].astype(f32), axis=2).reshape(tokens, -1)
    square, logits, code = spare_lanes(total, own, experts)
    x = both[..., :block].transpose(0, 1, 3, 2, 4).reshape(tokens, -1)
    scale = lax.rsqrt(square / x.shape[1] + norm_eps)
    weight = row_weight(logits * scale, code, ep)
    gate_val = jnp.dot(x, gate, preferred_element_type=f32) * scale
    up_val = jnp.dot(x, up, preferred_element_type=f32) * scale
    act = (jax.nn.silu(gate_val) * up_val * weight).astype(bf16)
    partial = jnp.dot(act, down, preferred_element_type=f32).astype(bf16)
    split = partial.reshape(tokens, n_y, 2, part).transpose(2, 1, 0, 3)
    return (
        lax.dynamic_index_in_dim(split, c, 0, keepdims=False),
        lax.dynamic_index_in_dim(split, 1 - c, 0, keepdims=False),
    )


def exchange(block, axis, size, mine):
    pieces = []
    for k in range(1, size):
        sent = lax.dynamic_index_in_dim(block, mine ^ k, 0, keepdims=False)
        pieces.append(lax.ppermute(sent, axis, [(i, i ^ k) for i in range(size)]))
    return lax.dynamic_index_in_dim(block, mine, 0, keepdims=False), pieces


def high_low(value):
    high = lax.reduce_precision(value, 8, 7)
    return [high, value - high]


def swap_cores(block):
    return lax.ppermute(block, "c", [(0, 1), (1, 0)])


def per_device(
    query_latent,
    query_rope,
    cache_latent,
    cache_rope,
    cache_lengths,
    value_up,
    out_proj,
    residual,
    norm_gain,
    router,
    trainer_gate,
    trainer_up,
    trainer_down,
    hot_experts,
    replica_index,
    token_experts,
    replica_pick,
):
    n_ep, n_y, n_c = lax.axis_size("ep"), lax.axis_size("y"), lax.axis_size("c")
    n_tp = n_y * n_c
    ep, y, c = lax.axis_index("ep"), lax.axis_index("y"), lax.axis_index("c")
    tp = y * n_c + c
    here, width = residual.shape
    tokens = here * n_ep
    quarter = tokens // n_tp
    experts = router.shape[1]
    block = out_proj.shape[0]
    sub = block // n_tp
    part = width // n_tp

    wide = -(-(block + 2 + 3 * experts) // LANES) * LANES
    apart = block % LANES == LANES // 2 == wide - block and block % 16 == 0
    apart = apart and n_ep & (n_ep - 1) == 0 and n_y == CORES and n_ep // n_tp % 2 == 0 and tokens <= 256
    parcels = attend(
        query_latent, query_rope, cache_latent, cache_rope, cache_lengths, value_up,
        residual, n_ep, sub, block, apart,
    )
    codes = keep_codes(token_experts, replica_pick, hot_experts, replica_index, experts)
    gain_part = lax.dynamic_slice_in_dim(norm_gain, ep * block, block, 0)[None, :]
    router_part = lax.dynamic_slice_in_dim(router.T, ep * block, block, 1)
    gain_own = lax.dynamic_slice_in_dim(norm_gain, tp * part, part, 0)
    weights = (trainer_gate[0], trainer_up[0], trainer_down[0])

    if apart:
        moe, x_own = near(
            parcels, out_proj, codes, gain_part, router_part, weights, sub, wide
        )
    else:
        moe, x_own = wide_slice(
            parcels[0], out_proj, codes, gain_part, router_part, weights, sub, wide
        )

    hidden_own = x_own.astype(f32) / gain_own[None, :]
    return (hidden_own + moe).astype(bf16)


def send_to(block, axis, size, flip):
    return lax.ppermute(block, axis, [(i, i ^ flip) for i in range(size)])


def gather(blocks, size):
    got = [blocks[0]] + [None] * (size - 1)
    far = list(range(2, size, 2))
    for k in far[1:] + far[:1]:
        got[k] = send_to(blocks[k // 2], "ep", size, k)
    for k in [0] + far[1:] + far[:1]:
        got[k + 1] = send_to(got[k], "ep", size, 1)
    return got


def scatter(far_send, far_keep, near_send, near_keep):
    n_ep = lax.axis_size("ep")
    wide = lambda a: a.astype(f32)
    far_got, near_got = swap_cores(far_send), swap_cores(near_send)
    far = [(wide(far_keep[i]) + wide(far_got[i])).astype(bf16) for i in (0, 1)]
    far = [send_to(far[i], "y", 2, 1) for i in (1, 0)]
    mixed = lambda i: wide(near_keep[i]) + wide(near_got[i]) + wide(far[1 - i])
    crossed = send_to(mixed(1).astype(bf16), "ep", n_ep, 1)
    total = mixed(0) + wide(crossed)
    moe = total[0]
    rounded = [total[j].astype(bf16) for j in range(n_ep // 2)]
    for j in range(n_ep // 2 - 1, 0, -1):
        moe = moe + wide(send_to(rounded[j], "ep", n_ep, 2 * j))
    return moe


def near(parcels, out_proj, codes, gain_part, router_part, weights, sub, wide):
    n_ep, n_y = lax.axis_size("ep"), lax.axis_size("y")
    ep, c = lax.axis_index("ep"), lax.axis_index("c")
    block = out_proj.shape[0]
    here, experts = codes.shape
    half = here * n_ep // 2
    landed = gather(parcels, n_ep)
    landed[-1], gain_part, router_part = lax.optimization_barrier(
        (landed[-1], gain_part, router_part)
    )
    keep, send = project(landed, out_proj, sub)
    summed = (keep + swap_cores(send)).astype(bf16)
    summed, weights = lax.optimization_barrier((summed, weights))
    *weights, gain_part = fetch(*weights, gain_part)
    total = sum(send_to(summed, "y", n_y, k).astype(f32) for k in range(1, n_y))
    rows = lax.iota(jnp.int32, half)
    placed = jnp.where((rows // here + c * (half // here) == ep)[:, None], jnp.tile(codes, (half // here, 1)), 0.0)
    sent = bundle(summed, total, gain_part, router_part, placed.astype(bf16), wide)
    mine = gather([sent] * (n_ep // 2), n_ep)
    other = [swap_cores(block_k) for block_k in mine]
    *parts, x_own = expert_block(mine, other, *weights, n_y, block, experts)
    return scatter(*parts), x_own


def wide_slice(parcel, out_proj, codes, gain_part, router_part, weights, sub, wide):
    n_ep, n_y, n_c = lax.axis_size("ep"), lax.axis_size("y"), lax.axis_size("c")
    n_tp = n_y * n_c
    ep, y, c = lax.axis_index("ep"), lax.axis_index("y"), lax.axis_index("c")
    tp = y * n_c + c
    block, inner = out_proj.shape
    here, experts = codes.shape
    tokens = here * n_ep
    quarter = tokens // n_tp
    landed = lax.all_to_all(parcel, "ep", split_axis=0, concat_axis=0, tiled=True)
    landed = landed.reshape(tokens, -1)
    at_row = lax.broadcasted_iota(jnp.int32, (LANES, block), 0)
    at_col = lax.broadcasted_iota(jnp.int32, (LANES, block), 1)
    spot = ((at_row + tp * sub == at_col) & (at_row < sub)).astype(bf16)
    column_part = lax.dot_general(
        landed[:, :inner], out_proj, (((1,), (1,)), ((), ())), preferred_element_type=f32
    ) + jnp.dot(landed[:, inner:], spot, preferred_element_type=f32)
    halves = column_part.reshape(n_y, n_c, quarter, block).transpose(1, 0, 2, 3)
    own, others = exchange(halves, "c", n_c, c)
    own, others = exchange(own + sum(others), "y", n_y, y)
    hidden_part = own + sum(others)
    codes = jnp.pad(codes.astype(bf16), ((0, quarter - here), (0, 0)))
    scaled = (hidden_part * gain_part).astype(bf16)
    square = jnp.sum(hidden_part * hidden_part, axis=1, keepdims=True)
    logits = jnp.dot(scaled, router_part.T, preferred_element_type=f32)
    both = high_low(square) + high_low(logits)
    sent = jnp.concatenate([scaled] + [b.astype(bf16) for b in both] + [codes], axis=1)
    sent = jnp.pad(sent, ((0, 0), (0, wide - sent.shape[1])))
    sent = jnp.broadcast_to(sent[None], (n_y * n_ep, quarter, wide))
    mine = lax.all_to_all(
        sent, ("y", "ep"), split_axis=0, concat_axis=0, tiled=True
    ).reshape(n_y, n_ep, quarter, wide)
    other = swap_cores(mine)
    keep, send = expert_plain(ep, c, mine, other, *weights, block, experts)
    summed = (keep.astype(f32) + swap_cores(send).astype(f32)).astype(bf16)
    outbound = summed.reshape(n_y * n_ep, here, -1)
    returned = lax.all_to_all(outbound, ("y", "ep"), split_axis=0, concat_axis=0, tiled=True)
    moe = jnp.sum(returned.astype(f32), axis=0)

    part = keep.shape[2]
    per_part = n_ep // n_tp
    first = ep * here
    of_tp, row = first // quarter, first % quarter
    cut = lambda a: lax.dynamic_slice(
        a, (of_tp // n_c, tp * per_part, row, 0), (1, per_part, here, wide)
    )[0]
    rows = jnp.where(of_tp % n_c == c, cut(mine), cut(other))
    return moe, rows[:, :, :block].transpose(1, 0, 2).reshape(here, part)


def solution(mesh):
    n_ep, n_tp = mesh.shape["ep"], mesh.shape["tp"]
    fine = Mesh(mesh.devices.reshape(n_ep, n_tp // CORES, CORES), ("ep", "y", "c"))
    tp = ("y", "c")
    placed = (
        P("ep", tp, None),
        P("ep", tp, None),
        P("ep", None, None),
        P("ep", None, None),
        P("ep"),
        P(tp, None, None),
        P("ep", tp),
        P("ep", None),
        P(),
        P(),
        P("ep", None, tp),
        P("ep", None, tp),
        P("ep", tp, None),
        P(),
        P(),
        P("ep", None),
        P("ep", None),
    )
    return jax.shard_map(
        per_device, mesh=fine, in_specs=placed, out_specs=P("ep", tp), check_vma=False
    )
```

```python
import functools

import jax
import jax.numpy as jnp
from jax import lax
from jax.experimental import pallas as pl
from jax.experimental.pallas import tpu as pltpu
from jax.sharding import Mesh, PartitionSpec as P

TOPK = 8
SLOT_DEV = 2
CAP = 2
HOT = 2
CORES = 2
LANES = 128

score_scale = 192.0 ** (-0.5)
route_scale = 2.5
norm_eps = 1e-06

bf16 = jnp.bfloat16
f32 = jnp.float32


def keep_codes(token_experts, replica_pick, hot_experts, replica_index, experts):
    ids = lax.iota(jnp.int32, experts)
    held = jnp.where(
        replica_index[:, None] == lax.iota(jnp.int32, HOT)[None, :], hot_experts[None, :], 0
    ).sum(axis=1)
    count = 1 + jnp.sum((held[:, None] == ids[None, :]).astype(jnp.int32), axis=0)
    match = token_experts[:, :, None] == ids[None, None, :]
    named = jnp.any(match, axis=1)
    place = jnp.sum(jnp.where(match, replica_pick[:, :, None], 0), axis=1) % count[None, :]
    place = jnp.where(named, place, -1)
    tokens = lax.iota(jnp.int32, place.shape[0])
    ahead = (tokens[None, :] < tokens[:, None])[:, :, None] & (
        place[None, :, :] == place[:, None, :]
    )
    prior = jnp.sum(ahead.astype(jnp.int32), axis=1)
    return jnp.where(named, jnp.where(prior < CAP, 2.0, 1.0), 0.0)


def attend_kernel(steps, dests, sub, block, lengths, ql, qr, cl, cr, residual, vu_hbm, *refs):
    *outs, lat, vu, wide_res, sem = refs
    apart = len(outs) > 1
    ep = lax.axis_index("ep")
    outs = outs if apart else [outs[0].at[j] for j in range(dests)]
    step = pl.program_id(0)
    per, heads = ql.shape[:2]
    here = per * steps
    tp = lax.axis_index("y") * lax.axis_size("c") + lax.axis_index("c")
    copy = pltpu.make_async_copy(vu_hbm, vu, sem)
    vdim = vu.shape[2]
    values = heads * vdim

    @pl.when(step == 0)
    def _():
        copy.start()
        width = residual.shape[1]
        wide_res[...] = residual[...].astype(f32)
        span = 2 * LANES
        lane = lax.broadcasted_iota(jnp.int32, (here, LANES), 1)
        spots = [(out, j, values) for j, out in enumerate(outs)]
        if apart:
            spots = [
                (out, ep ^ (2 * j + i), values + i * LANES) for j, out in enumerate(outs) for i in (0, 1)
            ]
        for out, dest, at in spots:
            base = dest * block + tp * sub
            start = jnp.minimum(base // LANES * LANES, width - span)
            piece = wide_res[:, pl.ds(pl.multiple_of(start, LANES), span)]
            piece = pltpu.roll(piece, span - (base - start), axis=1)[:, :LANES]
            out[:, at : at + LANES] = jnp.where(lane < sub, piece, 0.0).astype(bf16)

    scores = [
        lax.dot_general(ql[i], cl[i], (((1,), (1,)), ((), ())), preferred_element_type=f32)
        for i in range(per)
    ]
    scores = [
        (s + jnp.dot(qr[i], cr[i], preferred_element_type=f32)) * score_scale
        for i, s in enumerate(scores)
    ]
    places = lax.broadcasted_iota(jnp.int32, scores[0].shape, 1)
    scores = [
        jnp.where(places < lengths[step * per + i], s, -1e30) for i, s in enumerate(scores)
    ]
    peaks = [jnp.max(s, axis=1, keepdims=True) for s in scores]
    shifted = [jnp.exp(s - m) for s, m in zip(scores, peaks)]
    inverse = [1.0 / jnp.sum(p, axis=1, keepdims=True) for p in shifted]
    mixed = [
        jnp.dot(p.astype(bf16), cl[i], preferred_element_type=f32)
        for i, p in enumerate(shifted)
    ]
    for i in range(per):
        got = mixed[i] * inverse[i]
        for j in range(lat.shape[0]):
            lat[j, pl.ds((step * per + i) * heads, heads), :] = got[
                :, j * LANES : (j + 1) * LANES
            ]

    @pl.when(step == steps - 1)
    def _():
        copy.wait()
        head_rows = lambda h: jnp.concatenate(
            [lat[j, pl.ds(h, here, stride=heads), :] for j in range(lat.shape[0])], axis=1
        ).astype(bf16)
        for h in range(0, heads, 2):
            rows = jnp.concatenate([head_rows(h), head_rows(h + 1)], axis=0)
            both = jnp.concatenate([vu[h], vu[h + 1]], axis=1)
            got = jnp.dot(rows, both, preferred_element_type=f32).astype(bf16)
            for out in outs:
                out[:, h * vdim : (h + 1) * vdim] = got[:here, :vdim]
                out[:, (h + 1) * vdim : (h + 2) * vdim] = got[here:, vdim:]


def in_hbm(array):
    return pltpu.with_memory_space_constraint(array, pltpu.HBM)


def fetch_kernel(count, *refs):
    sems = refs[-1]
    ins, outs = refs[:count], refs[count : 2 * count]
    copies = [pltpu.make_async_copy(a, b, sems.at[i]) for i, (a, b) in enumerate(zip(ins, outs))]
    for copy in copies:
        copy.start()
    for copy in copies:
        copy.wait()


def fetch(*arrays):
    count = len(arrays)
    return pl.pallas_call(
        functools.partial(fetch_kernel, count),
        out_shape=tuple(jax.ShapeDtypeStruct(a.shape, a.dtype) for a in arrays),
        in_specs=[pl.BlockSpec(memory_space=pl.ANY)] * count,
        out_specs=(pl.BlockSpec(memory_space=pltpu.VMEM),) * count,
        scratch_shapes=[pltpu.SemaphoreType.DMA((count,))],
        compiler_params=pltpu.CompilerParams(vmem_limit_bytes=12 * 2**20),
        cost_estimate=pl.CostEstimate(
            flops=0, bytes_accessed=sum(2 * a.size * a.dtype.itemsize for a in arrays), transcendentals=0
        ),
        name="fetch",
    )(*map(in_hbm, arrays))


def project_kernel(sub, *refs):
    *parcels, out_proj, keep, send, landed = refs
    half, block = keep.shape
    here = parcels[0].shape[0]
    inner = out_proj.shape[1]
    core, ep = lax.axis_index("c"), lax.axis_index("ep")
    tp = lax.axis_index("y") * lax.axis_size("c") + core
    for k, parcel in enumerate(parcels):
        rows = pl.ds(pl.multiple_of((ep ^ k) * here, here), here)
        share = inner + k % 2 * LANES
        landed[rows, :inner] = parcel[:, :inner]
        landed[rows, inner:] = parcel[:, share : share + LANES]
    rest = landed.shape[1] - inner
    at_row = lax.broadcasted_iota(jnp.int32, (rest, block), 0)
    at_col = lax.broadcasted_iota(jnp.int32, (rest, block), 1)
    spot = jnp.where((at_row + tp * sub == at_col) & (at_row < sub), 1.0, 0.0).astype(bf16)
    part = lax.dot_general(
        landed[:, :inner], out_proj[...], (((1,), (1,)), ((), ())), preferred_element_type=f32
    ) + jnp.dot(landed[:, inner:], spot, preferred_element_type=f32)
    keep[...] = jnp.where(core == 0, part[:half], part[half:]).astype(bf16)
    send[...] = jnp.where(core == 0, part[half:], part[:half]).astype(bf16)


def project(parcels, out_proj, sub):
    here = parcels[0].shape[0]
    inner = out_proj.shape[1] + LANES
    tokens = here * len(parcels)
    vmem = pl.BlockSpec(memory_space=pltpu.VMEM)
    shape = jax.ShapeDtypeStruct((tokens // 2, out_proj.shape[0]), bf16)
    return pl.pallas_call(
        functools.partial(project_kernel, sub),
        out_shape=(shape, shape),
        in_specs=[vmem] * (len(parcels) + 1),
        out_specs=(vmem, vmem),
        scratch_shapes=[pltpu.VMEM((tokens, inner), bf16)],
        compiler_params=pltpu.CompilerParams(vmem_limit_bytes=8 * 2**20),
        name="project",
    )(*parcels, out_proj)


def bundle_kernel(own, got, gain, router_t, codes, out):
    hidden = own[...].astype(f32) + got[...].astype(f32)
    rows, block = hidden.shape
    experts = router_t.shape[0]
    scaled = (hidden * gain[...]).astype(bf16)
    square = jnp.sum(hidden * hidden, axis=1, keepdims=True)
    logits = lax.dot_general(
        scaled, router_t[...], (((1,), (1,)), ((), ())), preferred_element_type=f32
    )
    spare = out.shape[1] - block
    both = high_low(square) + high_low(logits) + [codes[...]]
    extras = jnp.concatenate(
        [b.astype(f32) for b in both] + [jnp.zeros((rows, spare - 2 - 3 * experts), f32)], axis=1
    ).astype(bf16)
    odd = lax.rem(lax.axis_index("ep"), 2) == 1

    @pl.when(jnp.logical_not(odd))
    def _():
        out[...] = jnp.concatenate([scaled, extras], axis=1)

    @pl.when(odd)
    def _():
        out[...] = jnp.concatenate([extras, scaled], axis=1)


def bundle(own, got, gain, router_t, codes, wide):
    rows = own.shape[0]
    vmem = pl.BlockSpec(memory_space=pltpu.VMEM)
    return pl.pallas_call(
        bundle_kernel,
        out_shape=jax.ShapeDtypeStruct((rows, wide), bf16),
        in_specs=[vmem] * 5,
        out_specs=vmem,
        compiler_params=pltpu.CompilerParams(vmem_limit_bytes=4 * 2**20),
        name="bundle",
    )(own, got, gain, router_t, codes)


def attend(
    query_latent, query_rope, cache_latent, cache_rope, lengths, value_up, residual, dests, sub, block, apart
):
    here, heads, latent = query_latent.shape
    rope, places = cache_rope.shape[1:]
    vdim = value_up.shape[2]
    steps = 2
    per = here // steps
    spec = lambda *dims: pl.BlockSpec((per,) + dims, lambda t: (t,) + (0,) * len(dims))
    whole = lambda shape: pl.BlockSpec(shape, lambda t: (0,) * len(shape))
    values = heads * vdim
    shapes = [(dests, here, values + LANES)]
    if apart:
        shapes = [(here, values + 2 * LANES)] * (dests // 2)
    return pl.pallas_call(
        functools.partial(attend_kernel, steps, dests, sub, block),
        grid=(steps,),
        out_shape=[jax.ShapeDtypeStruct(shape, bf16) for shape in shapes],
        in_specs=[
            pl.BlockSpec(memory_space=pltpu.SMEM),
            spec(heads, latent),
            spec(heads, rope),
            spec(places, latent),
            spec(rope, places),
            whole(residual.shape),
            pl.BlockSpec(memory_space=pl.ANY),
        ],
        out_specs=[whole(shape) for shape in shapes],
        scratch_shapes=[
            pltpu.VMEM((latent // LANES, here * heads, LANES), f32),
            pltpu.VMEM(value_up.shape, bf16),
            pltpu.VMEM(residual.shape, f32),
            pltpu.SemaphoreType.DMA,
        ],
        compiler_params=pltpu.CompilerParams(
            dimension_semantics=("arbitrary",), vmem_limit_bytes=24 * 2**20
        ),
        name="attend",
    )(*map(in_hbm, (lengths, query_latent, query_rope, cache_latent, cache_rope, residual, value_up)))


def expert_kernel(dims, *refs):
    n_ep, n_y, block, experts, part = dims
    mine, other, rest = refs[:n_ep], refs[n_ep : 2 * n_ep], refs[2 * n_ep :]
    gate, up, down, *outs, own_out, x, sums = rest
    y = lax.axis_index("y")
    core, ep = lax.axis_index("c"), lax.axis_index("ep")
    tp = lax.axis_index("y") * lax.axis_size("c") + core
    half, wide = mine[0].shape
    here = 2 * half // n_ep
    spare = wide - block

    lane = lax.broadcasted_iota(jnp.int32, (half, LANES), 1)
    even = lax.rem(ep, 2) == 0
    for i, blocks in enumerate((mine, other)):
        rows = pl.ds(pl.multiple_of((core ^ i) * half, half), half)
        total = jnp.zeros((half, LANES), f32)
        for k in range(0, n_ep, 2):
            low = jnp.where(even, blocks[k][...], blocks[k + 1][...])
            high = jnp.where(even, blocks[k + 1][...], blocks[k][...])
            shared = jnp.where(lane < spare, low[:, -LANES:], high[:, :LANES])
            pair = jnp.concatenate([low[:, :-LANES], shared, high[:, LANES:]], axis=1)
            at = pl.multiple_of(((ep ^ k) // 2) * (2 * block), LANES)
            x[rows, pl.ds(at, 2 * block)] = pair
            total += jnp.where(
                lane < spare, high[:, :LANES].astype(f32), low[:, -LANES:].astype(f32)
            )
        sums[rows, :] = total[:, :spare] + total[:, spare:]
    own_out[...] = x[
        pl.ds(pl.multiple_of(ep * here, here), here), pl.ds(pl.multiple_of(tp * part, LANES), part)
    ]
    total = sums[...]
    square, logits, code = spare_lanes(total, total, experts)

    gate_val = jnp.dot(x[...], gate[...], preferred_element_type=f32)
    up_val = jnp.dot(x[...], up[...], preferred_element_type=f32)
    scale = lax.rsqrt(square / (n_ep * block) + norm_eps)
    weight = row_weight(logits * scale, code, ep)
    act = (jax.nn.silu(gate_val * scale) * (up_val * (scale * weight))).astype(bf16)
    for i, out in enumerate(outs):
        far, flip = 1 - i // 2, 1 - i % 2
        cols = pl.ds(pl.multiple_of(((y ^ far) * 2 + (core ^ flip)) * part, LANES), part)
        got = jnp.dot(act, down[:, cols], preferred_element_type=f32).astype(bf16)
        for group in range(n_ep):
            k = ep ^ group
            out[k % 2, k // 2] = got[group * here : (group + 1) * here]


def spare_lanes(total, own, experts):
    square = total[:, 0:1] + total[:, 1:2]
    logits = total[:, 2 : 2 + experts] + total[:, 2 + experts : 2 + 2 * experts]
    return square, logits, own[:, 2 + 2 * experts : 2 + 3 * experts]


def row_weight(logits, code, ep):
    affinity = jnp.where(code > 0.5, jax.nn.sigmoid(logits), 0.0)
    gates = route_scale * affinity / jnp.sum(affinity, axis=1, keepdims=True)
    mine_only = lax.broadcasted_iota(jnp.int32, gates.shape, 1) == ep
    return jnp.sum(jnp.where(mine_only & (code > 1.5), gates, 0.0), axis=1, keepdims=True)


def expert_block(mine, other, gate, up, down, n_y, block, experts):
    n_ep = len(mine)
    half, wide = mine[0].shape
    part = down.shape[1] // (2 * n_y)
    dims = (n_ep, n_y, block, experts, part)
    vmem = pl.BlockSpec(memory_space=pltpu.VMEM)
    shape = jax.ShapeDtypeStruct((2, n_ep // 2, 2 * half // n_ep, part), bf16)
    own = jax.ShapeDtypeStruct((2 * half // n_ep, part), bf16)
    return pl.pallas_call(
        functools.partial(expert_kernel, dims),
        out_shape=(shape,) * 4 + (own,),
        in_specs=[vmem] * (2 * n_ep + 3),
        out_specs=(vmem,) * 5,
        scratch_shapes=[
            pltpu.VMEM((2 * half, n_ep * block), bf16),
            pltpu.VMEM((2 * half, wide - block), f32),
        ],
        compiler_params=pltpu.CompilerParams(vmem_limit_bytes=16 * 2**20),
        name="experts",
    )(*mine, *other, gate, up, down)


def expert_plain(ep, c, mine, other, gate, up, down, block, experts):
    n_y, n_ep, quarter, _ = mine.shape
    tokens = 2 * n_y * quarter
    here = tokens // n_ep
    part = down.shape[1] // (2 * n_y)
    both = jnp.stack([jnp.where(c == 0, mine, other), jnp.where(c == 0, other, mine)], axis=1)
    own = both[0, 0, :, :here, block:].reshape(tokens, -1).astype(f32)
    total = jnp.sum(both[..., block:].astype(f32), axis=2).reshape(tokens, -1)
    square, logits, code = spare_lanes(total, own, experts)
    x = both[..., :block].transpose(0, 1, 3, 2, 4).reshape(tokens, -1)
    scale = lax.rsqrt(square / x.shape[1] + norm_eps)
    weight = row_weight(logits * scale, code, ep)
    gate_val = jnp.dot(x, gate, preferred_element_type=f32) * scale
    up_val = jnp.dot(x, up, preferred_element_type=f32) * scale
    act = (jax.nn.silu(gate_val) * up_val * weight).astype(bf16)
    partial = jnp.dot(act, down, preferred_element_type=f32).astype(bf16)
    split = partial.reshape(tokens, n_y, 2, part).transpose(2, 1, 0, 3)
    return (
        lax.dynamic_index_in_dim(split, c, 0, keepdims=False),
        lax.dynamic_index_in_dim(split, 1 - c, 0, keepdims=False),
    )


def exchange(block, axis, size, mine):
    pieces = []
    for k in range(1, size):
        sent = lax.dynamic_index_in_dim(block, mine ^ k, 0, keepdims=False)
        pieces.append(lax.ppermute(sent, axis, [(i, i ^ k) for i in range(size)]))
    return lax.dynamic_index_in_dim(block, mine, 0, keepdims=False), pieces


def high_low(value):
    high = lax.reduce_precision(value, 8, 7)
    return [high, value - high]


def swap_cores(block):
    return lax.ppermute(block, "c", [(0, 1), (1, 0)])


def per_device(
    query_latent,
    query_rope,
    cache_latent,
    cache_rope,
    cache_lengths,
    value_up,
    out_proj,
    residual,
    norm_gain,
    router,
    trainer_gate,
    trainer_up,
    trainer_down,
    hot_experts,
    replica_index,
    token_experts,
    replica_pick,
):
    n_ep, n_y, n_c = lax.axis_size("ep"), lax.axis_size("y"), lax.axis_size("c")
    n_tp = n_y * n_c
    ep, y, c = lax.axis_index("ep"), lax.axis_index("y"), lax.axis_index("c")
    tp = y * n_c + c
    here, width = residual.shape
    tokens = here * n_ep
    quarter = tokens // n_tp
    experts = router.shape[1]
    block = out_proj.shape[0]
    sub = block // n_tp
    part = width // n_tp

    wide = -(-(block + 2 + 3 * experts) // LANES) * LANES
    apart = block % LANES == LANES // 2 == wide - block and block % 16 == 0
    apart = apart and n_ep & (n_ep - 1) == 0 and n_y == CORES and n_ep // n_tp % 2 == 0 and tokens <= 256
    parcels = attend(
        query_latent, query_rope, cache_latent, cache_rope, cache_lengths, value_up,
        residual, n_ep, sub, block, apart,
    )
    codes = keep_codes(token_experts, replica_pick, hot_experts, replica_index, experts)
    gain_part = lax.dynamic_slice_in_dim(norm_gain, ep * block, block, 0)[None, :]
    router_part = lax.dynamic_slice_in_dim(router.T, ep * block, block, 1)
    gain_own = lax.dynamic_slice_in_dim(norm_gain, tp * part, part, 0)
    weights = (trainer_gate[0], trainer_up[0], trainer_down[0])

    if apart:
        moe, x_own = near(
            parcels, out_proj, codes, gain_part, router_part, weights, sub, wide
        )
    else:
        moe, x_own = wide_slice(
            parcels[0], out_proj, codes, gain_part, router_part, weights, sub, wide
        )

    hidden_own = x_own.astype(f32) / gain_own[None, :]
    return (hidden_own + moe).astype(bf16)


def send_to(block, axis, size, flip):
    return lax.ppermute(block, axis, [(i, i ^ flip) for i in range(size)])


def gather(blocks, size):
    got = [blocks[0]] + [None] * (size - 1)
    far = list(range(2, size, 2))
    for k in far[1:] + far[:1]:
        got[k] = send_to(blocks[k // 2], "ep", size, k)
    for k in [0] + far[1:] + far[:1]:
        got[k + 1] = send_to(got[k], "ep", size, 1)
    return got


def scatter(far_send, far_keep, near_send, near_keep):
    n_ep = lax.axis_size("ep")
    wide = lambda a: a.astype(f32)
    far_got, near_got = swap_cores(far_send), swap_cores(near_send)
    far = [(wide(far_keep[i]) + wide(far_got[i])).astype(bf16) for i in (0, 1)]
    far = [send_to(far[i], "y", 2, 1) for i in (1, 0)]
    mixed = lambda i: wide(near_keep[i]) + wide(near_got[i]) + wide(far[1 - i])
    crossed = send_to(mixed(1).astype(bf16), "ep", n_ep, 1)
    total = mixed(0) + wide(crossed)
    moe = total[0]
    rounded = [total[j].astype(bf16) for j in range(n_ep // 2)]
    for j in range(n_ep // 2 - 1, 0, -1):
        moe = moe + wide(send_to(rounded[j], "ep", n_ep, 2 * j))
    return moe


def near(parcels, out_proj, codes, gain_part, router_part, weights, sub, wide):
    n_ep, n_y = lax.axis_size("ep"), lax.axis_size("y")
    ep, c = lax.axis_index("ep"), lax.axis_index("c")
    block = out_proj.shape[0]
    here, experts = codes.shape
    half = here * n_ep // 2
    landed = gather(parcels, n_ep)
    landed[-1], gain_part, router_part = lax.optimization_barrier(
        (landed[-1], gain_part, router_part)
    )
    keep, send = project(landed, out_proj, sub)
    keep, weights = lax.optimization_barrier((keep, weights))
    *weights, gain_part = fetch(*weights, gain_part)
    across = [(i, i ^ (2 * n_y - 1)) for i in range(2 * n_y)]
    got = [lax.ppermute(send, ("y", "c"), across), send_to(keep, "y", n_y, 1), swap_cores(send)]
    total = sum(piece.astype(f32) for piece in got)
    rows = lax.iota(jnp.int32, half)
    placed = jnp.where((rows // here + c * (half // here) == ep)[:, None], jnp.tile(codes, (half // here, 1)), 0.0)
    sent = bundle(keep, total, gain_part, router_part, placed.astype(bf16), wide)
    mine = gather([sent] * (n_ep // 2), n_ep)
    other = [swap_cores(block_k) for block_k in mine]
    *parts, x_own = expert_block(mine, other, *weights, n_y, block, experts)
    return scatter(*parts), x_own


def wide_slice(parcel, out_proj, codes, gain_part, router_part, weights, sub, wide):
    n_ep, n_y, n_c = lax.axis_size("ep"), lax.axis_size("y"), lax.axis_size("c")
    n_tp = n_y * n_c
    ep, y, c = lax.axis_index("ep"), lax.axis_index("y"), lax.axis_index("c")
    tp = y * n_c + c
    block, inner = out_proj.shape
    here, experts = codes.shape
    tokens = here * n_ep
    quarter = tokens // n_tp
    landed = lax.all_to_all(parcel, "ep", split_axis=0, concat_axis=0, tiled=True)
    landed = landed.reshape(tokens, -1)
    at_row = lax.broadcasted_iota(jnp.int32, (LANES, block), 0)
    at_col = lax.broadcasted_iota(jnp.int32, (LANES, block), 1)
    spot = ((at_row + tp * sub == at_col) & (at_row < sub)).astype(bf16)
    column_part = lax.dot_general(
        landed[:, :inner], out_proj, (((1,), (1,)), ((), ())), preferred_element_type=f32
    ) + jnp.dot(landed[:, inner:], spot, preferred_element_type=f32)
    halves = column_part.reshape(n_y, n_c, quarter, block).transpose(1, 0, 2, 3)
    own, others = exchange(halves, "c", n_c, c)
    own, others = exchange(own + sum(others), "y", n_y, y)
    hidden_part = own + sum(others)
    codes = jnp.pad(codes.astype(bf16), ((0, quarter - here), (0, 0)))
    scaled = (hidden_part * gain_part).astype(bf16)
    square = jnp.sum(hidden_part * hidden_part, axis=1, keepdims=True)
    logits = jnp.dot(scaled, router_part.T, preferred_element_type=f32)
    both = high_low(square) + high_low(logits)
    sent = jnp.concatenate([scaled] + [b.astype(bf16) for b in both] + [codes], axis=1)
    sent = jnp.pad(sent, ((0, 0), (0, wide - sent.shape[1])))
    sent = jnp.broadcast_to(sent[None], (n_y * n_ep, quarter, wide))
    mine = lax.all_to_all(
        sent, ("y", "ep"), split_axis=0, concat_axis=0, tiled=True
    ).reshape(n_y, n_ep, quarter, wide)
    other = swap_cores(mine)
    keep, send = expert_plain(ep, c, mine, other, *weights, block, experts)
    summed = (keep.astype(f32) + swap_cores(send).astype(f32)).astype(bf16)
    outbound = summed.reshape(n_y * n_ep, here, -1)
    returned = lax.all_to_all(outbound, ("y", "ep"), split_axis=0, concat_axis=0, tiled=True)
    moe = jnp.sum(returned.astype(f32), axis=0)

    part = keep.shape[2]
    per_part = n_ep // n_tp
    first = ep * here
    of_tp, row = first // quarter, first % quarter
    cut = lambda a: lax.dynamic_slice(
        a, (of_tp // n_c, tp * per_part, row, 0), (1, per_part, here, wide)
    )[0]
    rows = jnp.where(of_tp % n_c == c, cut(mine), cut(other))
    return moe, rows[:, :, :block].transpose(1, 0, 2).reshape(here, part)


def solution(mesh):
    n_ep, n_tp = mesh.shape["ep"], mesh.shape["tp"]
    fine = Mesh(mesh.devices.reshape(n_ep, n_tp // CORES, CORES), ("ep", "y", "c"))
    tp = ("y", "c")
    placed = (
        P("ep", tp, None),
        P("ep", tp, None),
        P("ep", None, None),
        P("ep", None, None),
        P("ep"),
        P(tp, None, None),
        P("ep", tp),
        P("ep", None),
        P(),
        P(),
        P("ep", None, tp),
        P("ep", None, tp),
        P("ep", tp, None),
        P(),
        P(),
        P("ep", None),
        P("ep", None),
    )
    return jax.shard_map(
        per_device, mesh=fine, in_specs=placed, out_specs=P("ep", tp), check_vma=False
    )
```
